32 devices in a mesh: fsdp: 16 (over z, x, core), tp: 2 (over y).
Axes of the slice: x: 2, y: 2, z: 4, core: 2. Of those that a mesh axis runs over, the one named last changes fastest.
Arguments:
- hidden_in: bfloat16 [1024, 2, 768], P(('fsdp', 'tp')), may hold values from -6 to 6
- cotangent: bfloat16 [1024, 2, 768], P(('fsdp', 'tp')), may hold values from -6 to 6
- lengths: int32 [2], replicated, may hold values from 256 to 1024, as said below
- w_query: bfloat16 [768, 768], P('fsdp', 'tp'), may hold values from -0.21875 to 0.21875
- b_query: bfloat16 [768], P('fsdp'), may hold values from -1.796875 to 1.796875
- w_key: bfloat16 [768, 768], P('fsdp', 'tp'), may hold values from -0.3125 to 0.3125
- w_value: bfloat16 [768, 768], P('fsdp', 'tp'), may hold values from -0.21875 to 0.21875
- b_value: bfloat16 [768], P('fsdp'), may hold values from -0.1796875 to 0.1796875
- w_out: bfloat16 [768, 768], P('tp', 'fsdp'), may hold values from -4 to 4
- b_out: bfloat16 [768], P('fsdp'), may hold values from -0.8984375 to 0.8984375
- first_gain: bfloat16 [768], P('fsdp'), may hold values from 0.099609375 to 1.8984375
- first_shift: bfloat16 [768], P('fsdp'), may hold values from -0.8984375 to 0.8984375
- w_up: bfloat16 [768, 3072], P('fsdp', 'tp'), may hold values from -0.21875 to 0.21875
- b_up: bfloat16 [3072], P('fsdp'), may hold values from -1.796875 to 1.796875
- w_down: bfloat16 [3072, 768], P('tp', 'fsdp'), may hold values from -0.109375 to 0.109375
- b_down: bfloat16 [768], P('fsdp'), may hold values from -0.8984375 to 0.8984375
- second_gain: bfloat16 [768], P('fsdp'), may hold values from 0.099609375 to 1.8984375
- second_shift: bfloat16 [768], P('fsdp'), may hold values from -0.8984375 to 0.8984375
Outputs:
- output: bfloat16 [1024, 2, 768], P(('fsdp', 'tp'))
- grad_hidden: float32 [1024, 2, 768], P(('fsdp', 'tp'))
- grad_w_query: float32 [768, 768], P('fsdp', 'tp')
- grad_b_query: float32 [768], P('fsdp')
- grad_w_key: float32 [768, 768], P('fsdp', 'tp')
- grad_w_value: float32 [768, 768], P('fsdp', 'tp')
- grad_b_value: float32 [768], P('fsdp')
- grad_w_out: float32 [768, 768], P('tp', 'fsdp')
- grad_b_out: float32 [768], P('fsdp')
- grad_first_gain: float32 [768], P('fsdp')
- grad_first_shift: float32 [768], P('fsdp')
- grad_w_up: float32 [768, 3072], P('fsdp', 'tp')
- grad_b_up: float32 [3072], P('fsdp')
- grad_w_down: float32 [3072, 768], P('tp', 'fsdp')
- grad_b_down: float32 [768], P('fsdp')
- grad_second_gain: float32 [768], P('fsdp')
- grad_second_shift: float32 [768], P('fsdp')
The draws below stay inside these ranges and needn't reach their ends.
Inputs may be any that keep to these rules, and one draw needn't show every extreme that they name: `lengths`: every slot's valid tokens stand at its start; in every draw one slot, drawn from the seed, is full.
All inputs are finite; a program needn't handle non-finite values.
Results may differ from the reference program's by a relative error of at most 0.019.
Values may be sent and summed in bfloat16 or wider, within the bound.
No kernel may reach another device: no remote copies, remote signals or barrier semaphores. Data moves between devices by JAX's collectives and lax.ppermute only.
A program may use at most 192 MiB of HBM per device.

```python
from functools import partial
import jax
import jax.numpy as jnp
from jax import lax

H = 12
HD = 64
D = 768
FF = 3072
SLOT = 1024
SEQS = 2
TOKENS = 2048


def draw_lengths(key, part):
    first_key = jax.random.fold_in(key, 11)
    second_key = jax.random.fold_in(key, 23)
    drawn_lengths = jax.random.randint(first_key, (SEQS,), SLOT // 4, SLOT + 1)
    chosen = jax.random.randint(second_key, (), 0, SEQS)
    slot_ids = jnp.arange(SEQS)
    drawn_lengths = jnp.where(slot_ids == chosen, SLOT, drawn_lengths)
    return drawn_lengths.astype(jnp.int32)


def spiked(values, stream_key, source, target, parts, factor):
    def block_of(dim):
        return (jnp.arange(values.shape[dim]) // (values.shape[dim] // parts)).reshape((-1,) + (1,) * (values.ndim - 1 - dim))

    near = jax.random.permutation(stream_key, parts)[block_of(target)]
    far = (block_of(target) + parts // 2) % parts
    return jnp.where((block_of(source) == near) | (block_of(source) == far), factor * values, values)


def shard_levels(rng, dims, pieces, smallest, largest):
    def one(position, blocks):
        heights = jax.random.uniform(jax.random.fold_in(jax.random.fold_in(rng, 6), position), (blocks,), jnp.float32, smallest / len(pieces), largest / len(pieces))
        return jnp.repeat(jnp.exp(heights), dims[position] // blocks).reshape((-1,) + (1,) * (len(dims) - position - 1))

    factor_of = one(*pieces[0])
    for cut in pieces[1:]:
        factor_of = factor_of * one(*cut)
    return factor_of


def normal_values(key, shape, scale, reach, split=(), dtype=jnp.bfloat16):
    values = scale * jax.random.normal(key, shape, jnp.float32)
    if split:
        values = values * shard_levels(key, shape, split, -0.22, 0.18)
    return jnp.clip(values, -reach, reach).astype(dtype)


def heavy_noise(rng, shape, width, limit, shards, heavy, kind=jnp.bfloat16):
    result = width * jax.random.normal(rng, shape, jnp.float32)
    if shards:
        result = result * shard_levels(rng, shape, shards, -0.22, 0.18)
    return jnp.clip(spiked(result, jax.random.fold_in(rng, 3), *heavy), -limit, limit).astype(kind)


def setup_inputs(seed: int = 0) -> dict:
    arg_keys = jax.random.split(jax.random.key(seed), 19)
    return {
        "hidden_in": normal_values(arg_keys[0], (SLOT, SEQS, D), 1.0, 6.0, ((0, 32),)),
        "cotangent": heavy_noise(arg_keys[1], (SLOT, SEQS, D), 1.0, 6.0, ((0, 32),), (0, 2, 32, 2.75)),
        "lengths": draw_lengths(jax.random.fold_in(arg_keys[18], 71), 0),
        "w_query": normal_values(arg_keys[3], (D, D), D ** -0.5, 0.21875, ((0, 16), (1, 2))),
        "b_query": normal_values(arg_keys[4], (D,), 0.3, 1.796875, ((0, 16),)),
        "w_key": normal_values(arg_keys[5], (D, D), (D // 2) ** -0.5, 0.3125, ((0, 16), (1, 2))),
        "w_value": normal_values(arg_keys[6], (D, D), D ** -0.5, 0.21875, ((0, 16), (1, 2))),
        "b_value": normal_values(arg_keys[7], (D,), 0.03, 0.1796875, ((0, 16),)),
        "w_out": normal_values(arg_keys[8], (D, D), 2 ** -0.5, 4.0, ((0, 2), (1, 16))),
        "b_out": normal_values(arg_keys[9], (D,), 0.15, 0.8984375, ((0, 16),)),
        "first_gain": jnp.clip(1.0 + 0.18 * jax.random.normal(arg_keys[10], (D,), jnp.float32), 0.099609375, 1.8984375).astype(jnp.bfloat16),
        "first_shift": normal_values(arg_keys[11], (D,), 0.15, 0.8984375, ((0, 16),)),
        "w_up": normal_values(arg_keys[12], (D, FF), D ** -0.5, 0.21875, ((0, 16), (1, 2))),
        "b_up": normal_values(arg_keys[13], (FF,), 0.3, 1.796875, ((0, 16),)),
        "w_down": normal_values(arg_keys[14], (FF, D), FF ** -0.5, 0.109375, ((0, 2), (1, 16))),
        "b_down": normal_values(arg_keys[15], (D,), 0.15, 0.8984375, ((0, 16),)),
        "second_gain": jnp.clip(1.0 + 0.18 * jax.random.normal(arg_keys[16], (D,), jnp.float32), 0.099609375, 1.8984375).astype(jnp.bfloat16),
        "second_shift": normal_values(arg_keys[17], (D,), 0.15, 0.8984375, ((0, 16),)),
    }


@jax.custom_vjp
def low(v):
    return lax.optimization_barrier(v.astype(jnp.bfloat16)).astype(jnp.float32)

@jax.custom_vjp
def low_back(v):
    return v

def low_keep(v):
    return (low(v), None)

def low_pass(kept, grad):
    return (grad,)

def back_keep(v):
    return (v, None)

def back_low(kept, grad):
    return (low(grad),)
low.defvjp(low_keep, low_pass)
low_back.defvjp(back_keep, back_low)
layer_eps = 1e-12
highest = lax.Precision.HIGHEST

def layer_norm(values, gain_vector, shift_vector):
    centre = values - lax.optimization_barrier(jnp.mean(values, axis=-1, keepdims=True))
    spread = lax.optimization_barrier(jnp.mean(centre * centre, axis=-1, keepdims=True))
    return centre * lax.rsqrt(spread + layer_eps) * gain_vector + shift_vector

def product(left_side, right_side):
    return jnp.dot(left_side, right_side, precision=highest)

def attend_rows(query_block, key_seq, value_seq, key_live):
    scores = jnp.einsum('qhd,khd->hqk', query_block, key_seq, precision=highest) * HD ** (-0.5)
    scores = low_back(scores)
    masked = jnp.where(key_live[None, None, :], scores, -1e+30)
    weights = low(jax.nn.softmax(masked, axis=-1))
    return jnp.einsum('hqk,khd->qhd', weights, value_seq, precision=highest)

def attend_sequence(operands):
    query_seq, key_seq, value_seq, key_live = operands
    block_rows = min(512, SLOT)
    blocks = query_seq.reshape(SLOT // block_rows, block_rows, H, HD)

    def one_block(query_block):
        return attend_rows(query_block, key_seq, value_seq, key_live)
    return lax.map(jax.checkpoint(one_block), blocks).reshape(SLOT, H, HD)

def by_sequence(rows):
    return jnp.transpose(rows.reshape(SLOT, SEQS, H, HD), (1, 0, 2, 3))

def forward(lengths, hidden, w_query, b_query, w_key, w_value, b_value, w_out, b_out, first_gain, first_shift, w_up, b_up, w_down, b_down, second_gain, second_shift):
    flat = hidden.reshape(TOKENS, D)
    key_live = jnp.arange(SLOT)[None, :] < lengths[:, None]
    queries = low_back(low(product(flat, w_query) + b_query))
    keys_all = low_back(low(product(flat, w_key)))
    values_all = low_back(low(product(flat, w_value) + b_value))
    attended = lax.map(attend_sequence, (by_sequence(queries), by_sequence(keys_all), by_sequence(values_all), key_live))
    attended = low_back(low(jnp.transpose(attended, (1, 0, 2, 3)).reshape(TOKENS, D)))
    branch_one = low_back(product(attended, w_out) + b_out)
    first_out = layer_norm(flat + branch_one, first_gain, first_shift)
    preact = low_back(product(low(first_out), w_up) + b_up)
    active = low(jax.nn.gelu(preact, approximate=False))
    branch_two = low_back(product(active, w_down) + b_down)
    return layer_norm(first_out + branch_two, second_gain, second_shift).reshape(SLOT, SEQS, D)

def reference(hidden_in, cotangent, lengths, w_query, b_query, w_key, w_value, b_value, w_out, b_out, first_gain, first_shift, w_up, b_up, w_down, b_down, second_gain, second_shift):
    members = [member.astype(jnp.float32) for member in (hidden_in, w_query, b_query, w_key, w_value, b_value, w_out, b_out, first_gain, first_shift, w_up, b_up, w_down, b_down, second_gain, second_shift)]
    output, pullback = jax.vjp(partial(forward, lengths), *members)
    row_live = (jnp.arange(SLOT)[:, None] < lengths[None, :]).astype(jnp.float32)
    gradients = pullback(cotangent.astype(jnp.float32) * row_live[:, :, None])
    return (output.astype(jnp.bfloat16), gradients[0], gradients[1], gradients[2], gradients[3], gradients[4], gradients[5], gradients[6], gradients[7], gradients[8], gradients[9], gradients[10], gradients[11], gradients[12], gradients[13], gradients[14], gradients[15])
```

```python
import jax
import jax.numpy as jnp
from jax import lax
from jax.sharding import PartitionSpec as P

HD = 64
layer_eps = 1e-12
masked_score = -1e30
AXES = ("fsdp", "tp")
low_type = jnp.bfloat16
wide = jnp.float32

TP_BIT, CORE_BIT, SLOT_BIT, GROUP = 1, 2, 4, 8


def device_count():
    return lax.axis_size("fsdp") * lax.axis_size("tp")


def swap(values, bit):
    return lax.ppermute(values, AXES, [(i, i ^ bit) for i in range(device_count())])


def over_blocks(values):
    total = device_count()
    groups = [list(range(first, total, GROUP)) for first in range(GROUP)]
    return lax.all_to_all(values, AXES, 0, 0, axis_index_groups=groups)


def gather_blocks(values):
    blocks = device_count() // GROUP
    return over_blocks(jnp.broadcast_to(values[None], (blocks,) + values.shape))


def in_order(first_bit, own, other, axis):
    return jnp.where(
        first_bit == 0, jnp.stack([own, other], axis), jnp.stack([other, own], axis)
    )


def gather_group(rows):
    pair = jnp.concatenate([rows, swap(rows, TP_BIT)], 0)
    return jnp.concatenate([pair, swap(pair, CORE_BIT)], 0)


def sum_group(partial):
    half = partial.shape[0] // 2
    kept = partial[:half] + swap(partial[half:].astype(low_type), CORE_BIT).astype(wide)
    quarter = half // 2
    return kept[:quarter] + swap(kept[quarter:].astype(low_type), TP_BIT).astype(wide)


def norm_parts(values):
    centre = values - jnp.mean(values, axis=-1, keepdims=True)
    spread = jnp.mean(centre * centre, axis=-1, keepdims=True)
    scale = lax.rsqrt(spread + layer_eps)
    return centre * scale, scale


def norm_back(grad, normed, scale, gain):
    scaled = grad * gain
    mean_one = jnp.mean(scaled, axis=-1, keepdims=True)
    mean_two = jnp.mean(scaled * normed, axis=-1, keepdims=True)
    return scale * (scaled - mean_one - normed * mean_two)


def local(
    hidden_in,
    cotangent,
    lengths,
    w_query,
    b_query,
    w_key,
    w_value,
    b_value,
    w_out,
    b_out,
    first_gain,
    first_shift,
    w_up,
    b_up,
    w_down,
    b_down,
    second_gain,
    second_shift,
):
    fsdp_index = lax.axis_index("fsdp")
    tp_bit = lax.axis_index("tp")
    core_bit = fsdp_index % 2
    slot_bit = (fsdp_index // 2) % 2
    block = fsdp_index // 4
    blocks = lax.axis_size("fsdp") // 4
    shard_pos, seq_count, width = hidden_in.shape
    rows_here = 2 * shard_pos
    shard_rows = w_query.shape[0]
    head_cols = w_query.shape[1] // 2
    unit_cols = w_up.shape[1] // 2
    heads = head_cols // HD
    score_scale = HD ** (-0.5)

    def halves(weight):
        return weight.reshape(shard_rows, 2, weight.shape[1] // 2)

    def for_core(parts, which):
        return jnp.concatenate(
            [lax.dynamic_index_in_dim(part, which, 1, keepdims=False) for part in parts], 1
        )

    vectors = jnp.concatenate(
        [
            vector.reshape(shard_rows, -1)
            for vector in (
                b_query,
                b_value,
                b_out,
                first_gain,
                first_shift,
                b_down,
                second_gain,
                second_shift,
                b_up,
            )
        ],
        1,
    )
    vectors = jnp.pad(vectors, ((0, 0), (0, 128 - vectors.shape[1])))
    first_parts = [halves(w_query), halves(w_key), halves(w_value)]
    later_parts = [halves(jnp.transpose(w_out)), halves(w_up), halves(jnp.transpose(w_down))]

    def to_core(parts, shared):
        own, other = for_core(parts, core_bit), for_core(parts, 1 - core_bit)
        if shared is not None:
            own = jnp.concatenate([own, shared], 1)
            other = jnp.concatenate([other, shared], 1)
        return in_order(core_bit, own, swap(other, CORE_BIT), 0)

    def full_rows(pieces):
        stacked = in_order(slot_bit, pieces, swap(pieces, SLOT_BIT), 1)
        return stacked.reshape(width, pieces.shape[-1])

    def to_slot(values):
        own = lax.dynamic_index_in_dim(values, slot_bit, 1, keepdims=False)
        other = lax.dynamic_index_in_dim(values, 1 - slot_bit, 1, keepdims=False)
        return jnp.concatenate([own, swap(other, SLOT_BIT)], 0)

    def from_slot(rows):
        returned = swap(rows[shard_pos:], SLOT_BIT)
        return in_order(slot_bit, rows[:shard_pos], returned, 1)

    rows_low = to_slot(hidden_in)
    first_pack = to_core(first_parts, vectors)
    gathered_rows = gather_blocks(rows_low)
    gathered_first = gather_blocks(first_pack.reshape(2 * shard_rows, -1))
    pair_rows = jnp.stack([gathered_rows, swap(gathered_rows, TP_BIT)], 1)
    slot_rows = jnp.stack([pair_rows, swap(pair_rows, CORE_BIT)], 1)
    slot_rows = slot_rows.reshape(-1, width)
    first_full = full_rows(gathered_first)
    later_pack = to_core(later_parts, None).reshape(2 * shard_rows, -1)
    out_piece = gather_blocks(later_pack[:, :head_cols])
    up_piece = gather_blocks(later_pack[:, head_cols : head_cols + unit_cols])
    down_piece = gather_blocks(later_pack[:, head_cols + unit_cols :])
    out_weight = full_rows(out_piece)
    up_weight = full_rows(up_piece)
    down_weight = full_rows(down_piece)
    qkv_weight = first_full[:, : 3 * head_cols]
    vector_cols = first_full[:, 3 * head_cols :].astype(wide)
    (
        query_bias_all,
        value_bias_all,
        out_bias,
        gain_one,
        shift_one,
        down_bias,
        gain_two,
        shift_two,
    ) = [vector_cols[:, i] for i in range(8)]
    up_bias_all = vector_cols[:, 8 : 8 + b_up.shape[0] // shard_rows].reshape(-1)
    quarter = 2 * tp_bit + core_bit
    query_bias = lax.dynamic_slice_in_dim(query_bias_all, quarter * head_cols, head_cols)
    value_bias = lax.dynamic_slice_in_dim(value_bias_all, quarter * head_cols, head_cols)
    up_bias = lax.dynamic_slice_in_dim(up_bias_all, quarter * unit_cols, unit_cols)

    def positions_of(block_ids):
        shape = (block_ids.shape[0], 2, 2, 2, shard_pos)
        iota = lambda dim: lax.broadcasted_iota(jnp.int32, shape, dim)
        place = block_ids.reshape(-1, 1, 1, 1, 1) * 2 + (iota(3) ^ slot_bit)
        place = (place * 2 + (iota(1) ^ core_bit)) * 2 + (iota(2) ^ tp_bit)
        return (place * shard_pos + iota(4)).reshape(-1)

    length = lax.dynamic_index_in_dim(lengths, slot_bit, 0, keepdims=False)
    slot_live = positions_of(jnp.arange(blocks)) < length
    group_live = positions_of(block.reshape(1)) < length
    row_live = group_live[:rows_here]

    group_count = 4 * rows_here
    own_rows = lax.dynamic_slice_in_dim(slot_rows, block * group_count, group_count, 0)

    def as_heads(values):
        return values.reshape(values.shape[0], heads, HD)

    queries = (
        jnp.dot(slot_rows, qkv_weight[:, :head_cols], preferred_element_type=wide) + query_bias
    ).astype(low_type)
    keys = jnp.dot(
        slot_rows, qkv_weight[:, head_cols : 2 * head_cols], preferred_element_type=wide
    ).astype(low_type)
    values = (
        jnp.dot(slot_rows, qkv_weight[:, 2 * head_cols :], preferred_element_type=wide)
        + value_bias
    ).astype(low_type)
    query_all, key_all, value_all = as_heads(queries), as_heads(keys), as_heads(values)

    def own_of(array):
        return lax.dynamic_slice_in_dim(array, block * group_count, group_count, 0)

    query_own, key_own, value_own = own_of(query_all), own_of(key_all), own_of(value_all)
    scores = (
        jnp.einsum("qhd,khd->hqk", query_own, key_all, preferred_element_type=wide) * score_scale
    )
    masked = jnp.where(slot_live[None, None, :], scores, masked_score)
    top = jnp.max(masked, axis=2, keepdims=True)
    total = jnp.sum(jnp.exp(masked - top), axis=2, keepdims=True)
    log_total = top + jnp.log(total)
    weights = jnp.exp(masked - log_total)
    attended = jnp.einsum(
        "hqk,khd->qhd", weights.astype(low_type), value_all, preferred_element_type=wide
    )
    attended_low = attended.reshape(group_count, head_cols).astype(low_type)

    branch_one = sum_group(
        jnp.einsum("th,dh->td", attended_low, out_weight, preferred_element_type=wide)
    )
    first_sum = rows_low.astype(wide) + branch_one + out_bias
    normed_one, scale_one = norm_parts(first_sum)
    first_out = normed_one * gain_one + shift_one
    group_first = gather_group(first_out.astype(low_type))
    preact = jnp.dot(group_first, up_weight, preferred_element_type=wide) + up_bias
    spread = 0.5 * (1.0 + lax.erf(preact * (0.5**0.5)))
    active_low = (preact * spread).astype(low_type)
    branch_two = sum_group(
        jnp.einsum("tf,df->td", active_low, down_weight, preferred_element_type=wide)
    )
    normed_two, scale_two = norm_parts(first_out + branch_two + down_bias)
    output = normed_two * gain_two + shift_two
    grad_out = to_slot(cotangent).astype(wide) * row_live[:, None].astype(wide)
    second_grad = norm_back(grad_out, normed_two, scale_two, gain_two)
    gain_two_grad = jnp.sum(grad_out * normed_two, axis=0)
    shift_two_grad = jnp.sum(grad_out, axis=0)
    branch_two_grad = second_grad.astype(low_type)
    down_bias_grad = jnp.sum(branch_two_grad.astype(wide), axis=0)
    group_two = gather_group(branch_two_grad)
    active_grad = jnp.einsum("td,df->tf", group_two, down_weight, preferred_element_type=wide)
    slope = spread + preact * jnp.exp(-0.5 * preact * preact) * (2.0 * jnp.pi) ** (-0.5)
    preact_grad = (active_grad * slope).astype(low_type)
    up_bias_grad = jnp.sum(preact_grad.astype(wide), axis=0)
    first_out_grad = second_grad + sum_group(
        jnp.einsum("tf,df->td", preact_grad, up_weight, preferred_element_type=wide)
    )

    def sum_weight(partial):
        cols = partial.shape[1]
        split = partial.astype(low_type).reshape(blocks, 2, 2 * shard_rows, cols)
        own = lax.dynamic_index_in_dim(split, slot_bit, 1, keepdims=False)
        other = lax.dynamic_index_in_dim(split, 1 - slot_bit, 1, keepdims=False)
        half = own.astype(wide) + swap(other, SLOT_BIT).astype(wide)
        pieces = over_blocks(half.astype(low_type))
        summed = jnp.sum(pieces.astype(wide), axis=0).reshape(2, shard_rows, cols)
        mine = lax.dynamic_index_in_dim(summed, core_bit, 0, keepdims=False)
        theirs = lax.dynamic_index_in_dim(summed, 1 - core_bit, 0, keepdims=False)
        return in_order(core_bit, mine, swap(theirs, CORE_BIT), 1)

    up_grad = sum_weight(
        jnp.einsum("td,tf->df", group_first, preact_grad, preferred_element_type=wide)
    )
    down_grad = sum_weight(
        jnp.einsum("td,tf->df", group_two, active_low, preferred_element_type=wide)
    )
    gain_one_grad = jnp.sum(first_out_grad * normed_one, axis=0)
    shift_one_grad = jnp.sum(first_out_grad, axis=0)
    first_grad = norm_back(first_out_grad, normed_one, scale_one, gain_one)
    branch_one_grad = first_grad.astype(low_type)
    out_bias_grad = jnp.sum(branch_one_grad.astype(wide), axis=0)
    group_one = gather_group(branch_one_grad)
    attended_grad = jnp.dot(group_one, out_weight, preferred_element_type=wide).astype(low_type)
    grad_all = as_heads(gather_blocks(attended_grad).reshape(-1, head_cols))
    grad_own = as_heads(attended_grad)
    delta = jnp.einsum("qhd,qhd->hq", grad_own.astype(wide), attended)
    row_stats = gather_blocks(jnp.stack([log_total[:, :, 0], delta]))
    row_stats = jnp.moveaxis(row_stats, 0, 2).reshape(2, heads, -1)
    out_grad = sum_weight(
        jnp.einsum("td,th->dh", group_one, attended_low, preferred_element_type=wide)
    )

    weight_grad = jnp.einsum("qhd,khd->hqk", grad_own, value_all, preferred_element_type=wide)
    score_grad = (weights * (weight_grad - delta[:, :, None])).astype(low_type)
    query_grad = (
        jnp.einsum("hqk,khd->qhd", score_grad, key_all, preferred_element_type=wide) * score_scale
    )
    scores_back = (
        jnp.einsum("qhd,khd->hqk", query_all, key_own, preferred_element_type=wide) * score_scale
    )
    weights_back = jnp.where(
        group_live[None, None, :], jnp.exp(scores_back - row_stats[0][:, :, None]), 0.0
    )
    value_grad = jnp.einsum(
        "hqk,qhd->khd", weights_back.astype(low_type), grad_all, preferred_element_type=wide
    )
    back_grad = jnp.einsum("qhd,khd->hqk", grad_all, value_own, preferred_element_type=wide)
    back_score = (weights_back * (back_grad - row_stats[1][:, :, None])).astype(low_type)
    key_grad = (
        jnp.einsum("hqk,qhd->khd", back_score, query_all, preferred_element_type=wide)
        * score_scale
    )
    qkv_grad = jnp.concatenate(
        [
            grad.reshape(group_count, head_cols).astype(low_type)
            for grad in (query_grad, key_grad, value_grad)
        ],
        1,
    )
    qkv_sums = sum_weight(
        jnp.einsum("td,te->de", own_rows, qkv_grad, preferred_element_type=wide)
    )
    hidden_grad = first_grad + sum_group(
        jnp.einsum("te,de->td", qkv_grad, qkv_weight, preferred_element_type=wide)
    )
    bias_sums = jnp.sum(qkv_grad.astype(wide), axis=0)

    def widen(part):
        full = jnp.zeros((4 * part.shape[0],), wide)
        return lax.dynamic_update_slice_in_dim(full, part, quarter * part.shape[0], 0)

    fsdp_count = lax.axis_size("fsdp")
    all_vectors = jnp.concatenate(
        [
            vector.reshape(fsdp_count, -1)
            for vector in (
                widen(bias_sums[:head_cols]),
                widen(bias_sums[2 * head_cols :]),
                out_bias_grad,
                gain_one_grad,
                shift_one_grad,
                down_bias_grad,
                gain_two_grad,
                shift_two_grad,
                widen(up_bias_grad),
            )
        ],
        1,
    )
    vector_sum = jnp.sum(lax.all_to_all(all_vectors, "fsdp", 0, 0, tiled=True), axis=0)
    vector_sum = vector_sum + swap(vector_sum, TP_BIT)
    vector_grads = [
        vector_sum[i * shard_rows : (i + 1) * shard_rows] for i in range(8)
    ] + [vector_sum[8 * shard_rows :]]

    def columns(array):
        return array.reshape(shard_rows, -1)

    query_sum, key_sum, value_sum = [
        columns(qkv_sums[:, :, i * head_cols : (i + 1) * head_cols]) for i in range(3)
    ]
    return (
        from_slot(output.astype(low_type)),
        from_slot(hidden_grad),
        query_sum,
        vector_grads[0],
        key_sum,
        value_sum,
        vector_grads[1],
        jnp.transpose(columns(out_grad)),
        vector_grads[2],
        vector_grads[3],
        vector_grads[4],
        columns(up_grad),
        vector_grads[8],
        jnp.transpose(columns(down_grad)),
        vector_grads[5],
        vector_grads[6],
        vector_grads[7],
    )


def solution(mesh):
    in_specs = (
        P(("fsdp", "tp"), None, None),
        P(("fsdp", "tp"), None, None),
        P(),
        P("fsdp", "tp"),
        P("fsdp"),
        P("fsdp", "tp"),
        P("fsdp", "tp"),
        P("fsdp"),
        P("tp", "fsdp"),
        P("fsdp"),
        P("fsdp"),
        P("fsdp"),
        P("fsdp", "tp"),
        P("fsdp"),
        P("tp", "fsdp"),
        P("fsdp"),
        P("fsdp"),
        P("fsdp"),
    )
    out_specs = (
        P(("fsdp", "tp"), None, None),
        P(("fsdp", "tp"), None, None),
        P("fsdp", "tp"),
        P("fsdp"),
        P("fsdp", "tp"),
        P("fsdp", "tp"),
        P("fsdp"),
        P("tp", "fsdp"),
        P("fsdp"),
        P("fsdp"),
        P("fsdp"),
        P("fsdp", "tp"),
        P("fsdp"),
        P("tp", "fsdp"),
        P("fsdp"),
        P("fsdp"),
        P("fsdp"),
    )
    return jax.shard_map(local, mesh=mesh, in_specs=in_specs, out_specs=out_specs, check_vma=False)
```

```python
import functools
import math

import jax
import jax.numpy as jnp
from jax import lax
from jax.experimental import pallas as pl
from jax.experimental.pallas import tpu as pltpu
from jax.sharding import PartitionSpec as P

HD = 64
layer_eps = 1e-12
masked_score = -1e30
AXES = ("fsdp", "tp")
low_type = jnp.bfloat16
wide = jnp.float32

TP_BIT, CORE_BIT, SLOT_BIT, GROUP = 1, 2, 4, 8


def device_count():
    return lax.axis_size("fsdp") * lax.axis_size("tp")


def swap(values, bit):
    return lax.ppermute(values, AXES, [(i, i ^ bit) for i in range(device_count())])


def over_blocks(values):
    total = device_count()
    groups = [list(range(first, total, GROUP)) for first in range(GROUP)]
    return lax.all_to_all(values, AXES, 0, 0, axis_index_groups=groups)


def gather_blocks(values):
    blocks = device_count() // GROUP
    return over_blocks(jnp.broadcast_to(values[None], (blocks,) + values.shape))


def in_order(first_bit, own, other, axis):
    return jnp.where(
        first_bit == 0, jnp.stack([own, other], axis), jnp.stack([other, own], axis)
    )


def gather_group(rows):
    pair = jnp.concatenate([rows, swap(rows, TP_BIT)], 0)
    return jnp.concatenate([pair, swap(pair, CORE_BIT)], 0)


def sum_group(partial):
    half = partial.shape[0] // 2
    kept = partial[:half] + swap(partial[half:].astype(low_type), CORE_BIT).astype(wide)
    quarter = half // 2
    return kept[:quarter] + swap(kept[quarter:].astype(low_type), TP_BIT).astype(wide)


def norm_parts(values):
    centre = values - jnp.mean(values, axis=-1, keepdims=True)
    spread = jnp.mean(centre * centre, axis=-1, keepdims=True)
    scale = lax.rsqrt(spread + layer_eps)
    return centre * scale, scale


def norm_back(grad, normed, scale, gain):
    scaled = grad * gain
    mean_one = jnp.mean(scaled, axis=-1, keepdims=True)
    mean_two = jnp.mean(scaled * normed, axis=-1, keepdims=True)
    return scale * (scaled - mean_one - normed * mean_two)


def local(
    hidden_in,
    cotangent,
    lengths,
    w_query,
    b_query,
    w_key,
    w_value,
    b_value,
    w_out,
    b_out,
    first_gain,
    first_shift,
    w_up,
    b_up,
    w_down,
    b_down,
    second_gain,
    second_shift,
):
    fsdp_index = lax.axis_index("fsdp")
    tp_bit = lax.axis_index("tp")
    core_bit = fsdp_index % 2
    slot_bit = (fsdp_index // 2) % 2
    block = fsdp_index // 4
    blocks = lax.axis_size("fsdp") // 4
    shard_pos, seq_count, width = hidden_in.shape
    rows_here = 2 * shard_pos
    shard_rows = w_query.shape[0]
    head_cols = w_query.shape[1] // 2
    unit_cols = w_up.shape[1] // 2
    heads = head_cols // HD
    score_scale = HD ** (-0.5)

    def halves(weight):
        return weight.reshape(shard_rows, 2, weight.shape[1] // 2)

    def for_core(parts, which):
        return jnp.concatenate(
            [lax.dynamic_index_in_dim(part, which, 1, keepdims=False) for part in parts], 1
        )

    vectors = jnp.concatenate(
        [
            vector.reshape(shard_rows, -1)
            for vector in (
                b_query,
                b_value,
                b_out,
                first_gain,
                first_shift,
                b_down,
                second_gain,
                second_shift,
                b_up,
            )
        ],
        1,
    )
    vectors = jnp.pad(vectors, ((0, 0), (0, 128 - vectors.shape[1])))
    first_parts = [halves(w_query), halves(w_key), halves(w_value)]
    later_parts = [halves(jnp.transpose(w_out)), halves(w_up), halves(jnp.transpose(w_down))]

    def to_core(parts, shared):
        own, other = for_core(parts, core_bit), for_core(parts, 1 - core_bit)
        if shared is not None:
            own = jnp.concatenate([own, shared], 1)
            other = jnp.concatenate([other, shared], 1)
        return in_order(core_bit, own, swap(other, CORE_BIT), 0)

    def full_rows(pieces):
        stacked = in_order(slot_bit, pieces, swap(pieces, SLOT_BIT), 1)
        return stacked.reshape(width, pieces.shape[-1])

    def to_slot(values):
        own = lax.dynamic_index_in_dim(values, slot_bit, 1, keepdims=False)
        other = lax.dynamic_index_in_dim(values, 1 - slot_bit, 1, keepdims=False)
        return jnp.concatenate([own, swap(other, SLOT_BIT)], 0)

    def from_slot(rows):
        returned = swap(rows[shard_pos:], SLOT_BIT)
        return in_order(slot_bit, rows[:shard_pos], returned, 1)

    rows_low = to_slot(hidden_in)
    first_pack = to_core(first_parts, vectors)
    gathered_rows = gather_blocks(rows_low)
    gathered_first = gather_blocks(first_pack.reshape(2 * shard_rows, -1))
    pair_rows = jnp.stack([gathered_rows, swap(gathered_rows, TP_BIT)], 1)
    slot_rows = jnp.stack([pair_rows, swap(pair_rows, CORE_BIT)], 1)
    slot_rows = slot_rows.reshape(-1, width)
    first_full = full_rows(gathered_first)
    later_pack = to_core(later_parts, None).reshape(2 * shard_rows, -1)
    out_piece = gather_blocks(later_pack[:, :head_cols])
    up_piece = gather_blocks(later_pack[:, head_cols : head_cols + unit_cols])
    down_piece = gather_blocks(later_pack[:, head_cols + unit_cols :])
    out_weight = full_rows(out_piece)
    up_weight = full_rows(up_piece)
    down_weight = full_rows(down_piece)
    qkv_weight = first_full[:, : 3 * head_cols]
    vector_cols = first_full[:, 3 * head_cols :].astype(wide)
    (
        query_bias_all,
        value_bias_all,
        out_bias,
        gain_one,
        shift_one,
        down_bias,
        gain_two,
        shift_two,
    ) = [vector_cols[:, i] for i in range(8)]
    up_bias_all = vector_cols[:, 8 : 8 + b_up.shape[0] // shard_rows].reshape(-1)
    quarter = 2 * tp_bit + core_bit
    query_bias = lax.dynamic_slice_in_dim(query_bias_all, quarter * head_cols, head_cols)
    value_bias = lax.dynamic_slice_in_dim(value_bias_all, quarter * head_cols, head_cols)
    up_bias = lax.dynamic_slice_in_dim(up_bias_all, quarter * unit_cols, unit_cols)

    def positions_of(block_ids):
        shape = (block_ids.shape[0], 2, 2, 2, shard_pos)
        iota = lambda dim: lax.broadcasted_iota(jnp.int32, shape, dim)
        place = block_ids.reshape(-1, 1, 1, 1, 1) * 2 + (iota(3) ^ slot_bit)
        place = (place * 2 + (iota(1) ^ core_bit)) * 2 + (iota(2) ^ tp_bit)
        return (place * shard_pos + iota(4)).reshape(-1)

    length = lax.dynamic_index_in_dim(lengths, slot_bit, 0, keepdims=False)
    slot_live = positions_of(jnp.arange(blocks)) < length
    group_live = positions_of(block.reshape(1)) < length
    row_live = group_live[:rows_here]

    group_count = 4 * rows_here
    own_rows = lax.dynamic_slice_in_dim(slot_rows, block * group_count, group_count, 0)

    def as_heads(values):
        return values.reshape(values.shape[0], heads, HD)

    queries = (
        jnp.dot(slot_rows, qkv_weight[:, :head_cols], preferred_element_type=wide) + query_bias
    ).astype(low_type)
    keys = jnp.dot(
        slot_rows, qkv_weight[:, head_cols : 2 * head_cols], preferred_element_type=wide
    ).astype(low_type)
    values = (
        jnp.dot(slot_rows, qkv_weight[:, 2 * head_cols :], preferred_element_type=wide)
        + value_bias
    ).astype(low_type)
    query_all, key_all, value_all = as_heads(queries), as_heads(keys), as_heads(values)

    def own_of(array):
        return lax.dynamic_slice_in_dim(array, block * group_count, group_count, 0)

    query_own, key_own, value_own = own_of(query_all), own_of(key_all), own_of(value_all)
    scores = (
        jnp.einsum("qhd,khd->hqk", query_own, key_all, preferred_element_type=wide) * score_scale
    )
    masked = jnp.where(slot_live[None, None, :], scores, masked_score)
    top = jnp.max(masked, axis=2, keepdims=True)
    total = jnp.sum(jnp.exp(masked - top), axis=2, keepdims=True)
    log_total = top + jnp.log(total)
    weights = jnp.exp(masked - log_total)
    attended = jnp.einsum(
        "hqk,khd->qhd", weights.astype(low_type), value_all, preferred_element_type=wide
    )
    attended_low = attended.reshape(group_count, head_cols).astype(low_type)

    branch_one = sum_group(
        jnp.einsum("th,dh->td", attended_low, out_weight, preferred_element_type=wide)
    )
    first_sum = rows_low.astype(wide) + branch_one + out_bias
    normed_one, scale_one = norm_parts(first_sum)
    first_out = normed_one * gain_one + shift_one
    group_first = gather_group(first_out.astype(low_type))
    preact = jnp.dot(group_first, up_weight, preferred_element_type=wide) + up_bias
    spread = 0.5 * (1.0 + lax.erf(preact * (0.5**0.5)))
    active_low = (preact * spread).astype(low_type)
    branch_two = sum_group(
        jnp.einsum("tf,df->td", active_low, down_weight, preferred_element_type=wide)
    )
    normed_two, scale_two = norm_parts(first_out + branch_two + down_bias)
    output = normed_two * gain_two + shift_two
    grad_out = to_slot(cotangent).astype(wide) * row_live[:, None].astype(wide)
    second_grad = norm_back(grad_out, normed_two, scale_two, gain_two)
    gain_two_grad = jnp.sum(grad_out * normed_two, axis=0)
    shift_two_grad = jnp.sum(grad_out, axis=0)
    branch_two_grad = second_grad.astype(low_type)
    down_bias_grad = jnp.sum(branch_two_grad.astype(wide), axis=0)
    group_two = gather_group(branch_two_grad)
    active_grad = jnp.einsum("td,df->tf", group_two, down_weight, preferred_element_type=wide)
    slope = spread + preact * jnp.exp(-0.5 * preact * preact) * (2.0 * jnp.pi) ** (-0.5)
    preact_grad = (active_grad * slope).astype(low_type)
    up_bias_grad = jnp.sum(preact_grad.astype(wide), axis=0)
    first_out_grad = second_grad + sum_group(
        jnp.einsum("tf,df->td", preact_grad, up_weight, preferred_element_type=wide)
    )

    def sum_weight(partial):
        cols = partial.shape[1]
        split = partial.astype(low_type).reshape(blocks, 2, 2 * shard_rows, cols)
        own = lax.dynamic_index_in_dim(split, slot_bit, 1, keepdims=False)
        other = lax.dynamic_index_in_dim(split, 1 - slot_bit, 1, keepdims=False)
        half = own.astype(wide) + swap(other, SLOT_BIT).astype(wide)
        pieces = over_blocks(half.astype(low_type))
        summed = jnp.sum(pieces.astype(wide), axis=0).reshape(2, shard_rows, cols)
        mine = lax.dynamic_index_in_dim(summed, core_bit, 0, keepdims=False)
        theirs = lax.dynamic_index_in_dim(summed, 1 - core_bit, 0, keepdims=False)
        return in_order(core_bit, mine, swap(theirs, CORE_BIT), 1)

    up_grad = sum_weight(
        jnp.einsum("td,tf->df", group_first, preact_grad, preferred_element_type=wide)
    )
    down_grad = sum_weight(
        jnp.einsum("td,tf->df", group_two, active_low, preferred_element_type=wide)
    )
    gain_one_grad = jnp.sum(first_out_grad * normed_one, axis=0)
    shift_one_grad = jnp.sum(first_out_grad, axis=0)
    first_grad = norm_back(first_out_grad, normed_one, scale_one, gain_one)
    branch_one_grad = first_grad.astype(low_type)
    out_bias_grad = jnp.sum(branch_one_grad.astype(wide), axis=0)
    group_one = gather_group(branch_one_grad)
    attended_grad = jnp.dot(group_one, out_weight, preferred_element_type=wide).astype(low_type)
    grad_all = as_heads(gather_blocks(attended_grad).reshape(-1, head_cols))
    grad_own = as_heads(attended_grad)
    delta = jnp.einsum("qhd,qhd->hq", grad_own.astype(wide), attended)
    row_stats = gather_blocks(jnp.stack([log_total[:, :, 0], delta]))
    row_stats = jnp.moveaxis(row_stats, 0, 2).reshape(2, heads, -1)
    out_grad = sum_weight(
        jnp.einsum("td,th->dh", group_one, attended_low, preferred_element_type=wide)
    )

    weight_grad = jnp.einsum("qhd,khd->hqk", grad_own, value_all, preferred_element_type=wide)
    score_grad = (weights * (weight_grad - delta[:, :, None])).astype(low_type)
    query_grad = (
        jnp.einsum("hqk,khd->qhd", score_grad, key_all, preferred_element_type=wide) * score_scale
    )
    scores_back = (
        jnp.einsum("qhd,khd->hqk", query_all, key_own, preferred_element_type=wide) * score_scale
    )
    weights_back = jnp.where(
        group_live[None, None, :], jnp.exp(scores_back - row_stats[0][:, :, None]), 0.0
    )
    value_grad = jnp.einsum(
        "hqk,qhd->khd", weights_back.astype(low_type), grad_all, preferred_element_type=wide
    )
    back_grad = jnp.einsum("qhd,khd->hqk", grad_all, value_own, preferred_element_type=wide)
    back_score = (weights_back * (back_grad - row_stats[1][:, :, None])).astype(low_type)
    key_grad = (
        jnp.einsum("hqk,qhd->khd", back_score, query_all, preferred_element_type=wide)
        * score_scale
    )
    qkv_grad = jnp.concatenate(
        [
            grad.reshape(group_count, head_cols).astype(low_type)
            for grad in (query_grad, key_grad, value_grad)
        ],
        1,
    )
    qkv_sums = sum_weight(
        jnp.einsum("td,te->de", own_rows, qkv_grad, preferred_element_type=wide)
    )
    hidden_grad = first_grad + sum_group(
        jnp.einsum("te,de->td", qkv_grad, qkv_weight, preferred_element_type=wide)
    )
    bias_sums = jnp.sum(qkv_grad.astype(wide), axis=0)

    def widen(part):
        full = jnp.zeros((4 * part.shape[0],), wide)
        return lax.dynamic_update_slice_in_dim(full, part, quarter * part.shape[0], 0)

    fsdp_count = lax.axis_size("fsdp")
    all_vectors = jnp.concatenate(
        [
            vector.reshape(fsdp_count, -1)
            for vector in (
                widen(bias_sums[:head_cols]),
                widen(bias_sums[2 * head_cols :]),
                out_bias_grad,
                gain_one_grad,
                shift_one_grad,
                down_bias_grad,
                gain_two_grad,
                shift_two_grad,
                widen(up_bias_grad),
            )
        ],
        1,
    )
    vector_sum = jnp.sum(lax.all_to_all(all_vectors, "fsdp", 0, 0, tiled=True), axis=0)
    vector_sum = vector_sum + swap(vector_sum, TP_BIT)
    vector_grads = [
        vector_sum[i * shard_rows : (i + 1) * shard_rows] for i in range(8)
    ] + [vector_sum[8 * shard_rows :]]

    def columns(array):
        return array.reshape(shard_rows, -1)

    query_sum, key_sum, value_sum = [
        columns(qkv_sums[:, :, i * head_cols : (i + 1) * head_cols]) for i in range(3)
    ]
    return (
        from_slot(output.astype(low_type)),
        from_slot(hidden_grad),
        query_sum,
        vector_grads[0],
        key_sum,
        value_sum,
        vector_grads[1],
        jnp.transpose(columns(out_grad)),
        vector_grads[2],
        vector_grads[3],
        vector_grads[4],
        columns(up_grad),
        vector_grads[8],
        jnp.transpose(columns(down_grad)),
        vector_grads[5],
        vector_grads[6],
        vector_grads[7],
    )

BIT_TP, BIT_CORE, BIT_SIDE, BIT_LOW, BIT_HIGH = 1, 2, 4, 8, 16
TEAM_BITS = (BIT_TP, BIT_LOW, BIT_TP | BIT_LOW)
PART_BITS = (BIT_SIDE, BIT_CORE, BIT_SIDE | BIT_CORE)


class Place:
    def __init__(self):
        fsdp = lax.axis_index("fsdp")
        self.tp = lax.axis_index("tp")
        self.core = fsdp & 1
        self.side = (fsdp >> 1) & 1
        self.low = (fsdp >> 2) & 1
        self.high = fsdp >> 3
        self.quarter = 2 * self.tp + self.low


def run_kernel(body, outs, *operands, scratch=(), name=None):
    specs = [
        pl.BlockSpec(memory_space=pltpu.SMEM if op.dtype == jnp.int32 else pltpu.VMEM)
        for op in operands
    ]
    return pl.pallas_call(
        body,
        out_shape=[jax.ShapeDtypeStruct(shape, kind) for shape, kind in outs],
        in_specs=specs,
        out_specs=[pl.BlockSpec(memory_space=pltpu.VMEM)] * len(outs),
        scratch_shapes=[pltpu.VMEM(shape, kind) for shape, kind in scratch],
        compiler_params=pltpu.CompilerParams(vmem_limit_bytes=8 << 20),
        name=name,
    )(*operands)


def mul(left, right, left_dim=1, right_dim=0):
    return lax.dot_general(
        left, right, (((left_dim,), (right_dim,)), ((), ())), preferred_element_type=wide
    )


def bit_of(index, stride):
    return (index // stride) & 1


def place_of(index, parts, shard_pos):
    here = Place()
    shard = index & (shard_pos - 1)
    high = here.high ^ bit_of(index, shard_pos)
    tp = here.tp ^ bit_of(index, 2 * shard_pos)
    low = here.low ^ bit_of(index, 4 * shard_pos)
    side, core = here.side, here.core
    if parts:
        side = side ^ bit_of(index, 8 * shard_pos)
        core = core ^ bit_of(index, 16 * shard_pos)
    block = (high * 2 + low) * 4 + side * 2 + core
    return (block * 2 + tp) * shard_pos + shard


def live_rows_of(lengths_ref, index, parts, shard_pos):
    return place_of(index, parts, shard_pos) < lengths_ref[Place().high]


def row_of(chip, core, rows):
    return pl.ds(pl.multiple_of((2 * chip + core) * rows, 16), rows)


def join_rows(own_ref, core_ref, full_ref, rows, cols):
    core = Place().core
    for chip in range(own_ref.shape[0]):
        full_ref[row_of(chip, core, rows), :] = own_ref[chip, 0:rows, cols]
        full_ref[row_of(chip, 1 - core, rows), :] = core_ref[chip, 0:rows, cols]


def join_pieces(piece_refs, full_ref, rows, cols):
    here = Place()
    for part, ref in enumerate(piece_refs):
        side, core = here.side ^ (part & 1), here.core ^ (part >> 1)
        for inner in range(4):
            block = (here.high ^ (inner >> 1)) * 2 + (here.low ^ (inner & 1))
            full_ref[row_of(block * 2 + side, core, rows), :] = ref[inner, :, cols]


def split_rows(full_ref, keep_ref, send_ref, rows, cols):
    core = Place().core
    width = cols.stop - cols.start
    for chip in range(keep_ref.shape[0]):
        keep_ref[chip, :, cols] = full_ref[row_of(chip, core, rows), 0:width]
        send_ref[chip, :, cols] = full_ref[row_of(chip, 1 - core, rows), 0:width]


def pack_kernel(
    wq_ref, wk_ref, wv_ref, wo_ref, wu_ref, wd_ref,
    v0_ref, v1_ref, v2_ref, v3_ref, v4_ref, v5_ref, v6_ref, v7_ref, v8_ref,
    first_ref, own_ref, send_ref, down_ref, down_send_ref,
):
    rows = wq_ref.shape[0]
    head_cols = wq_ref.shape[1] // 2
    unit_cols = wu_ref.shape[1] // 2
    for chip in range(first_ref.shape[0]):
        half = (chip // 2) % 2
        heads = slice(half * head_cols, (half + 1) * head_cols)
        for i, ref in enumerate((wq_ref, wk_ref, wv_ref)):
            first_ref[chip, 0:rows, i * head_cols : (i + 1) * head_cols] = ref[:, heads]
    vectors = [
        r[...].astype(wide).reshape(1, rows)
        for r in (v0_ref, v1_ref, v2_ref, v3_ref, v4_ref, v5_ref, v6_ref, v7_ref)
    ]
    block = jnp.concatenate(
        [
            jnp.pad(jnp.concatenate(vectors, 0), ((0, 0), (0, 4 * rows - rows))),
            v8_ref[...].astype(wide).reshape(1, 4 * rows),
            jnp.zeros((7, 4 * rows), wide),
        ],
        0,
    ).astype(low_type)
    for chip in range(first_ref.shape[0]):
        first_ref[chip, rows : rows + 16, 0 : 4 * rows] = block
    out_rows = jnp.transpose(wo_ref[...].astype(wide)).astype(low_type)
    down_rows = jnp.transpose(wd_ref[...].astype(wide)).astype(low_type)
    low = Place().low
    for half in range(2):
        heads = slice(half * head_cols, (half + 1) * head_cols)
        units = slice(half * unit_cols, (half + 1) * unit_cols)

        def put(up_out_ref, down_half_ref):
            up_out_ref[:, 0:unit_cols] = wu_ref[:, units]
            up_out_ref[:, unit_cols : unit_cols + head_cols] = out_rows[:, heads]
            down_half_ref[...] = down_rows[:, units]

        @pl.when(low == half)
        def _():
            put(own_ref, down_ref)

        @pl.when(low != half)
        def _():
            put(send_ref, down_send_ref)


def project_kernel(
    keep_ref, got_ref, tp_ref, low_ref, both_ref, own_ref, core_ref,
    rows_ref, query_ref, pair_ref, weight_ref,
):
    rows = own_ref.shape[1] - 16
    head_cols = query_ref.shape[1]
    join_rows(own_ref, core_ref, weight_ref, rows, slice(None))
    shard = keep_ref.shape[0]
    rows_ref[0:shard, :] = keep_ref[...]
    rows_ref[shard : 2 * shard, :] = got_ref[...]
    for i, ref in enumerate((tp_ref, low_ref, both_ref)):
        rows_ref[2 * shard * (i + 1) : 2 * shard * (i + 2), :] = ref[...]
    here = Place()
    even = here.core == 0
    pieces = []
    for side in range(2):
        own = own_ref[2 * here.quarter + side, rows : rows + 16, 0:rows].astype(wide)
        core = core_ref[2 * here.quarter + side, rows : rows + 16, 0:rows].astype(wide)
        pieces += [jnp.where(even, own, core), jnp.where(even, core, own)]
    biases = jnp.concatenate(pieces, 1)
    query_bias, value_bias = biases[0:1], biases[1:2]
    made = mul(rows_ref[...], weight_ref[...])
    query_ref[...] = (made[:, 0:head_cols] + query_bias).astype(low_type)
    pair_ref[:, 0:head_cols] = made[:, head_cols : 2 * head_cols].astype(low_type)
    pair_ref[:, head_cols:] = (made[:, 2 * head_cols :] + value_bias).astype(low_type)


def head_of(array, head):
    return array[:, head * HD : (head + 1) * HD]


def attend_kernel(shard_pos, lengths_ref, query_ref, p0_ref, p1_ref, p2_ref, p3_ref, low_ref, extra_ref):
    head_cols = query_ref.shape[1]
    count = query_ref.shape[0]
    pair = jnp.concatenate([ref[...] for ref in (p0_ref, p1_ref, p2_ref, p3_ref)], 0)
    keys, values = pair[:, 0:head_cols], pair[:, head_cols:]
    queries = query_ref[...] * HD ** (-0.5)
    lanes = lax.broadcasted_iota(jnp.int32, (1, pair.shape[0]), 1)
    live = live_rows_of(lengths_ref, lanes, True, shard_pos)
    column = lax.broadcasted_iota(jnp.int32, (count, 128), 1)
    stats = jnp.zeros((count, 128), wide)
    parts = []
    for head in range(head_cols // HD):
        scores = mul(head_of(queries, head), head_of(keys, head), 1, 1)
        scores = jnp.where(live, scores, masked_score)
        top = jnp.max(scores, axis=1, keepdims=True)
        grown = jnp.exp(scores - top)
        total = jnp.sum(grown, axis=1, keepdims=True)
        weights = (grown * (1.0 / total)).astype(low_type)
        parts.append(mul(weights, head_of(values, head)))
        log_total = top + jnp.log(total)
        for level in range(3):
            piece = log_total.astype(low_type).astype(wide)
            log_total = log_total - piece
            stats = jnp.where(column == 3 * head + level, piece, stats)
    attended = jnp.concatenate(parts, 1).astype(low_type)
    low_ref[...] = attended
    extra_ref[:, 0:head_cols] = query_ref[...]
    extra_ref[:, head_cols : 2 * head_cols] = attended
    extra_ref[:, 2 * head_cols :] = stats.astype(low_type)


def full_kernel(cols, p0_ref, p1_ref, p2_ref, p3_ref, *outs):
    pieces = (p0_ref, p1_ref, p2_ref, p3_ref)
    for out_ref, (begin, end) in zip(outs, cols):
        join_pieces(pieces, out_ref, p0_ref.shape[1], slice(begin, end))


def lines_kernel(own_ref, core_ref, vector_ref, bias_ref):
    here = Place()
    rows = own_ref.shape[1] - 16
    even = here.core == 0
    vectors = []
    for chip in range(own_ref.shape[0]):
        own = own_ref[chip, rows : rows + 16, 0:rows].astype(wide)
        core = core_ref[chip, rows : rows + 16, 0:rows].astype(wide)
        vectors += [jnp.where(even, own, core), jnp.where(even, core, own)]
    vector_ref[...] = jnp.concatenate(vectors, 1)[0:8]
    biases = []
    for side in range(2):
        own = own_ref[2 * here.quarter + side, rows : rows + 16, 0 : 4 * rows].astype(wide)
        core = core_ref[2 * here.quarter + side, rows : rows + 16, 0 : 4 * rows].astype(wide)
        biases += [jnp.where(even, own, core), jnp.where(even, core, own)]
    bias_ref[...] = jnp.concatenate(biases, 1)[8:9]


def give_out(partial, keep_ref, sends):
    count = keep_ref.shape[0]
    keep_ref[...] = partial[0:count]
    for i, ref in enumerate(sends):
        ref[...] = partial[(i + 1) * count : (i + 2) * count].astype(low_type)


def collect(keep_ref, *got):
    total = keep_ref[...]
    for ref in got:
        total = total + ref[...].astype(wide)
    return total


def out_kernel(low_ref, weight_ref, keep_ref, *sends):
    give_out(mul(low_ref[...], weight_ref[...], 1, 1), keep_ref, sends)


def vector_row(vector_ref, row):
    return vector_ref[row : row + 1, :]


def first_norm_kernel(
    keep_ref, got1_ref, got2_ref, got3_ref, own_ref, slot_ref, vector_ref,
    out_ref, low_ref, normed_ref, scale_ref,
):
    branch = collect(keep_ref, got1_ref, got2_ref, got3_ref)
    rows = jnp.concatenate([own_ref[...], slot_ref[...]], 0).astype(wide)
    normed, scale = norm_parts(rows + branch + vector_row(vector_ref, 2))
    out = normed * vector_row(vector_ref, 3) + vector_row(vector_ref, 4)
    out_ref[...] = out
    low_ref[...] = out.astype(low_type)
    normed_ref[...] = normed
    scale_ref[...] = jnp.broadcast_to(scale, scale_ref.shape)


def spread_of(values):
    scaled = jnp.clip(values * (0.5**0.5), -3.832506856900711, 3.832506856900711)
    square = scaled * scaled
    top = jnp.full_like(values, 0.00022905065861350646)
    for term in (0.0034082910107109506, 0.050955695062380861, 0.18520832239976145, 1.128379143519084):
        top = top * square + term
    under = jnp.full_like(values, -1.1791602954361697e-7)
    for term in (
        0.000023547966471313185,
        0.0010179625278914885,
        0.014070470171167667,
        0.11098505178285362,
        0.49746925110067538,
        1.0,
    ):
        under = under * square + term
    return 0.5 + 0.5 * (scaled * top / under)


def hidden_kernel(
    own_ref, got1_ref, got2_ref, got3_ref, up_ref, down_ref, bias_ref,
    keep_ref, send1_ref, send2_ref, send3_ref, active_ref, slope_ref, rows_ref,
):
    rows = jnp.concatenate([r[...] for r in (own_ref, got1_ref, got2_ref, got3_ref)], 0)
    rows_ref[...] = rows
    preact = mul(rows, up_ref[...]) + bias_ref[...]
    spread = spread_of(preact)
    active = (preact * spread).astype(low_type)
    active_ref[...] = active
    slope_ref[...] = spread + preact * jnp.exp(-0.5 * preact * preact) * (2.0 * math.pi) ** (-0.5)
    give_out(mul(active, down_ref[...], 1, 1), keep_ref, (send1_ref, send2_ref, send3_ref))


def second_norm_kernel(
    lengths_ref, keep_ref, got1_ref, got2_ref, got3_ref, first_ref, own_ref, slot_ref, vector_ref,
    output_ref, grad_ref, low_ref, sums_ref,
):
    shard_pos = own_ref.shape[0]
    branch = collect(keep_ref, got1_ref, got2_ref, got3_ref)
    normed, scale = norm_parts(first_ref[...] + branch + vector_row(vector_ref, 5))
    gain = vector_row(vector_ref, 6)
    output_ref[...] = (normed * gain + vector_row(vector_ref, 7)).astype(low_type)
    index = lax.broadcasted_iota(jnp.int32, (2 * shard_pos, 1), 0)
    live = live_rows_of(lengths_ref, index, False, shard_pos)
    grad = jnp.concatenate([own_ref[...], slot_ref[...]], 0).astype(wide)
    grad = jnp.where(live, grad, 0.0)
    second = norm_back(grad, normed, scale, gain)
    grad_ref[...] = second
    low = second.astype(low_type)
    low_ref[...] = low
    sums_ref[0:1, :] = jnp.sum(low.astype(wide), axis=0, keepdims=True)
    sums_ref[1:2, :] = jnp.sum(grad * normed, axis=0, keepdims=True)
    sums_ref[2:3, :] = jnp.sum(grad, axis=0, keepdims=True)


def hidden_back_kernel(
    own_ref, got1_ref, got2_ref, got3_ref, slope_ref, up_ref, down_ref,
    keep_ref, send1_ref, send2_ref, send3_ref, pre_ref, rows_ref, sums_ref,
):
    rows = jnp.concatenate([r[...] for r in (own_ref, got1_ref, got2_ref, got3_ref)], 0)
    rows_ref[...] = rows
    pre = (mul(rows, down_ref[...]) * slope_ref[...]).astype(low_type)
    pre_ref[...] = pre
    sums_ref[...] = jnp.sum(pre.astype(wide), axis=0, keepdims=True)
    give_out(mul(pre, up_ref[...], 1, 1), keep_ref, (send1_ref, send2_ref, send3_ref))


def weight_kernel(pairs, extra, *refs):
    operands = refs[: 2 * pairs + extra]
    keep_ref, send_ref, full_ref = refs[2 * pairs + extra :]
    rows = keep_ref.shape[1]
    begin = 0
    for i in range(pairs):
        left, right = operands[2 * i], operands[2 * i + 1]
        cols = right.shape[1]
        full_ref[:, 0:cols] = mul(left[...], right[...], 0, 0).astype(low_type)
        split_rows(full_ref, keep_ref, send_ref, rows, slice(begin, begin + cols))
        begin += cols
    if extra:
        mine, other = operands[-2:]
        cols = 128
        total = mine[...] + other[...]
        total = jnp.concatenate([total, jnp.zeros((cols - total.shape[0], total.shape[1]), wide)], 0)
        full_ref[:, 0:cols] = jnp.transpose(total).astype(low_type)
        split_rows(full_ref, keep_ref, send_ref, rows, slice(begin, begin + cols))


def fold_kernel(bits, stride, keep_ref, got_ref, *outs):
    here = Place()
    own = [getattr(here, bit) for bit in bits]
    count = outs[0].shape[0]
    for choice, out_ref in enumerate(outs):
        for block in range(count):
            index = block * stride[0]
            for i, (bit, step) in enumerate(zip(own, stride[1:])):
                index = index + (bit ^ ((choice >> i) & 1)) * step
            total = keep_ref[index].astype(wide) + got_ref[index].astype(wide)
            out_ref[block] = total.astype(out_ref.dtype)


def final_fold_kernel(*refs):
    inputs, (own_ref, send_ref) = refs[:-2], refs[-2:]
    low = Place().low
    for choice, out_ref in ((low, own_ref), (1 - low, send_ref)):
        total = inputs[0][choice].astype(wide)
        for ref in inputs[1:]:
            total = total + ref[choice].astype(wide)
        out_ref[...] = total.astype(out_ref.dtype)


def total_kernel(spans, own_ref, got_ref, *outs):
    even = Place().low == 0
    for out_ref, (begin, end, turned) in zip(outs, spans):
        cols = end - begin
        own = own_ref[:, begin:end]
        got = got_ref[:, begin:end].astype(wide)
        if turned is None:
            out_ref[...] = jnp.transpose(own + got)
            continue
        halves = jnp.where(even, own, got), jnp.where(even, got, own)
        for i, half in enumerate(halves):
            if turned:
                out_ref[i * cols : (i + 1) * cols, :] = jnp.transpose(half)
            else:
                out_ref[:, i * cols : (i + 1) * cols] = half


def first_back_kernel(
    keep_ref, got1_ref, got2_ref, got3_ref, second_ref, normed_ref, scale_ref, vector_ref,
    grad_ref, low_ref, sums_ref,
):
    grad = second_ref[...] + collect(keep_ref, got1_ref, got2_ref, got3_ref)
    normed = normed_ref[...]
    first = norm_back(grad, normed, scale_ref[:, 0:1], vector_row(vector_ref, 3))
    grad_ref[...] = first
    low = first.astype(low_type)
    low_ref[...] = low
    sums_ref[0:1, :] = jnp.sum(low.astype(wide), axis=0, keepdims=True)
    sums_ref[1:2, :] = jnp.sum(grad * normed, axis=0, keepdims=True)
    sums_ref[2:3, :] = jnp.sum(grad, axis=0, keepdims=True)


def attended_back_kernel(
    own_ref, got1_ref, got2_ref, got3_ref, weight_ref, grad_ref, rows_ref, sums_ref
):
    rows = jnp.concatenate([r[...] for r in (own_ref, got1_ref, got2_ref, got3_ref)], 0)
    rows_ref[...] = rows
    made = mul(rows, weight_ref[...])
    grad_ref[...] = made.astype(low_type)
    sums_ref[...] = jnp.sum(made, axis=0, keepdims=True)


def stat_of(extra, head_cols, head):
    base = 2 * head_cols + 3 * head
    total = extra[:, base : base + 1].astype(wide)
    for level in (1, 2):
        total = total + extra[:, base + level : base + level + 1].astype(wide)
    return total


def query_back_kernel(
    shard_pos, lengths_ref, extra_ref, grad_ref, p0_ref, p1_ref, p2_ref, p3_ref, out_ref, sums_ref
):
    head_cols = out_ref.shape[1]
    pair = jnp.concatenate([ref[...] for ref in (p0_ref, p1_ref, p2_ref, p3_ref)], 0)
    keys, values = pair[:, 0:head_cols], pair[:, head_cols:]
    extra, grad = extra_ref[...], grad_ref[...]
    queries = extra[:, 0:head_cols] * HD ** (-0.5)
    both = grad.astype(wide) * extra[:, head_cols : 2 * head_cols].astype(wide)
    lanes = lax.broadcasted_iota(jnp.int32, (1, pair.shape[0]), 1)
    live = live_rows_of(lengths_ref, lanes, True, shard_pos)
    parts = []
    for head in range(head_cols // HD):
        scores = mul(head_of(queries, head), head_of(keys, head), 1, 1)
        scores = jnp.where(live, scores, masked_score)
        weights = jnp.exp(scores - stat_of(extra, head_cols, head))
        delta = jnp.sum(head_of(both, head), axis=1, keepdims=True)
        weight_grad = mul(head_of(grad, head), head_of(values, head), 1, 1)
        score_grad = (weights * (weight_grad - delta)).astype(low_type)
        parts.append(mul(score_grad, head_of(keys, head)))
    made = (jnp.concatenate(parts, 1) * HD ** (-0.5)).astype(low_type)
    out_ref[...] = made
    sums_ref[...] = jnp.sum(made.astype(wide), axis=0, keepdims=True)


def pair_back_kernel(
    shard_pos, lengths_ref, pair_ref, query_grad_ref, weight_ref,
    e0_ref, e1_ref, e2_ref, e3_ref, g0_ref, g1_ref, g2_ref, g3_ref,
    keep_ref, send1_ref, send2_ref, send3_ref, made_ref,
):
    head_cols = query_grad_ref.shape[1]
    pair = pair_ref[...]
    keys, values = pair[:, 0:head_cols], pair[:, head_cols:]
    extra = jnp.concatenate([ref[...] for ref in (e0_ref, e1_ref, e2_ref, e3_ref)], 0)
    grad = jnp.concatenate([ref[...] for ref in (g0_ref, g1_ref, g2_ref, g3_ref)], 0)
    queries = extra[:, 0:head_cols] * HD ** (-0.5)
    both = grad.astype(wide) * extra[:, head_cols : 2 * head_cols].astype(wide)
    lanes = lax.broadcasted_iota(jnp.int32, (1, pair.shape[0]), 1)
    live = live_rows_of(lengths_ref, lanes, False, shard_pos)
    key_parts, value_parts = [], []
    for head in range(head_cols // HD):
        scores = mul(head_of(queries, head), head_of(keys, head), 1, 1)
        scores = jnp.where(live, scores, masked_score)
        weights = jnp.exp(scores - stat_of(extra, head_cols, head))
        delta = jnp.sum(head_of(both, head), axis=1, keepdims=True)
        weight_grad = mul(head_of(grad, head), head_of(values, head), 1, 1)
        score_grad = (weights * (weight_grad - delta)).astype(low_type)
        key_parts.append(mul(score_grad, head_of(queries, head), 0, 0))
        value_parts.append(mul(weights.astype(low_type), head_of(grad, head), 0, 0))
    made = jnp.concatenate([part.astype(low_type) for part in key_parts + value_parts], 1)
    made_ref[...] = made
    made = jnp.concatenate([query_grad_ref[...], made], 1)
    give_out(mul(made, weight_ref[...], 1, 1), keep_ref, (send1_ref, send2_ref, send3_ref))


def last_kernel(keep_ref, got1_ref, got2_ref, got3_ref, first_ref, own_ref, send_ref):
    total = first_ref[...] + collect(keep_ref, got1_ref, got2_ref, got3_ref)
    count = own_ref.shape[0]
    own_ref[...] = total[0:count]
    send_ref[...] = total[count:]


def vectors_kernel(shards, query_ref, value_ref, first_ref, second_ref, unit_ref, out_ref):
    width = out_ref.shape[1] // shards
    per = shards // 4
    quarter = Place().quarter
    out_ref[...] = jnp.zeros_like(out_ref)
    out_ref[2:5, :] = first_ref[0:3, :]
    out_ref[5:8, :] = second_ref[0:3, :]
    for which in range(4):

        @pl.when(quarter == which)
        def _():
            span = slice(which * per * width, (which + 1) * per * width)
            out_ref[0:1, span] = query_ref[...]
            out_ref[1:2, span] = value_ref[...]
            for i in range(4):
                parts = []
                for local in range(per):
                    begin = (4 * local + i) * width
                    parts.append(unit_ref[:, begin : begin + width])
                out_ref[8 + i : 9 + i, span] = jnp.concatenate(parts, 1)


def send_team(parts):
    return tuple(swap(part, bit) for part, bit in zip(parts, TEAM_BITS))


def gather_team(rows):
    return tuple(swap(rows, bit) for bit in TEAM_BITS)


def gather_parts(rows):
    side = swap(rows, BIT_SIDE)
    return rows, side, swap(rows, BIT_CORE), swap(side, BIT_CORE)


def over_chips(values):
    total = device_count()
    groups = [list(range(first, total, 4)) for first in range(4)]
    return lax.all_to_all(values, AXES, 0, 0, axis_index_groups=groups)


def local_32(
    hidden_in,
    cotangent,
    lengths,
    w_query,
    b_query,
    w_key,
    w_value,
    b_value,
    w_out,
    b_out,
    first_gain,
    first_shift,
    w_up,
    b_up,
    w_down,
    b_down,
    second_gain,
    second_shift,
):
    fsdp_index = lax.axis_index("fsdp")
    tp_bit = lax.axis_index("tp")
    core_bit = fsdp_index % 2
    side_bit = (fsdp_index // 2) % 2
    low_bit = (fsdp_index // 4) % 2
    high_bit = fsdp_index // 8
    shard_pos, seq_count, width = hidden_in.shape
    rows_here = 2 * shard_pos
    group = 4 * rows_here
    shard_rows = w_query.shape[0]
    head_cols = w_query.shape[1] // 2
    unit_cols = w_up.shape[1] // 2
    chips = lax.axis_size("fsdp") // 2
    def slot_parts(values):
        own = lax.dynamic_index_in_dim(values, high_bit, 1, keepdims=False)
        other = lax.dynamic_index_in_dim(values, 1 - high_bit, 1, keepdims=False)
        return own, swap(other, BIT_HIGH)

    def from_slot(own, returned):
        return in_order(high_bit, own, returned, 1)

    up_out = (shard_rows, unit_cols + head_cols)
    down = (shard_rows, unit_cols)
    first_pack, up_own, up_send, down_own, down_send = run_kernel(
        pack_kernel,
        [
            ((chips, shard_rows + 16, 3 * head_cols), low_type),
            (up_out, low_type),
            (up_out, low_type),
            (down, low_type),
            (down, low_type),
        ],
        w_query, w_key, w_value, w_out, w_up, w_down,
        b_query, b_value, b_out, first_gain, first_shift, b_down, second_gain, second_shift, b_up,
        name="pack",
    )

    def all_rows(own, send):
        pieces = jnp.stack([own, swap(send, BIT_LOW)])
        pieces = jnp.concatenate([pieces, swap(pieces, BIT_HIGH)], 0)
        return gather_parts(pieces)

    hidden_own, hidden_slot = slot_parts(hidden_in)
    first_own = over_chips(first_pack)
    first_core = swap(first_own, BIT_CORE)
    team_rows = gather_team(jnp.concatenate([hidden_own, hidden_slot], 0))
    up_pieces = all_rows(up_own, up_send)
    down_pieces = all_rows(down_own, down_send)
    cot_own, cot_slot = slot_parts(cotangent)

    group_rows, queries, pair, qkv_weight = run_kernel(
        project_kernel,
        [
            ((group, width), low_type),
            ((group, head_cols), low_type),
            ((group, 2 * head_cols), low_type),
            ((width, 3 * head_cols), low_type),
        ],
        hidden_own, hidden_slot, *team_rows, first_own, first_core,
        name="project",
    )
    pairs = gather_parts(pair)
    vectors, up_bias = run_kernel(
        lines_kernel, [((8, width), wide), ((1, unit_cols), wide)], first_own, first_core,
        name="lines",
    )
    attended_low, extra = run_kernel(
        functools.partial(attend_kernel, shard_pos),
        [((group, head_cols), low_type), ((group, 2 * head_cols + 128), low_type)],
        lengths, queries, *pairs,
        name="attend",
    )
    up_weight, out_weight = run_kernel(
        functools.partial(full_kernel, ((0, unit_cols), (unit_cols, unit_cols + head_cols))),
        [((width, unit_cols), low_type), ((width, head_cols), low_type)],
        *up_pieces,
        name="full_up_out",
    )
    (down_weight,) = run_kernel(
        functools.partial(full_kernel, ((0, unit_cols),)),
        [((width, unit_cols), low_type)],
        *down_pieces,
        name="full_down",
    )
    rows_shape = (rows_here, width)
    given = [(rows_shape, wide)] + [(rows_shape, low_type)] * 3

    keep, *sends = run_kernel(out_kernel, given, attended_low, out_weight, name="out")
    first_out, first_low, normed, scale = run_kernel(
        first_norm_kernel,
        [(rows_shape, wide), (rows_shape, low_type), (rows_shape, wide), ((rows_here, 128), wide)],
        keep, *send_team(sends), hidden_own, hidden_slot, vectors,
        name="first_norm",
    )
    extras = gather_parts(extra)
    keep, s1, s2, s3, active, slope, first_rows = run_kernel(
        hidden_kernel,
        given
        + [((group, unit_cols), low_type), ((group, unit_cols), wide), ((group, width), low_type)],
        first_low, *gather_team(first_low), up_weight, down_weight, up_bias,
        name="hidden",
    )
    output, second_grad, second_low, second_sums = run_kernel(
        second_norm_kernel,
        [(rows_shape, low_type), (rows_shape, wide), (rows_shape, low_type), ((8, width), wide)],
        lengths, keep, *send_team((s1, s2, s3)), first_out, cot_own, cot_slot, vectors,
        name="second_norm",
    )
    keep, s1, s2, s3, pre_grad, second_rows, unit_sums = run_kernel(
        hidden_back_kernel,
        given
        + [((group, unit_cols), low_type), ((group, width), low_type), ((1, unit_cols), wide)],
        second_low, *gather_team(second_low), slope, up_weight, down_weight,
        name="hidden_back",
    )
    backs = send_team((s1, s2, s3))

    def weight_parts(operands, name, extra=()):
        cols = sum(right.shape[1] for right in operands[1::2]) + (128 if extra else 0)
        shape = (chips, shard_rows, cols)
        most = max(right.shape[1] for right in operands[1::2])
        kept, sent = run_kernel(
            functools.partial(weight_kernel, len(operands) // 2, len(extra)),
            [(shape, low_type), (shape, low_type)],
            *operands, *extra,
            scratch=[((width, most), low_type)],
            name=name,
        )
        return kept, swap(sent, BIT_CORE)

    def finish(folded, spans, name):
        own, send = run_kernel(
            final_fold_kernel,
            [(folded[0].shape[1:], wide), (folded[0].shape[1:], low_type)],
            *folded,
            name=name + "_low",
        )
        outs = []
        for begin, end, turned in spans:
            across = 2 * (end - begin)
            if turned is None:
                outs.append((end - begin, shard_rows))
            else:
                outs.append((across, shard_rows) if turned else (shard_rows, across))
        return run_kernel(
            functools.partial(total_kernel, spans), [(s, wide) for s in outs],
            own, swap(send, BIT_LOW), name=name + "_total",
        )

    def in_steps(kept, got, spans, name):
        for bit, stride, mask in (("side", (2, 1), BIT_SIDE), ("high", (1, 2), BIT_HIGH)):
            shape = (kept.shape[0] // 2,) + kept.shape[1:]
            kept, sent = run_kernel(
                functools.partial(fold_kernel, (bit,), stride),
                [(shape, wide), (shape, low_type)],
                kept, got,
                name=name + "_" + bit,
            )
            got = swap(sent, mask)
        return finish((kept, got), spans, name)

    def at_once(kept, got, spans, name):
        shape = (kept.shape[0] // 4,) + kept.shape[1:]
        kept, *sent = run_kernel(
            functools.partial(fold_kernel, ("side", "high"), (2, 1, 4)),
            [(shape, wide)] + [(shape, low_type)] * 3,
            kept, got,
            name=name + "_fold",
        )
        masks = (BIT_SIDE, BIT_HIGH, BIT_SIDE | BIT_HIGH)
        got = [swap(part, mask) for part, mask in zip(sent, masks)]
        return finish((kept, *got), spans, name)

    down_grad, up_grad = in_steps(
        *weight_parts((second_rows, active, first_rows, pre_grad), "unit_weights"),
        ((0, unit_cols, True), (unit_cols, 2 * unit_cols, False)),
        "units",
    )
    first_grad, one_low, first_sums = run_kernel(
        first_back_kernel,
        [(rows_shape, wide), (rows_shape, low_type), ((8, width), wide)],
        keep, *backs, second_grad, normed, scale, vectors,
        name="first_back",
    )
    attended_grad, one_rows, value_sums = run_kernel(
        attended_back_kernel,
        [((group, head_cols), low_type), ((group, width), low_type), ((1, head_cols), wide)],
        one_low, *gather_team(one_low), out_weight,
        name="attended_back",
    )
    grads = gather_parts(attended_grad)
    query_grad, query_sums = run_kernel(
        functools.partial(query_back_kernel, shard_pos),
        [((group, head_cols), low_type), ((1, head_cols), wide)],
        lengths, extra, attended_grad, *pairs,
        name="query_back",
    )
    (sums,) = run_kernel(
        functools.partial(vectors_kernel, 2 * chips),
        [((16, width), wide)],
        query_sums, value_sums, first_sums, second_sums, unit_sums,
        name="vectors",
    )
    out_grad, query_total, shares = at_once(
        *weight_parts(
            (one_rows, attended_low, group_rows, query_grad),
            "early_weights",
            (sums, swap(sums, BIT_TP)),
        ),
        (
            (0, head_cols, True),
            (head_cols, 2 * head_cols, False),
            (2 * head_cols, 2 * head_cols + 128, None),
        ),
        "early",
    )
    keep, s1, s2, s3, pair_grad = run_kernel(
        functools.partial(pair_back_kernel, shard_pos),
        given + [((group, 2 * head_cols), low_type)],
        lengths, pair, query_grad, qkv_weight, *extras, *grads,
        name="pair_back",
    )
    lasts = send_team((s1, s2, s3))
    key_total, value_total = at_once(
        *weight_parts((group_rows, pair_grad), "late_weights"),
        ((0, head_cols, False), (head_cols, 2 * head_cols, False)),
        "late",
    )
    grad_own, grad_send = run_kernel(
        last_kernel,
        [((shard_pos, width), wide), ((shard_pos, width), wide)],
        keep, *lasts, first_grad,
        name="last",
    )
    return (
        from_slot(output[:shard_pos], swap(output[shard_pos:], BIT_HIGH)),
        from_slot(grad_own, swap(grad_send, BIT_HIGH)),
        query_total,
        shares[0],
        key_total,
        value_total,
        shares[1],
        out_grad,
        shares[2],
        shares[3],
        shares[4],
        up_grad,
        shares[8:12].reshape(-1),
        down_grad,
        shares[5],
        shares[6],
        shares[7],
    )


def solution(mesh):
    in_specs = (
        P(("fsdp", "tp"), None, None),
        P(("fsdp", "tp"), None, None),
        P(),
        P("fsdp", "tp"),
        P("fsdp"),
        P("fsdp", "tp"),
        P("fsdp", "tp"),
        P("fsdp"),
        P("tp", "fsdp"),
        P("fsdp"),
        P("fsdp"),
        P("fsdp"),
        P("fsdp", "tp"),
        P("fsdp"),
        P("tp", "fsdp"),
        P("fsdp"),
        P("fsdp"),
        P("fsdp"),
    )
    out_specs = (
        P(("fsdp", "tp"), None, None),
        P(("fsdp", "tp"), None, None),
        P("fsdp", "tp"),
        P("fsdp"),
        P("fsdp", "tp"),
        P("fsdp", "tp"),
        P("fsdp"),
        P("tp", "fsdp"),
        P("fsdp"),
        P("fsdp"),
        P("fsdp"),
        P("fsdp", "tp"),
        P("fsdp"),
        P("tp", "fsdp"),
        P("fsdp"),
        P("fsdp"),
        P("fsdp"),
    )
    program = local_32 if mesh.shape["fsdp"] == 16 else local
    return jax.shard_map(program, mesh=mesh, in_specs=in_specs, out_specs=out_specs, check_vma=False)
```

```python
import functools
import math

import jax
import jax.numpy as jnp
from jax import lax
from jax.experimental import pallas as pl
from jax.experimental.pallas import tpu as pltpu
from jax.sharding import PartitionSpec as P

HD = 64
layer_eps = 1e-12
masked_score = -1e30
AXES = ("fsdp", "tp")
low_type = jnp.bfloat16
wide = jnp.float32

TP_BIT, CORE_BIT, SLOT_BIT, GROUP = 1, 2, 4, 8


def device_count():
    return lax.axis_size("fsdp") * lax.axis_size("tp")


def swap(values, bit):
    return lax.ppermute(values, AXES, [(i, i ^ bit) for i in range(device_count())])


def over_blocks(values):
    total = device_count()
    groups = [list(range(first, total, GROUP)) for first in range(GROUP)]
    return lax.all_to_all(values, AXES, 0, 0, axis_index_groups=groups)


def gather_blocks(values):
    blocks = device_count() // GROUP
    return over_blocks(jnp.broadcast_to(values[None], (blocks,) + values.shape))


def in_order(first_bit, own, other, axis):
    return jnp.where(
        first_bit == 0, jnp.stack([own, other], axis), jnp.stack([other, own], axis)
    )


def gather_group(rows):
    pair = jnp.concatenate([rows, swap(rows, TP_BIT)], 0)
    return jnp.concatenate([pair, swap(pair, CORE_BIT)], 0)


def sum_group(partial):
    half = partial.shape[0] // 2
    kept = partial[:half] + swap(partial[half:].astype(low_type), CORE_BIT).astype(wide)
    quarter = half // 2
    return kept[:quarter] + swap(kept[quarter:].astype(low_type), TP_BIT).astype(wide)


def norm_parts(values):
    centre = values - jnp.mean(values, axis=-1, keepdims=True)
    spread = jnp.mean(centre * centre, axis=-1, keepdims=True)
    scale = lax.rsqrt(spread + layer_eps)
    return centre * scale, scale


def norm_back(grad, normed, scale, gain):
    scaled = grad * gain
    mean_one = jnp.mean(scaled, axis=-1, keepdims=True)
    mean_two = jnp.mean(scaled * normed, axis=-1, keepdims=True)
    return scale * (scaled - mean_one - normed * mean_two)


def local(
    hidden_in,
    cotangent,
    lengths,
    w_query,
    b_query,
    w_key,
    w_value,
    b_value,
    w_out,
    b_out,
    first_gain,
    first_shift,
    w_up,
    b_up,
    w_down,
    b_down,
    second_gain,
    second_shift,
):
    fsdp_index = lax.axis_index("fsdp")
    tp_bit = lax.axis_index("tp")
    core_bit = fsdp_index % 2
    slot_bit = (fsdp_index // 2) % 2
    block = fsdp_index // 4
    blocks = lax.axis_size("fsdp") // 4
    shard_pos, seq_count, width = hidden_in.shape
    rows_here = 2 * shard_pos
    shard_rows = w_query.shape[0]
    head_cols = w_query.shape[1] // 2
    unit_cols = w_up.shape[1] // 2
    heads = head_cols // HD
    score_scale = HD ** (-0.5)

    def halves(weight):
        return weight.reshape(shard_rows, 2, weight.shape[1] // 2)

    def for_core(parts, which):
        return jnp.concatenate(
            [lax.dynamic_index_in_dim(part, which, 1, keepdims=False) for part in parts], 1
        )

    vectors = jnp.concatenate(
        [
            vector.reshape(shard_rows, -1)
            for vector in (
                b_query,
                b_value,
                b_out,
                first_gain,
                first_shift,
                b_down,
                second_gain,
                second_shift,
                b_up,
            )
        ],
        1,
    )
    vectors = jnp.pad(vectors, ((0, 0), (0, 128 - vectors.shape[1])))
    first_parts = [halves(w_query), halves(w_key), halves(w_value)]
    later_parts = [halves(jnp.transpose(w_out)), halves(w_up), halves(jnp.transpose(w_down))]

    def to_core(parts, shared):
        own, other = for_core(parts, core_bit), for_core(parts, 1 - core_bit)
        if shared is not None:
            own = jnp.concatenate([own, shared], 1)
            other = jnp.concatenate([other, shared], 1)
        return in_order(core_bit, own, swap(other, CORE_BIT), 0)

    def full_rows(pieces):
        stacked = in_order(slot_bit, pieces, swap(pieces, SLOT_BIT), 1)
        return stacked.reshape(width, pieces.shape[-1])

    def to_slot(values):
        own = lax.dynamic_index_in_dim(values, slot_bit, 1, keepdims=False)
        other = lax.dynamic_index_in_dim(values, 1 - slot_bit, 1, keepdims=False)
        return jnp.concatenate([own, swap(other, SLOT_BIT)], 0)

    def from_slot(rows):
        returned = swap(rows[shard_pos:], SLOT_BIT)
        return in_order(slot_bit, rows[:shard_pos], returned, 1)

    rows_low = to_slot(hidden_in)
    first_pack = to_core(first_parts, vectors)
    gathered_rows = gather_blocks(rows_low)
    gathered_first = gather_blocks(first_pack.reshape(2 * shard_rows, -1))
    pair_rows = jnp.stack([gathered_rows, swap(gathered_rows, TP_BIT)], 1)
    slot_rows = jnp.stack([pair_rows, swap(pair_rows, CORE_BIT)], 1)
    slot_rows = slot_rows.reshape(-1, width)
    first_full = full_rows(gathered_first)
    later_pack = to_core(later_parts, None).reshape(2 * shard_rows, -1)
    out_piece = gather_blocks(later_pack[:, :head_cols])
    up_piece = gather_blocks(later_pack[:, head_cols : head_cols + unit_cols])
    down_piece = gather_blocks(later_pack[:, head_cols + unit_cols :])
    out_weight = full_rows(out_piece)
    up_weight = full_rows(up_piece)
    down_weight = full_rows(down_piece)
    qkv_weight = first_full[:, : 3 * head_cols]
    vector_cols = first_full[:, 3 * head_cols :].astype(wide)
    (
        query_bias_all,
        value_bias_all,
        out_bias,
        gain_one,
        shift_one,
        down_bias,
        gain_two,
        shift_two,
    ) = [vector_cols[:, i] for i in range(8)]
    up_bias_all = vector_cols[:, 8 : 8 + b_up.shape[0] // shard_rows].reshape(-1)
    quarter = 2 * tp_bit + core_bit
    query_bias = lax.dynamic_slice_in_dim(query_bias_all, quarter * head_cols, head_cols)
    value_bias = lax.dynamic_slice_in_dim(value_bias_all, quarter * head_cols, head_cols)
    up_bias = lax.dynamic_slice_in_dim(up_bias_all, quarter * unit_cols, unit_cols)

    def positions_of(block_ids):
        shape = (block_ids.shape[0], 2, 2, 2, shard_pos)
        iota = lambda dim: lax.broadcasted_iota(jnp.int32, shape, dim)
        place = block_ids.reshape(-1, 1, 1, 1, 1) * 2 + (iota(3) ^ slot_bit)
        place = (place * 2 + (iota(1) ^ core_bit)) * 2 + (iota(2) ^ tp_bit)
        return (place * shard_pos + iota(4)).reshape(-1)

    length = lax.dynamic_index_in_dim(lengths, slot_bit, 0, keepdims=False)
    slot_live = positions_of(jnp.arange(blocks)) < length
    group_live = positions_of(block.reshape(1)) < length
    row_live = group_live[:rows_here]

    group_count = 4 * rows_here
    own_rows = lax.dynamic_slice_in_dim(slot_rows, block * group_count, group_count, 0)

    def as_heads(values):
        return values.reshape(values.shape[0], heads, HD)

    queries = (
        jnp.dot(slot_rows, qkv_weight[:, :head_cols], preferred_element_type=wide) + query_bias
    ).astype(low_type)
    keys = jnp.dot(
        slot_rows, qkv_weight[:, head_cols : 2 * head_cols], preferred_element_type=wide
    ).astype(low_type)
    values = (
        jnp.dot(slot_rows, qkv_weight[:, 2 * head_cols :], preferred_element_type=wide)
        + value_bias
    ).astype(low_type)
    query_all, key_all, value_all = as_heads(queries), as_heads(keys), as_heads(values)

    def own_of(array):
        return lax.dynamic_slice_in_dim(array, block * group_count, group_count, 0)

    query_own, key_own, value_own = own_of(query_all), own_of(key_all), own_of(value_all)
    scores = (
        jnp.einsum("qhd,khd->hqk", query_own, key_all, preferred_element_type=wide) * score_scale
    )
    masked = jnp.where(slot_live[None, None, :], scores, masked_score)
    top = jnp.max(masked, axis=2, keepdims=True)
    total = jnp.sum(jnp.exp(masked - top), axis=2, keepdims=True)
    log_total = top + jnp.log(total)
    weights = jnp.exp(masked - log_total)
    attended = jnp.einsum(
        "hqk,khd->qhd", weights.astype(low_type), value_all, preferred_element_type=wide
    )
    attended_low = attended.reshape(group_count, head_cols).astype(low_type)

    branch_one = sum_group(
        jnp.einsum("th,dh->td", attended_low, out_weight, preferred_element_type=wide)
    )
    first_sum = rows_low.astype(wide) + branch_one + out_bias
    normed_one, scale_one = norm_parts(first_sum)
    first_out = normed_one * gain_one + shift_one
    group_first = gather_group(first_out.astype(low_type))
    preact = jnp.dot(group_first, up_weight, preferred_element_type=wide) + up_bias
    spread = 0.5 * (1.0 + lax.erf(preact * (0.5**0.5)))
    active_low = (preact * spread).astype(low_type)
    branch_two = sum_group(
        jnp.einsum("tf,df->td", active_low, down_weight, preferred_element_type=wide)
    )
    normed_two, scale_two = norm_parts(first_out + branch_two + down_bias)
    output = normed_two * gain_two + shift_two
    grad_out = to_slot(cotangent).astype(wide) * row_live[:, None].astype(wide)
    second_grad = norm_back(grad_out, normed_two, scale_two, gain_two)
    gain_two_grad = jnp.sum(grad_out * normed_two, axis=0)
    shift_two_grad = jnp.sum(grad_out, axis=0)
    branch_two_grad = second_grad.astype(low_type)
    down_bias_grad = jnp.sum(branch_two_grad.astype(wide), axis=0)
    group_two = gather_group(branch_two_grad)
    active_grad = jnp.einsum("td,df->tf", group_two, down_weight, preferred_element_type=wide)
    slope = spread + preact * jnp.exp(-0.5 * preact * preact) * (2.0 * jnp.pi) ** (-0.5)
    preact_grad = (active_grad * slope).astype(low_type)
    up_bias_grad = jnp.sum(preact_grad.astype(wide), axis=0)
    first_out_grad = second_grad + sum_group(
        jnp.einsum("tf,df->td", preact_grad, up_weight, preferred_element_type=wide)
    )

    def sum_weight(partial):
        cols = partial.shape[1]
        split = partial.astype(low_type).reshape(blocks, 2, 2 * shard_rows, cols)
        own = lax.dynamic_index_in_dim(split, slot_bit, 1, keepdims=False)
        other = lax.dynamic_index_in_dim(split, 1 - slot_bit, 1, keepdims=False)
        half = own.astype(wide) + swap(other, SLOT_BIT).astype(wide)
        pieces = over_blocks(half.astype(low_type))
        summed = jnp.sum(pieces.astype(wide), axis=0).reshape(2, shard_rows, cols)
        mine = lax.dynamic_index_in_dim(summed, core_bit, 0, keepdims=False)
        theirs = lax.dynamic_index_in_dim(summed, 1 - core_bit, 0, keepdims=False)
        return in_order(core_bit, mine, swap(theirs, CORE_BIT), 1)

    up_grad = sum_weight(
        jnp.einsum("td,tf->df", group_first, preact_grad, preferred_element_type=wide)
    )
    down_grad = sum_weight(
        jnp.einsum("td,tf->df", group_two, active_low, preferred_element_type=wide)
    )
    gain_one_grad = jnp.sum(first_out_grad * normed_one, axis=0)
    shift_one_grad = jnp.sum(first_out_grad, axis=0)
    first_grad = norm_back(first_out_grad, normed_one, scale_one, gain_one)
    branch_one_grad = first_grad.astype(low_type)
    out_bias_grad = jnp.sum(branch_one_grad.astype(wide), axis=0)
    group_one = gather_group(branch_one_grad)
    attended_grad = jnp.dot(group_one, out_weight, preferred_element_type=wide).astype(low_type)
    grad_all = as_heads(gather_blocks(attended_grad).reshape(-1, head_cols))
    grad_own = as_heads(attended_grad)
    delta = jnp.einsum("qhd,qhd->hq", grad_own.astype(wide), attended)
    row_stats = gather_blocks(jnp.stack([log_total[:, :, 0], delta]))
    row_stats = jnp.moveaxis(row_stats, 0, 2).reshape(2, heads, -1)
    out_grad = sum_weight(
        jnp.einsum("td,th->dh", group_one, attended_low, preferred_element_type=wide)
    )

    weight_grad = jnp.einsum("qhd,khd->hqk", grad_own, value_all, preferred_element_type=wide)
    score_grad = (weights * (weight_grad - delta[:, :, None])).astype(low_type)
    query_grad = (
        jnp.einsum("hqk,khd->qhd", score_grad, key_all, preferred_element_type=wide) * score_scale
    )
    scores_back = (
        jnp.einsum("qhd,khd->hqk", query_all, key_own, preferred_element_type=wide) * score_scale
    )
    weights_back = jnp.where(
        group_live[None, None, :], jnp.exp(scores_back - row_stats[0][:, :, None]), 0.0
    )
    value_grad = jnp.einsum(
        "hqk,qhd->khd", weights_back.astype(low_type), grad_all, preferred_element_type=wide
    )
    back_grad = jnp.einsum("qhd,khd->hqk", grad_all, value_own, preferred_element_type=wide)
    back_score = (weights_back * (back_grad - row_stats[1][:, :, None])).astype(low_type)
    key_grad = (
        jnp.einsum("hqk,qhd->khd", back_score, query_all, preferred_element_type=wide)
        * score_scale
    )
    qkv_grad = jnp.concatenate(
        [
            grad.reshape(group_count, head_cols).astype(low_type)
            for grad in (query_grad, key_grad, value_grad)
        ],
        1,
    )
    qkv_sums = sum_weight(
        jnp.einsum("td,te->de", own_rows, qkv_grad, preferred_element_type=wide)
    )
    hidden_grad = first_grad + sum_group(
        jnp.einsum("te,de->td", qkv_grad, qkv_weight, preferred_element_type=wide)
    )
    bias_sums = jnp.sum(qkv_grad.astype(wide), axis=0)

    def widen(part):
        full = jnp.zeros((4 * part.shape[0],), wide)
        return lax.dynamic_update_slice_in_dim(full, part, quarter * part.shape[0], 0)

    fsdp_count = lax.axis_size("fsdp")
    all_vectors = jnp.concatenate(
        [
            vector.reshape(fsdp_count, -1)
            for vector in (
                widen(bias_sums[:head_cols]),
                widen(bias_sums[2 * head_cols :]),
                out_bias_grad,
                gain_one_grad,
                shift_one_grad,
                down_bias_grad,
                gain_two_grad,
                shift_two_grad,
                widen(up_bias_grad),
            )
        ],
        1,
    )
    vector_sum = jnp.sum(lax.all_to_all(all_vectors, "fsdp", 0, 0, tiled=True), axis=0)
    vector_sum = vector_sum + swap(vector_sum, TP_BIT)
    vector_grads = [
        vector_sum[i * shard_rows : (i + 1) * shard_rows] for i in range(8)
    ] + [vector_sum[8 * shard_rows :]]

    def columns(array):
        return array.reshape(shard_rows, -1)

    query_sum, key_sum, value_sum = [
        columns(qkv_sums[:, :, i * head_cols : (i + 1) * head_cols]) for i in range(3)
    ]
    return (
        from_slot(output.astype(low_type)),
        from_slot(hidden_grad),
        query_sum,
        vector_grads[0],
        key_sum,
        value_sum,
        vector_grads[1],
        jnp.transpose(columns(out_grad)),
        vector_grads[2],
        vector_grads[3],
        vector_grads[4],
        columns(up_grad),
        vector_grads[8],
        jnp.transpose(columns(down_grad)),
        vector_grads[5],
        vector_grads[6],
        vector_grads[7],
    )

BIT_TP, BIT_CORE, BIT_SIDE, BIT_LOW, BIT_HIGH = 1, 2, 4, 8, 16
TEAM_BITS = (BIT_TP, BIT_LOW, BIT_TP | BIT_LOW)
PART_BITS = (BIT_SIDE, BIT_CORE, BIT_SIDE | BIT_CORE)


class Place:
    def __init__(self):
        fsdp = lax.axis_index("fsdp")
        self.tp = lax.axis_index("tp")
        self.core = fsdp & 1
        self.side = (fsdp >> 1) & 1
        self.low = (fsdp >> 2) & 1
        self.high = fsdp >> 3
        self.quarter = 2 * self.tp + self.low


def run_kernel(body, outs, *operands, scratch=(), sems=0, apart=False, us=1.0, name=None):
    def space(operand):
        if operand.dtype == jnp.int32:
            return pltpu.SMEM
        return pltpu.HBM if apart else pltpu.VMEM

    scratches = [pltpu.VMEM(shape, kind) for shape, kind in scratch]
    if sems:
        scratches.append(pltpu.SemaphoreType.DMA((sems,)))
    return pl.pallas_call(
        body,
        out_shape=[jax.ShapeDtypeStruct(shape, kind) for shape, kind in outs],
        in_specs=[pl.BlockSpec(memory_space=space(operand)) for operand in operands],
        out_specs=[pl.BlockSpec(memory_space=pltpu.VMEM)] * len(outs),
        scratch_shapes=scratches,
        compiler_params=pltpu.CompilerParams(vmem_limit_bytes=8 << 20),
        cost_estimate=pl.CostEstimate(
            flops=int(us * 1.0e7), transcendentals=0, bytes_accessed=int(us * 1.0e4)
        ),
        name=name,
    )(*[pltpu.with_memory_space_constraint(op, pltpu.HBM) if apart else op for op in operands])


def tie(value, *others):
    return lax.optimization_barrier((value, others))[0]


def mul(left, right, left_dim=1, right_dim=0):
    return lax.dot_general(
        left, right, (((left_dim,), (right_dim,)), ((), ())), preferred_element_type=wide
    )


def bit_of(index, stride):
    return (index // stride) & 1


def place_of(index, parts, shard_pos):
    here = Place()
    shard = index & (shard_pos - 1)
    high = here.high ^ bit_of(index, shard_pos)
    tp = here.tp ^ bit_of(index, 2 * shard_pos)
    low = here.low ^ bit_of(index, 4 * shard_pos)
    side, core = here.side, here.core
    if parts:
        side = side ^ bit_of(index, 8 * shard_pos)
        core = core ^ bit_of(index, 16 * shard_pos)
    block = (high * 2 + low) * 4 + side * 2 + core
    return (block * 2 + tp) * shard_pos + shard


def live_rows_of(lengths_ref, index, parts, shard_pos):
    return place_of(index, parts, shard_pos) < lengths_ref[Place().high]


def row_of(chip, core, rows):
    return pl.ds(pl.multiple_of((2 * chip + core) * rows, 16), rows)


def join_pieces(piece_refs, full_ref, rows, cols):
    here = Place()
    for which, ref in enumerate(piece_refs):
        side, core = here.side ^ ((which >> 1) & 1), here.core ^ (which >> 2)
        for inner in range(2):
            block = (here.high ^ (which & 1)) * 2 + (here.low ^ inner)
            full_ref[row_of(block * 2 + side, core, rows), :] = ref[inner, 0:rows, cols]


def split_rows(full_ref, keep_ref, send_ref, begin, cols):
    core = Place().core
    rows = keep_ref.shape[1]
    for chip in range(keep_ref.shape[0]):
        keep_ref[chip, :, begin : begin + cols] = full_ref[row_of(chip, core, rows), 0:cols]
        send_ref[chip] = full_ref[row_of(chip, 1 - core, rows), 0:cols]


def rows_kernel(hidden_hbm, cot_hbm, hidden_ref, cot_ref, other_ref, held0, held1, sems):
    copies = [
        pltpu.make_async_copy(source, target, sems.at[i])
        for i, (source, target) in enumerate(((hidden_hbm, held0), (cot_hbm, held1)))
    ]
    for copy in copies:
        copy.start()
    near = Place().high == 0
    shard = hidden_ref.shape[0]
    for i, (held, out_ref) in enumerate(((held0, hidden_ref), (held1, cot_ref))):
        copies[i].wait()
        first, second = held[:, 0, :], held[:, 1, :]
        out_ref[...] = jnp.where(near, first, second)
        other_ref[i * shard : (i + 1) * shard, :] = jnp.where(near, second, first)


def pack_kernel(count, *refs):
    sources, refs = refs[:count], refs[count:]
    outs, held, sems = refs[:4], refs[4:-1], refs[-1]
    copies = [
        pltpu.make_async_copy(source, target, sems.at[i])
        for i, (source, target) in enumerate(zip(sources, held))
    ]
    for copy in copies:
        copy.start()
    wq_ref, wk_ref, wv_ref, wo_ref, wu_ref, wd_ref = held[:6]
    own_ref, send_ref, later_own_ref, later_send_ref = outs
    rows = wq_ref.shape[0]
    head_cols = wq_ref.shape[1] // 2
    unit_cols = wu_ref.shape[1] // 2
    low = Place().low
    for copy in copies[6:]:
        copy.wait()
    vectors = [ref[...].astype(wide).reshape(1, rows) for ref in held[6:14]]
    block = jnp.concatenate(
        [
            jnp.pad(jnp.concatenate(vectors, 0), ((0, 0), (0, 4 * rows - rows))),
            held[14][...].astype(wide).reshape(1, 4 * rows),
            jnp.zeros((7, 4 * rows), wide),
        ],
        0,
    ).astype(low_type)
    for out_ref in (own_ref, send_ref):
        out_ref[rows : rows + 16, 0 : 4 * rows] = block
        out_ref[rows : rows + 16, 4 * rows :] = jnp.zeros(
            (16, out_ref.shape[1] - 4 * rows), low_type
        )
    for copy in copies[:6]:
        copy.wait()
    for half in range(2):
        heads = slice(half * head_cols, (half + 1) * head_cols)
        units = slice(half * unit_cols, (half + 1) * unit_cols)

        def put(first_ref, later_ref):
            for i, ref in enumerate((wq_ref, wk_ref, wv_ref, wo_ref)):
                first_ref[0:rows, i * head_cols : (i + 1) * head_cols] = ref[:, heads]
            later_ref[:, 0:unit_cols] = wu_ref[:, units]
            later_ref[:, unit_cols:] = wd_ref[:, units]

        @pl.when(low == half)
        def _():
            put(own_ref, later_own_ref)

        @pl.when(low != half)
        def _():
            put(send_ref, later_send_ref)


def by_chip_row(here, refs, high, low, rows, cols):
    near = high == 0
    p0, p1, p2, p3 = [
        jnp.where(
            near,
            refs[2 * part][low, rows : rows + 16, 0:cols].astype(wide),
            refs[2 * part + 1][low, rows : rows + 16, 0:cols].astype(wide),
        )
        for part in range(4)
    ]
    left = here.side == 0
    own = jnp.where(left, p0, p1), jnp.where(left, p1, p0)
    other = jnp.where(left, p2, p3), jnp.where(left, p3, p2)
    even = here.core == 0
    result = []
    for side in range(2):
        result.append(jnp.where(even, own[side], other[side]))
        result.append(jnp.where(even, other[side], own[side]))
    return result


def project_kernel(
    keep_ref, got_ref, tp_ref, low_ref, both_ref, *refs
):
    parts, outs = refs[:8], refs[8:]
    rows_ref, query_ref, key_ref, value_ref, weight_ref, out_weight_ref = outs
    rows = parts[0].shape[1] - 16
    head_cols = query_ref.shape[1]
    join_pieces(parts, weight_ref, rows, slice(0, 3 * head_cols))
    join_pieces(parts, out_weight_ref, rows, slice(3 * head_cols, 4 * head_cols))
    shard = keep_ref.shape[0]
    rows_ref[0:shard, :] = keep_ref[...]
    rows_ref[shard : 2 * shard, :] = got_ref[0:shard, :]
    for i, ref in enumerate((tp_ref, low_ref, both_ref)):
        rows_ref[2 * shard * (i + 1) : 2 * shard * (i + 2), :] = ref[...]
    here = Place()
    biases = jnp.concatenate(by_chip_row(here, parts, here.high ^ here.tp, 0, rows, rows), 1)
    query_bias, value_bias = biases[0:1], biases[1:2]
    made = mul(rows_ref[...], weight_ref[...])
    query_ref[...] = (made[:, 0:head_cols] + query_bias).astype(low_type)
    key_ref[...] = made[:, head_cols : 2 * head_cols].astype(low_type)
    value_ref[...] = (made[:, 2 * head_cols :] + value_bias).astype(low_type)


def head_of(array, head):
    return array[:, head * HD : (head + 1) * HD]


def attend_kernel(
    shard_pos, lengths_ref, query_ref, *refs
):
    pieces, (weight_ref, low_ref, stats_ref, keep_ref, *sends) = refs[:8], refs[8:]
    head_cols = query_ref.shape[1]
    count = query_ref.shape[0]
    keys = jnp.concatenate([ref[...] for ref in pieces[:4]], 0)
    values = jnp.concatenate([ref[...] for ref in pieces[4:]], 0)
    queries = query_ref[...] * HD ** (-0.5)
    lanes = lax.broadcasted_iota(jnp.int32, (1, keys.shape[0]), 1)
    live = live_rows_of(lengths_ref, lanes, True, shard_pos)
    column = lax.broadcasted_iota(jnp.int32, (count, 128), 1)
    stats = jnp.zeros((count, 128), wide)
    parts = []
    for head in range(head_cols // HD):
        scores = mul(head_of(queries, head), head_of(keys, head), 1, 1)
        scores = jnp.where(live, scores, masked_score)
        top = jnp.max(scores, axis=1, keepdims=True)
        grown = jnp.exp(scores - top)
        total = jnp.sum(grown, axis=1, keepdims=True)
        weights = (grown * (1.0 / total)).astype(low_type)
        parts.append(mul(weights, head_of(values, head)))
        stats = jnp.where(column == head, top + jnp.log(total), stats)
    attended = jnp.concatenate(parts, 1).astype(low_type)
    low_ref[...] = attended
    stats_ref[...] = stats
    give_out(mul(attended, weight_ref[...], 1, 1), keep_ref, sends)


def full_kernel(cols, *refs):
    pieces, outs = refs[:8], refs[8:]
    for out_ref, (begin, end) in zip(outs, cols):
        join_pieces(pieces, out_ref, pieces[0].shape[1], slice(begin, end))


def lines_kernel(*refs):
    parts, (vector_ref, bias_ref) = refs[:8], refs[8:]
    here = Place()
    rows = parts[0].shape[1] - 16
    vectors = []
    for block in range(4):
        high, low = (block >> 1) ^ here.high, (block & 1) ^ here.low
        vectors += by_chip_row(here, parts, high, low, rows, rows)
    vector_ref[...] = jnp.concatenate(vectors, 1)[0:8]
    bias = by_chip_row(here, parts, here.high ^ here.tp, 0, rows, 4 * rows)
    bias_ref[...] = jnp.concatenate(bias, 1)[8:9]


def give_out(partial, keep_ref, sends):
    count = keep_ref.shape[0]
    keep_ref[...] = partial[0:count]
    for i, ref in enumerate(sends):
        ref[...] = partial[(i + 1) * count : (i + 2) * count].astype(low_type)


def collect(keep_ref, *got):
    total = keep_ref[...]
    for ref in got:
        total = total + ref[...].astype(wide)
    return total


def vector_row(vector_ref, row):
    return vector_ref[row : row + 1, :]


def first_norm_kernel(
    keep_ref, got1_ref, got2_ref, got3_ref, own_ref, vector_ref,
    out_ref, low_ref, normed_ref, scale_ref,
):
    branch = collect(keep_ref, got1_ref, got2_ref, got3_ref)
    rows = own_ref[0 : branch.shape[0], :].astype(wide)
    normed, scale = norm_parts(rows + branch + vector_row(vector_ref, 2))
    out = normed * vector_row(vector_ref, 3) + vector_row(vector_ref, 4)
    out_ref[...] = out
    low_ref[...] = out.astype(low_type)
    normed_ref[...] = normed
    scale_ref[...] = jnp.broadcast_to(scale, scale_ref.shape)


def spread_of(values):
    scaled = jnp.clip(values * (0.5**0.5), -3.832506856900711, 3.832506856900711)
    square = scaled * scaled
    top = jnp.full_like(values, 0.00022905065861350646)
    for term in (0.0034082910107109506, 0.050955695062380861, 0.18520832239976145, 1.128379143519084):
        top = top * square + term
    under = jnp.full_like(values, -1.1791602954361697e-7)
    for term in (
        0.000023547966471313185,
        0.0010179625278914885,
        0.014070470171167667,
        0.11098505178285362,
        0.49746925110067538,
        1.0,
    ):
        under = under * square + term
    return 0.5 + 0.5 * (scaled * top / under)


def hidden_kernel(
    own_ref, got1_ref, got2_ref, got3_ref, up_ref, down_ref, bias_ref,
    keep_ref, send1_ref, send2_ref, send3_ref, active_ref, slope_ref, rows_ref,
):
    rows = jnp.concatenate([r[...] for r in (own_ref, got1_ref, got2_ref, got3_ref)], 0)
    rows_ref[...] = rows
    preact = mul(rows, up_ref[...]) + bias_ref[...]
    spread = spread_of(preact)
    active = (preact * spread).astype(low_type)
    active_ref[...] = active
    slope_ref[...] = spread + preact * jnp.exp(-0.5 * preact * preact) * (2.0 * math.pi) ** (-0.5)
    give_out(mul(active, down_ref[...], 1, 1), keep_ref, (send1_ref, send2_ref, send3_ref))


def second_norm_kernel(
    lengths_ref, keep_ref, got1_ref, got2_ref, got3_ref, first_ref, own_ref, slot_ref, vector_ref,
    output_ref, grad_ref, low_ref, sums_ref,
):
    shard_pos = own_ref.shape[0]
    branch = collect(keep_ref, got1_ref, got2_ref, got3_ref)
    normed, scale = norm_parts(first_ref[...] + branch + vector_row(vector_ref, 5))
    gain = vector_row(vector_ref, 6)
    output_ref[...] = (normed * gain + vector_row(vector_ref, 7)).astype(low_type)
    index = lax.broadcasted_iota(jnp.int32, (2 * shard_pos, 1), 0)
    live = live_rows_of(lengths_ref, index, False, shard_pos)
    grad = jnp.concatenate([own_ref[...], slot_ref[shard_pos:, :]], 0).astype(wide)
    grad = jnp.where(live, grad, 0.0)
    second = norm_back(grad, normed, scale, gain)
    grad_ref[...] = second
    low = second.astype(low_type)
    low_ref[...] = low
    sums_ref[0:1, :] = jnp.sum(low.astype(wide), axis=0, keepdims=True)
    sums_ref[1:2, :] = jnp.sum(grad * normed, axis=0, keepdims=True)
    sums_ref[2:3, :] = jnp.sum(grad, axis=0, keepdims=True)


def hidden_back_kernel(
    own_ref, got1_ref, got2_ref, got3_ref, slope_ref, up_ref, down_ref,
    keep_ref, send1_ref, send2_ref, send3_ref, pre_ref, rows_ref, sums_ref,
):
    rows = jnp.concatenate([r[...] for r in (own_ref, got1_ref, got2_ref, got3_ref)], 0)
    rows_ref[...] = rows
    pre = (mul(rows, down_ref[...]) * slope_ref[...]).astype(low_type)
    pre_ref[...] = pre
    sums_ref[...] = jnp.sum(pre.astype(wide), axis=0, keepdims=True)
    give_out(mul(pre, up_ref[...], 1, 1), keep_ref, (send1_ref, send2_ref, send3_ref))


def weight_kernel(pairs, extra, *refs):
    operands = refs[: 2 * pairs + extra]
    keep_ref, *sends, full_ref = refs[2 * pairs + extra :]
    begin = 0
    for i, send_ref in enumerate(sends):
        left, right = operands[2 * i], operands[2 * i + 1]
        cols = right.shape[1]
        full_ref[:, 0:cols] = mul(left[...], right[...], 0, 0).astype(low_type)
        if extra and i == pairs - 1:
            total = operands[-2][...] + operands[-1][...]
            blank = jnp.zeros((128 - total.shape[0], total.shape[1]), wide)
            total = jnp.transpose(jnp.concatenate([total, blank], 0))
            full_ref[:, cols : cols + 128] = total.astype(low_type)
            cols += 128
        split_rows(full_ref, keep_ref, send_ref, begin, cols)
        begin += cols


def fold_kernel(count, bit, stride, *refs):
    keeps, got, outs = refs[:count], refs[count:-2], refs[-2:]
    own = getattr(Place(), bit)
    for choice, out_ref in enumerate(outs):
        for block in range(out_ref.shape[0]):
            index = block * stride[0] + (own ^ choice) * stride[1]
            begin = 0
            for i, got_ref in enumerate(got):
                end = begin + got_ref.shape[2]
                if count == 1:
                    total = keeps[0][index, :, begin:end].astype(wide)
                else:
                    total = keeps[i][index].astype(wide)
                out_ref[block, :, begin:end] = (total + got_ref[index].astype(wide)).astype(
                    out_ref.dtype
                )
                begin = end


def block_fold_kernel(keep_ref, got_ref, *outs):
    here = Place()
    for choice, out_ref in enumerate(outs):
        index = (here.high ^ (choice >> 1)) * 2 + (here.low ^ (choice & 1))
        out_ref[...] = (keep_ref[index] + got_ref[index].astype(wide)).astype(out_ref.dtype)


def final_fold_kernel(*refs):
    inputs, (own_ref, send_ref) = refs[:-2], refs[-2:]
    low = Place().low
    for choice, out_ref in ((low, own_ref), (1 - low, send_ref)):
        total = inputs[0][choice].astype(wide)
        for ref in inputs[1:]:
            total = total + ref[choice].astype(wide)
        out_ref[...] = total.astype(out_ref.dtype)


def total_kernel(spans, count, *refs):
    sources, outs = refs[:count], refs[count:]
    even = Place().low == 0
    own, got = sources[0][...], sources[1][...].astype(wide)
    if count == 4:
        own = own + sources[2][...].astype(wide)
        got = got + sources[3][...].astype(wide)
    for out_ref, (begin, end) in zip(outs, spans):
        cols = end - begin
        mine, other = own[:, begin:end], got[:, begin:end]
        out_ref[:, 0:cols] = jnp.where(even, mine, other)
        out_ref[:, cols:] = jnp.where(even, other, mine)
    vectors = outs[len(spans) :]
    if vectors:
        end = own.shape[1]
        rows = jnp.transpose(own[:, end - 128 :] + got[:, end - 128 :])
        for i, out_ref in enumerate(vectors[:-1]):
            out_ref[...] = rows[i : i + 1, :].reshape(out_ref.shape)
        first = len(vectors) - 1
        parts = [rows[first + i : first + i + 1, :] for i in range(4)]
        vectors[-1][...] = jnp.concatenate(parts, 1).reshape(vectors[-1].shape)


def first_back_kernel(
    keep_ref, got1_ref, got2_ref, got3_ref, second_ref, normed_ref, scale_ref, vector_ref,
    grad_ref, low_ref, sums_ref,
):
    grad = second_ref[...] + collect(keep_ref, got1_ref, got2_ref, got3_ref)
    normed = normed_ref[...]
    first = norm_back(grad, normed, scale_ref[:, 0:1], vector_row(vector_ref, 3))
    grad_ref[...] = first
    low = first.astype(low_type)
    low_ref[...] = low
    sums_ref[0:1, :] = jnp.sum(low.astype(wide), axis=0, keepdims=True)
    sums_ref[1:2, :] = jnp.sum(grad * normed, axis=0, keepdims=True)
    sums_ref[2:3, :] = jnp.sum(grad, axis=0, keepdims=True)


def attended_back_kernel(
    own_ref, got1_ref, got2_ref, got3_ref, weight_ref, low_ref, stats_ref, query_ref,
    packet_ref, rows_ref, sums_ref,
):
    rows = jnp.concatenate([r[...] for r in (own_ref, got1_ref, got2_ref, got3_ref)], 0)
    rows_ref[...] = rows
    made = mul(rows, weight_ref[...])
    head_cols = made.shape[1]
    sums_ref[...] = jnp.sum(made, axis=0, keepdims=True)
    grad = made.astype(low_type)
    packet_ref[:, 0:head_cols] = grad
    packet_ref[:, head_cols : 2 * head_cols] = query_ref[...]
    both = grad.astype(wide) * low_ref[...].astype(wide)
    column = lax.broadcasted_iota(jnp.int32, (made.shape[0], 128), 1)
    stats = stats_ref[...]
    levels = jnp.zeros_like(stats)
    heads = head_cols // HD
    for head in range(heads):
        delta = jnp.sum(head_of(both, head), axis=1, keepdims=True)
        for place, left in ((head, stats[:, head : head + 1]), (heads + head, delta)):
            for level in range(3):
                piece = left.astype(low_type).astype(wide)
                left = left - piece
                levels = jnp.where(column == 3 * place + level, piece, levels)
    packet_ref[:, 2 * head_cols :] = levels.astype(low_type)


def stat_of(packet, head_cols, place):
    base = 2 * head_cols + 3 * place
    total = packet[:, base : base + 1].astype(wide)
    for level in (1, 2):
        total = total + packet[:, base + level : base + level + 1].astype(wide)
    return total


def query_back_kernel(shard_pos, lengths_ref, packet_ref, *refs):
    pieces, (out_ref, sums_ref) = refs[:8], refs[8:]
    head_cols = out_ref.shape[1]
    heads = head_cols // HD
    keys = jnp.concatenate([ref[...] for ref in pieces[:4]], 0)
    values = jnp.concatenate([ref[...] for ref in pieces[4:]], 0)
    packet = packet_ref[...]
    grad = packet[:, 0:head_cols]
    queries = packet[:, head_cols : 2 * head_cols] * HD ** (-0.5)
    lanes = lax.broadcasted_iota(jnp.int32, (1, keys.shape[0]), 1)
    live = live_rows_of(lengths_ref, lanes, True, shard_pos)
    parts = []
    for head in range(heads):
        scores = mul(head_of(queries, head), head_of(keys, head), 1, 1)
        scores = jnp.where(live, scores, masked_score)
        weights = jnp.exp(scores - stat_of(packet, head_cols, head))
        weight_grad = mul(head_of(grad, head), head_of(values, head), 1, 1)
        weight_grad = weight_grad - stat_of(packet, head_cols, heads + head)
        parts.append(mul((weights * weight_grad).astype(low_type), head_of(keys, head)))
    made = (jnp.concatenate(parts, 1) * HD ** (-0.5)).astype(low_type)
    out_ref[...] = made
    sums_ref[...] = jnp.sum(made.astype(wide), axis=0, keepdims=True)


def pair_back_kernel(
    shard_pos, lengths_ref, key_ref, value_ref, query_grad_ref, weight_ref,
    g0_ref, g1_ref, g2_ref, g3_ref,
    keep_ref, send1_ref, send2_ref, send3_ref, made_ref,
):
    head_cols = query_grad_ref.shape[1]
    heads = head_cols // HD
    keys, values = key_ref[...], value_ref[...]
    packet = jnp.concatenate([ref[...] for ref in (g0_ref, g1_ref, g2_ref, g3_ref)], 0)
    grad = packet[:, 0:head_cols]
    queries = packet[:, head_cols : 2 * head_cols] * HD ** (-0.5)
    lanes = lax.broadcasted_iota(jnp.int32, (1, keys.shape[0]), 1)
    live = live_rows_of(lengths_ref, lanes, False, shard_pos)
    key_parts, value_parts = [], []
    for head in range(heads):
        scores = mul(head_of(queries, head), head_of(keys, head), 1, 1)
        scores = jnp.where(live, scores, masked_score)
        weights = jnp.exp(scores - stat_of(packet, head_cols, head))
        weight_grad = mul(head_of(grad, head), head_of(values, head), 1, 1)
        weight_grad = weight_grad - stat_of(packet, head_cols, heads + head)
        score_grad = (weights * weight_grad).astype(low_type)
        key_parts.append(mul(score_grad, head_of(queries, head), 0, 0))
        value_parts.append(mul(weights.astype(low_type), head_of(grad, head), 0, 0))
    made = jnp.concatenate(
        [query_grad_ref[...]] + [part.astype(low_type) for part in key_parts + value_parts], 1
    )
    made_ref[...] = made
    give_out(mul(made, weight_ref[...], 1, 1), keep_ref, (send1_ref, send2_ref, send3_ref))


def slots_kernel(grad_ref, out_ref, got_ref, output_ref, hidden_grad_ref):
    near = Place().high == 0
    count, width = grad_ref.shape
    for target, own, got in (
        (hidden_grad_ref, grad_ref[...], got_ref[:, 0:width].astype(wide)),
        (output_ref, out_ref[0:count, :], got_ref[:, width:]),
    ):
        target[:, 0, :] = jnp.where(near, own, got)
        target[:, 1, :] = jnp.where(near, got, own)


def last_kernel(keep_ref, got1_ref, got2_ref, got3_ref, first_ref, output_ref, own_ref, send_ref):
    total = first_ref[...] + collect(keep_ref, got1_ref, got2_ref, got3_ref)
    count, width = own_ref.shape
    own_ref[...] = total[0:count]
    send_ref[:, 0:width] = total[count:].astype(send_ref.dtype)
    send_ref[:, width:] = output_ref[count:, :]


def vectors_kernel(shards, query_ref, value_ref, first_ref, second_ref, unit_ref, out_ref):
    width = out_ref.shape[1] // shards
    per = shards // 4
    quarter = Place().quarter
    out_ref[...] = jnp.zeros_like(out_ref)
    out_ref[2:5, :] = first_ref[0:3, :]
    out_ref[5:8, :] = second_ref[0:3, :]
    for which in range(4):

        @pl.when(quarter == which)
        def _():
            span = slice(which * per * width, (which + 1) * per * width)
            out_ref[0:1, span] = query_ref[...]
            out_ref[1:2, span] = value_ref[...]
            for i in range(4):
                parts = []
                for local in range(per):
                    begin = (4 * local + i) * width
                    parts.append(unit_ref[:, begin : begin + width])
                out_ref[8 + i : 9 + i, span] = jnp.concatenate(parts, 1)


def send_team(parts):
    return tuple(swap(part, bit) for part, bit in zip(parts, TEAM_BITS))


def gather_team(rows):
    return tuple(swap(rows, bit) for bit in TEAM_BITS[::-1])[::-1]


def gather_parts(rows):
    side = swap(rows, BIT_SIDE)
    return rows, side, swap(rows, BIT_CORE), swap(side, BIT_CORE)


def local_32(
    hidden_in,
    cotangent,
    lengths,
    w_query,
    b_query,
    w_key,
    w_value,
    b_value,
    w_out,
    b_out,
    first_gain,
    first_shift,
    w_up,
    b_up,
    w_down,
    b_down,
    second_gain,
    second_shift,
):
    shard_pos, seq_count, width = hidden_in.shape
    rows_here = 2 * shard_pos
    group = 4 * rows_here
    shard_rows = w_query.shape[0]
    head_cols = w_query.shape[1] // 2
    unit_cols = w_up.shape[1] // 2
    chips = lax.axis_size("fsdp") // 2

    sources = (
        w_query, w_key, w_value, jnp.transpose(w_out), w_up, jnp.transpose(w_down),
        b_query, b_value, b_out, first_gain, first_shift, b_down, second_gain, second_shift, b_up,
    )
    first = ((shard_rows + 16, 4 * head_cols), low_type)
    later = ((shard_rows, 2 * unit_cols), low_type)
    shard = ((shard_pos, width), low_type)
    hidden_own, cot_own, other = run_kernel(
        rows_kernel,
        [shard, shard, ((rows_here, width), low_type)],
        hidden_in, cotangent,
        scratch=[(hidden_in.shape, low_type)] * 2,
        sems=2,
        apart=True,
        name="rows",
    )
    slot_rows = swap(other, BIT_HIGH)
    packs = run_kernel(
        functools.partial(pack_kernel, len(sources)),
        [first, first, later, later],
        *tie(sources, other),
        scratch=[(source.shape, source.dtype) for source in sources],
        sems=len(sources),
        apart=True,
        us=3.0,
        name="pack",
    )

    def over_blocks_of(own, send):
        return own, swap(send, BIT_LOW), swap(own, BIT_HIGH), swap(send, BIT_HIGH | BIT_LOW)

    first_own, first_send, later_own, later_send = tuple(packs)
    f0, f1, f2, f3 = over_blocks_of(first_own, first_send)
    first_near = jnp.stack([f0, f1])
    first_near_side = swap(first_near, BIT_SIDE)
    team_rows = gather_team(
        tie(jnp.concatenate([hidden_own, slot_rows[:shard_pos]], 0), packs)
    )
    first_far = tie(jnp.stack([f2, f3]), first_near_side)
    first_far_side = swap(first_far, BIT_SIDE)
    later_near = jnp.stack([later_own, swap(tie(later_send, first_near), BIT_LOW)])
    later_far = swap(tie(later_near, first_far), BIT_HIGH)
    first_pieces = (
        first_near,
        first_far,
        first_near_side,
        first_far_side,
        swap(first_near, BIT_CORE),
        swap(first_far, BIT_CORE),
        swap(first_near_side, BIT_CORE),
        swap(tie(first_far_side, team_rows, later_near), BIT_CORE),
    )

    group_rows, queries, keys, values, qkv_weight, out_weight = run_kernel(
        project_kernel,
        [
            ((group, width), low_type),
            ((group, head_cols), low_type),
            ((group, head_cols), low_type),
            ((group, head_cols), low_type),
            ((width, 3 * head_cols), low_type),
            ((width, head_cols), low_type),
        ],
        hidden_own, slot_rows, *team_rows, *first_pieces,
        name="project",
    )
    key_parts, value_parts = gather_parts(keys), gather_parts(values)
    later_near_side = swap(tie(later_near, key_parts[1]), BIT_SIDE)
    vectors, up_bias = run_kernel(
        lines_kernel,
        [((8, width), wide), ((1, unit_cols), wide)],
        *tie(first_pieces, keys),
        us=0.5,
        name="lines",
    )
    rows_shape = (rows_here, width)
    given = [(rows_shape, wide)] + [(rows_shape, low_type)] * 3
    attended_low, stats, keep, *sends = run_kernel(
        functools.partial(attend_kernel, shard_pos),
        [((group, head_cols), low_type), ((group, 128), wide)] + given,
        lengths, tie(queries, vectors), *key_parts, *value_parts, out_weight,
        us=3.0,
        name="attend",
    )
    sends = send_team(sends)
    later_far_side = swap(tie(later_far, attended_low), BIT_SIDE)
    first_out, first_low, normed, scale = run_kernel(
        first_norm_kernel,
        [(rows_shape, wide), (rows_shape, low_type), (rows_shape, wide), ((rows_here, 128), wide)],
        keep, *sends, group_rows, vectors,
        us=0.5,
        name="first_norm",
    )
    first_team = gather_team(first_low)
    later_sides = tie((later_near, later_far, later_near_side, later_far_side), first_low)
    later_pieces = later_sides + tuple(swap(part, BIT_CORE) for part in later_sides)
    up_weight, down_weight = run_kernel(
        functools.partial(full_kernel, ((0, unit_cols), (unit_cols, 2 * unit_cols))),
        [((width, unit_cols), low_type)] * 2,
        *later_pieces,
        us=1.0,
        name="full_units",
    )
    keep, s1, s2, s3, active, slope, first_rows = run_kernel(
        hidden_kernel,
        given
        + [((group, unit_cols), low_type), ((group, unit_cols), wide), ((group, width), low_type)],
        first_low, *first_team, up_weight, down_weight, up_bias,
        us=2.0,
        name="hidden",
    )
    sends = send_team((s1, s2, s3))
    output, second_grad, second_low, second_sums = run_kernel(
        second_norm_kernel,
        [(rows_shape, low_type), (rows_shape, wide), (rows_shape, low_type), ((8, width), wide)],
        lengths, keep, *sends, first_out, cot_own, slot_rows, vectors,
        name="second_norm",
    )
    second_team = gather_team(second_low)
    def weight_parts(operands, name, extra=()):
        parts = [right.shape[1] for right in operands[1::2]]
        parts[-1] += 128 if extra else 0
        shapes = [(chips, shard_rows, cols) for cols in [sum(parts)] + parts]
        kept, *sent = run_kernel(
            functools.partial(weight_kernel, len(parts), len(extra)),
            [(shape, low_type) for shape in shapes],
            *operands, *extra,
            scratch=[((width, max(parts)), low_type)],
            name=name,
        )
        return kept, sent

    def finish(sources, spans, name, vectors=()):
        outs = [(shard_rows, 2 * (end - begin)) for begin, end in spans] + list(vectors)
        return run_kernel(
            functools.partial(total_kernel, spans, len(sources)),
            [(shape, wide) for shape in outs],
            *sources,
            us=0.7,
            name=name,
        )

    def fold(bit, stride, kept, got, name):
        cols = sum(part.shape[2] for part in kept)
        shape = (kept[0].shape[0] // 2, shard_rows, cols)
        return run_kernel(
            functools.partial(fold_kernel, len(kept), bit, stride),
            [(shape, wide), (shape, low_type)],
            *kept, *got,
            us=0.7,
            name=name + "_fold_" + bit,
        )

    keep, s1, s2, s3, pre_grad, second_rows, unit_sums = run_kernel(
        hidden_back_kernel,
        given
        + [((group, unit_cols), low_type), ((group, width), low_type), ((1, unit_cols), wide)],
        second_low, *second_team, slope, up_weight, down_weight,
        us=1.5,
        name="hidden_back",
    )
    unit_kept, unit_sent = weight_parts(
        (second_rows, active, first_rows, pre_grad), "unit_weights"
    )
    unit_got = [swap(part, BIT_CORE) for part in unit_sent]
    unit_kept, unit_sent = fold("side", (2, 1), [unit_kept], unit_got, "unit")
    unit_got = swap(unit_sent, BIT_SIDE)
    sends = send_team(tie((s1, s2, s3), unit_sent))
    first_grad, one_low, first_sums = run_kernel(
        first_back_kernel,
        [(rows_shape, wide), (rows_shape, low_type), ((8, width), wide)],
        keep, *sends, second_grad, normed, scale, vectors,
        us=0.7,
        name="first_back",
    )
    one_team = gather_team(one_low)
    packet, one_rows, value_sums = run_kernel(
        attended_back_kernel,
        [
            ((group, 2 * head_cols + 128), low_type),
            ((group, width), low_type),
            ((1, head_cols), wide),
        ],
        one_low, *one_team, out_weight, attended_low, stats, queries,
        us=0.7,
        name="attended_back",
    )
    packet_side = swap(packet, BIT_SIDE)
    query_grad, query_sums = run_kernel(
        functools.partial(query_back_kernel, shard_pos),
        [((group, head_cols), low_type), ((1, head_cols), wide)],
        lengths, packet, *key_parts, *value_parts,
        us=3.0,
        name="query_back",
    )
    packets = (
        packet,
        packet_side,
        swap(packet, BIT_CORE),
        swap(tie(packet_side, query_grad), BIT_CORE),
    )
    (sums,) = run_kernel(
        functools.partial(vectors_kernel, 2 * chips),
        [((16, width), wide)],
        query_sums, value_sums, first_sums, second_sums, unit_sums,
        us=0.5,
        name="vectors",
    )
    sums_got = swap(sums, BIT_TP)
    unit_kept, unit_sent = fold("high", (1, 2), [tie(unit_kept, packet)], [unit_got], "unit")
    unit_got = swap(unit_sent, BIT_HIGH)
    keep, s1, s2, s3, qkv_grad = run_kernel(
        functools.partial(pair_back_kernel, shard_pos),
        given + [((group, 3 * head_cols), low_type)],
        lengths, tie(keys, unit_kept), values, query_grad, qkv_weight, *packets,
        us=4.0,
        name="pair_back",
    )
    late_kept, late_sent = weight_parts(
        (one_rows, attended_low, group_rows, tie(qkv_grad, unit_got)),
        "head_weights",
        (sums, sums_got),
    )
    late_got = [swap(part, BIT_CORE) for part in late_sent]
    lasts = send_team(tie((s1, s2, s3), *late_sent))
    late_kept, late_sent = fold("side", (2, 1), [late_kept], late_got, "late")
    late_got = swap(late_sent, BIT_SIDE)
    late_shape = late_kept.shape[1:]
    late_own, s1, s2, s3 = run_kernel(
        block_fold_kernel,
        [(late_shape, wide)] + [(late_shape, low_type)] * 3,
        late_kept, late_got,
        us=0.5,
        name="late_block",
    )
    late_sums = (
        late_own, swap(s1, BIT_LOW), swap(s2, BIT_HIGH), swap(s3, BIT_HIGH | BIT_LOW)
    )
    grad_own, grad_send = run_kernel(
        last_kernel,
        [((shard_pos, width), wide), ((shard_pos, 2 * width), low_type)],
        tie(keep, late_kept), *lasts, first_grad, output,
        us=0.5,
        name="last",
    )
    grad_got = swap(grad_send, BIT_HIGH)
    unit_own, unit_sent = run_kernel(
        final_fold_kernel,
        [(unit_kept.shape[1:], wide), (unit_kept.shape[1:], low_type)],
        unit_kept, unit_got,
        us=0.5,
        name="unit_low",
    )
    down_grad, up_grad = finish(
        (unit_own, swap(unit_sent, BIT_LOW)), ((0, unit_cols), (unit_cols, 2 * unit_cols)), "unit_total"
    )
    out_grad, query_total, key_total, value_total, *shares = finish(
        tie(late_sums, down_grad, up_grad),
        [(i * head_cols, (i + 1) * head_cols) for i in range(4)],
        "late_total",
        [(shard_rows,)] * 8 + [b_up.shape],
    )
    whole_output, hidden_grad = run_kernel(
        slots_kernel,
        [(hidden_in.shape, low_type), (hidden_in.shape, wide)],
        grad_own, output, grad_got,
        us=0.5,
        name="slots",
    )
    return (
        whole_output,
        hidden_grad,
        query_total,
        shares[0],
        key_total,
        value_total,
        shares[1],
        jnp.transpose(out_grad),
        shares[2],
        shares[3],
        shares[4],
        up_grad,
        shares[8],
        jnp.transpose(down_grad),
        shares[5],
        shares[6],
        shares[7],
    )


def solution(mesh):
    in_specs = (
        P(("fsdp", "tp"), None, None),
        P(("fsdp", "tp"), None, None),
        P(),
        P("fsdp", "tp"),
        P("fsdp"),
        P("fsdp", "tp"),
        P("fsdp", "tp"),
        P("fsdp"),
        P("tp", "fsdp"),
        P("fsdp"),
        P("fsdp"),
        P("fsdp"),
        P("fsdp", "tp"),
        P("fsdp"),
        P("tp", "fsdp"),
        P("fsdp"),
        P("fsdp"),
        P("fsdp"),
    )
    out_specs = (
        P(("fsdp", "tp"), None, None),
        P(("fsdp", "tp"), None, None),
        P("fsdp", "tp"),
        P("fsdp"),
        P("fsdp", "tp"),
        P("fsdp", "tp"),
        P("fsdp"),
        P("tp", "fsdp"),
        P("fsdp"),
        P("fsdp"),
        P("fsdp"),
        P("fsdp", "tp"),
        P("fsdp"),
        P("tp", "fsdp"),
        P("fsdp"),
        P("fsdp"),
        P("fsdp"),
    )
    program = local_32 if mesh.shape["fsdp"] == 16 else local
    return jax.shard_map(program, mesh=mesh, in_specs=in_specs, out_specs=out_specs, check_vma=False)
```

```python
import functools
import math

import jax
import jax.numpy as jnp
from jax import lax
from jax.experimental import pallas as pl
from jax.experimental.pallas import tpu as pltpu
from jax.sharding import PartitionSpec as P

HD = 64
layer_eps = 1e-12
masked_score = -1e30
AXES = ("fsdp", "tp")
low_type = jnp.bfloat16
wide = jnp.float32

TP_BIT, CORE_BIT, SLOT_BIT, GROUP = 1, 2, 4, 8


def device_count():
    return lax.axis_size("fsdp") * lax.axis_size("tp")


def swap(values, bit):
    return lax.ppermute(values, AXES, [(i, i ^ bit) for i in range(device_count())])


def over_blocks(values):
    total = device_count()
    groups = [list(range(first, total, GROUP)) for first in range(GROUP)]
    return lax.all_to_all(values, AXES, 0, 0, axis_index_groups=groups)


def gather_blocks(values):
    blocks = device_count() // GROUP
    return over_blocks(jnp.broadcast_to(values[None], (blocks,) + values.shape))


def in_order(first_bit, own, other, axis):
    return jnp.where(
        first_bit == 0, jnp.stack([own, other], axis), jnp.stack([other, own], axis)
    )


def gather_group(rows):
    pair = jnp.concatenate([rows, swap(rows, TP_BIT)], 0)
    return jnp.concatenate([pair, swap(pair, CORE_BIT)], 0)


def sum_group(partial):
    half = partial.shape[0] // 2
    kept = partial[:half] + swap(partial[half:].astype(low_type), CORE_BIT).astype(wide)
    quarter = half // 2
    return kept[:quarter] + swap(kept[quarter:].astype(low_type), TP_BIT).astype(wide)


def norm_parts(values):
    centre = values - jnp.mean(values, axis=-1, keepdims=True)
    spread = jnp.mean(centre * centre, axis=-1, keepdims=True)
    scale = lax.rsqrt(spread + layer_eps)
    return centre * scale, scale


def norm_back(grad, normed, scale, gain):
    scaled = grad * gain
    mean_one = jnp.mean(scaled, axis=-1, keepdims=True)
    mean_two = jnp.mean(scaled * normed, axis=-1, keepdims=True)
    return scale * (scaled - mean_one - normed * mean_two)


def local(
    hidden_in,
    cotangent,
    lengths,
    w_query,
    b_query,
    w_key,
    w_value,
    b_value,
    w_out,
    b_out,
    first_gain,
    first_shift,
    w_up,
    b_up,
    w_down,
    b_down,
    second_gain,
    second_shift,
):
    fsdp_index = lax.axis_index("fsdp")
    tp_bit = lax.axis_index("tp")
    core_bit = fsdp_index % 2
    slot_bit = (fsdp_index // 2) % 2
    block = fsdp_index // 4
    blocks = lax.axis_size("fsdp") // 4
    shard_pos, seq_count, width = hidden_in.shape
    rows_here = 2 * shard_pos
    shard_rows = w_query.shape[0]
    head_cols = w_query.shape[1] // 2
    unit_cols = w_up.shape[1] // 2
    heads = head_cols // HD
    score_scale = HD ** (-0.5)

    def halves(weight):
        return weight.reshape(shard_rows, 2, weight.shape[1] // 2)

    def for_core(parts, which):
        return jnp.concatenate(
            [lax.dynamic_index_in_dim(part, which, 1, keepdims=False) for part in parts], 1
        )

    vectors = jnp.concatenate(
        [
            vector.reshape(shard_rows, -1)
            for vector in (
                b_query,
                b_value,
                b_out,
                first_gain,
                first_shift,
                b_down,
                second_gain,
                second_shift,
                b_up,
            )
        ],
        1,
    )
    vectors = jnp.pad(vectors, ((0, 0), (0, 128 - vectors.shape[1])))
    first_parts = [halves(w_query), halves(w_key), halves(w_value)]
    later_parts = [halves(jnp.transpose(w_out)), halves(w_up), halves(jnp.transpose(w_down))]

    def to_core(parts, shared):
        own, other = for_core(parts, core_bit), for_core(parts, 1 - core_bit)
        if shared is not None:
            own = jnp.concatenate([own, shared], 1)
            other = jnp.concatenate([other, shared], 1)
        return in_order(core_bit, own, swap(other, CORE_BIT), 0)

    def full_rows(pieces):
        stacked = in_order(slot_bit, pieces, swap(pieces, SLOT_BIT), 1)
        return stacked.reshape(width, pieces.shape[-1])

    def to_slot(values):
        own = lax.dynamic_index_in_dim(values, slot_bit, 1, keepdims=False)
        other = lax.dynamic_index_in_dim(values, 1 - slot_bit, 1, keepdims=False)
        return jnp.concatenate([own, swap(other, SLOT_BIT)], 0)

    def from_slot(rows):
        returned = swap(rows[shard_pos:], SLOT_BIT)
        return in_order(slot_bit, rows[:shard_pos], returned, 1)

    rows_low = to_slot(hidden_in)
    first_pack = to_core(first_parts, vectors)
    gathered_rows = gather_blocks(rows_low)
    gathered_first = gather_blocks(first_pack.reshape(2 * shard_rows, -1))
    pair_rows = jnp.stack([gathered_rows, swap(gathered_rows, TP_BIT)], 1)
    slot_rows = jnp.stack([pair_rows, swap(pair_rows, CORE_BIT)], 1)
    slot_rows = slot_rows.reshape(-1, width)
    first_full = full_rows(gathered_first)
    later_pack = to_core(later_parts, None).reshape(2 * shard_rows, -1)
    out_piece = gather_blocks(later_pack[:, :head_cols])
    up_piece = gather_blocks(later_pack[:, head_cols : head_cols + unit_cols])
    down_piece = gather_blocks(later_pack[:, head_cols + unit_cols :])
    out_weight = full_rows(out_piece)
    up_weight = full_rows(up_piece)
    down_weight = full_rows(down_piece)
    qkv_weight = first_full[:, : 3 * head_cols]
    vector_cols = first_full[:, 3 * head_cols :].astype(wide)
    (
        query_bias_all,
        value_bias_all,
        out_bias,
        gain_one,
        shift_one,
        down_bias,
        gain_two,
        shift_two,
    ) = [vector_cols[:, i] for i in range(8)]
    up_bias_all = vector_cols[:, 8 : 8 + b_up.shape[0] // shard_rows].reshape(-1)
    quarter = 2 * tp_bit + core_bit
    query_bias = lax.dynamic_slice_in_dim(query_bias_all, quarter * head_cols, head_cols)
    value_bias = lax.dynamic_slice_in_dim(value_bias_all, quarter * head_cols, head_cols)
    up_bias = lax.dynamic_slice_in_dim(up_bias_all, quarter * unit_cols, unit_cols)

    def positions_of(block_ids):
        shape = (block_ids.shape[0], 2, 2, 2, shard_pos)
        iota = lambda dim: lax.broadcasted_iota(jnp.int32, shape, dim)
        place = block_ids.reshape(-1, 1, 1, 1, 1) * 2 + (iota(3) ^ slot_bit)
        place = (place * 2 + (iota(1) ^ core_bit)) * 2 + (iota(2) ^ tp_bit)
        return (place * shard_pos + iota(4)).reshape(-1)

    length = lax.dynamic_index_in_dim(lengths, slot_bit, 0, keepdims=False)
    slot_live = positions_of(jnp.arange(blocks)) < length
    group_live = positions_of(block.reshape(1)) < length
    row_live = group_live[:rows_here]

    group_count = 4 * rows_here
    own_rows = lax.dynamic_slice_in_dim(slot_rows, block * group_count, group_count, 0)

    def as_heads(values):
        return values.reshape(values.shape[0], heads, HD)

    queries = (
        jnp.dot(slot_rows, qkv_weight[:, :head_cols], preferred_element_type=wide) + query_bias
    ).astype(low_type)
    keys = jnp.dot(
        slot_rows, qkv_weight[:, head_cols : 2 * head_cols], preferred_element_type=wide
    ).astype(low_type)
    values = (
        jnp.dot(slot_rows, qkv_weight[:, 2 * head_cols :], preferred_element_type=wide)
        + value_bias
    ).astype(low_type)
    query_all, key_all, value_all = as_heads(queries), as_heads(keys), as_heads(values)

    def own_of(array):
        return lax.dynamic_slice_in_dim(array, block * group_count, group_count, 0)

    query_own, key_own, value_own = own_of(query_all), own_of(key_all), own_of(value_all)
    scores = (
        jnp.einsum("qhd,khd->hqk", query_own, key_all, preferred_element_type=wide) * score_scale
    )
    masked = jnp.where(slot_live[None, None, :], scores, masked_score)
    top = jnp.max(masked, axis=2, keepdims=True)
    total = jnp.sum(jnp.exp(masked - top), axis=2, keepdims=True)
    log_total = top + jnp.log(total)
    weights = jnp.exp(masked - log_total)
    attended = jnp.einsum(
        "hqk,khd->qhd", weights.astype(low_type), value_all, preferred_element_type=wide
    )
    attended_low = attended.reshape(group_count, head_cols).astype(low_type)

    branch_one = sum_group(
        jnp.einsum("th,dh->td", attended_low, out_weight, preferred_element_type=wide)
    )
    first_sum = rows_low.astype(wide) + branch_one + out_bias
    normed_one, scale_one = norm_parts(first_sum)
    first_out = normed_one * gain_one + shift_one
    group_first = gather_group(first_out.astype(low_type))
    preact = jnp.dot(group_first, up_weight, preferred_element_type=wide) + up_bias
    spread = 0.5 * (1.0 + lax.erf(preact * (0.5**0.5)))
    active_low = (preact * spread).astype(low_type)
    branch_two = sum_group(
        jnp.einsum("tf,df->td", active_low, down_weight, preferred_element_type=wide)
    )
    normed_two, scale_two = norm_parts(first_out + branch_two + down_bias)
    output = normed_two * gain_two + shift_two
    grad_out = to_slot(cotangent).astype(wide) * row_live[:, None].astype(wide)
    second_grad = norm_back(grad_out, normed_two, scale_two, gain_two)
    gain_two_grad = jnp.sum(grad_out * normed_two, axis=0)
    shift_two_grad = jnp.sum(grad_out, axis=0)
    branch_two_grad = second_grad.astype(low_type)
    down_bias_grad = jnp.sum(branch_two_grad.astype(wide), axis=0)
    group_two = gather_group(branch_two_grad)
    active_grad = jnp.einsum("td,df->tf", group_two, down_weight, preferred_element_type=wide)
    slope = spread + preact * jnp.exp(-0.5 * preact * preact) * (2.0 * jnp.pi) ** (-0.5)
    preact_grad = (active_grad * slope).astype(low_type)
    up_bias_grad = jnp.sum(preact_grad.astype(wide), axis=0)
    first_out_grad = second_grad + sum_group(
        jnp.einsum("tf,df->td", preact_grad, up_weight, preferred_element_type=wide)
    )

    def sum_weight(partial):
        cols = partial.shape[1]
        split = partial.astype(low_type).reshape(blocks, 2, 2 * shard_rows, cols)
        own = lax.dynamic_index_in_dim(split, slot_bit, 1, keepdims=False)
        other = lax.dynamic_index_in_dim(split, 1 - slot_bit, 1, keepdims=False)
        half = own.astype(wide) + swap(other, SLOT_BIT).astype(wide)
        pieces = over_blocks(half.astype(low_type))
        summed = jnp.sum(pieces.astype(wide), axis=0).reshape(2, shard_rows, cols)
        mine = lax.dynamic_index_in_dim(summed, core_bit, 0, keepdims=False)
        theirs = lax.dynamic_index_in_dim(summed, 1 - core_bit, 0, keepdims=False)
        return in_order(core_bit, mine, swap(theirs, CORE_BIT), 1)

    up_grad = sum_weight(
        jnp.einsum("td,tf->df", group_first, preact_grad, preferred_element_type=wide)
    )
    down_grad = sum_weight(
        jnp.einsum("td,tf->df", group_two, active_low, preferred_element_type=wide)
    )
    gain_one_grad = jnp.sum(first_out_grad * normed_one, axis=0)
    shift_one_grad = jnp.sum(first_out_grad, axis=0)
    first_grad = norm_back(first_out_grad, normed_one, scale_one, gain_one)
    branch_one_grad = first_grad.astype(low_type)
    out_bias_grad = jnp.sum(branch_one_grad.astype(wide), axis=0)
    group_one = gather_group(branch_one_grad)
    attended_grad = jnp.dot(group_one, out_weight, preferred_element_type=wide).astype(low_type)
    grad_all = as_heads(gather_blocks(attended_grad).reshape(-1, head_cols))
    grad_own = as_heads(attended_grad)
    delta = jnp.einsum("qhd,qhd->hq", grad_own.astype(wide), attended)
    row_stats = gather_blocks(jnp.stack([log_total[:, :, 0], delta]))
    row_stats = jnp.moveaxis(row_stats, 0, 2).reshape(2, heads, -1)
    out_grad = sum_weight(
        jnp.einsum("td,th->dh", group_one, attended_low, preferred_element_type=wide)
    )

    weight_grad = jnp.einsum("qhd,khd->hqk", grad_own, value_all, preferred_element_type=wide)
    score_grad = (weights * (weight_grad - delta[:, :, None])).astype(low_type)
    query_grad = (
        jnp.einsum("hqk,khd->qhd", score_grad, key_all, preferred_element_type=wide) * score_scale
    )
    scores_back = (
        jnp.einsum("qhd,khd->hqk", query_all, key_own, preferred_element_type=wide) * score_scale
    )
    weights_back = jnp.where(
        group_live[None, None, :], jnp.exp(scores_back - row_stats[0][:, :, None]), 0.0
    )
    value_grad = jnp.einsum(
        "hqk,qhd->khd", weights_back.astype(low_type), grad_all, preferred_element_type=wide
    )
    back_grad = jnp.einsum("qhd,khd->hqk", grad_all, value_own, preferred_element_type=wide)
    back_score = (weights_back * (back_grad - row_stats[1][:, :, None])).astype(low_type)
    key_grad = (
        jnp.einsum("hqk,qhd->khd", back_score, query_all, preferred_element_type=wide)
        * score_scale
    )
    qkv_grad = jnp.concatenate(
        [
            grad.reshape(group_count, head_cols).astype(low_type)
            for grad in (query_grad, key_grad, value_grad)
        ],
        1,
    )
    qkv_sums = sum_weight(
        jnp.einsum("td,te->de", own_rows, qkv_grad, preferred_element_type=wide)
    )
    hidden_grad = first_grad + sum_group(
        jnp.einsum("te,de->td", qkv_grad, qkv_weight, preferred_element_type=wide)
    )
    bias_sums = jnp.sum(qkv_grad.astype(wide), axis=0)

    def widen(part):
        full = jnp.zeros((4 * part.shape[0],), wide)
        return lax.dynamic_update_slice_in_dim(full, part, quarter * part.shape[0], 0)

    fsdp_count = lax.axis_size("fsdp")
    all_vectors = jnp.concatenate(
        [
            vector.reshape(fsdp_count, -1)
            for vector in (
                widen(bias_sums[:head_cols]),
                widen(bias_sums[2 * head_cols :]),
                out_bias_grad,
                gain_one_grad,
                shift_one_grad,
                down_bias_grad,
                gain_two_grad,
                shift_two_grad,
                widen(up_bias_grad),
            )
        ],
        1,
    )
    vector_sum = jnp.sum(lax.all_to_all(all_vectors, "fsdp", 0, 0, tiled=True), axis=0)
    vector_sum = vector_sum + swap(vector_sum, TP_BIT)
    vector_grads = [
        vector_sum[i * shard_rows : (i + 1) * shard_rows] for i in range(8)
    ] + [vector_sum[8 * shard_rows :]]

    def columns(array):
        return array.reshape(shard_rows, -1)

    query_sum, key_sum, value_sum = [
        columns(qkv_sums[:, :, i * head_cols : (i + 1) * head_cols]) for i in range(3)
    ]
    return (
        from_slot(output.astype(low_type)),
        from_slot(hidden_grad),
        query_sum,
        vector_grads[0],
        key_sum,
        value_sum,
        vector_grads[1],
        jnp.transpose(columns(out_grad)),
        vector_grads[2],
        vector_grads[3],
        vector_grads[4],
        columns(up_grad),
        vector_grads[8],
        jnp.transpose(columns(down_grad)),
        vector_grads[5],
        vector_grads[6],
        vector_grads[7],
    )

BIT_TP, BIT_CORE, BIT_SIDE, BIT_LOW, BIT_HIGH = 1, 2, 4, 8, 16
TEAM_BITS = (BIT_TP, BIT_LOW, BIT_TP | BIT_LOW)
PART_BITS = (BIT_SIDE, BIT_CORE, BIT_SIDE | BIT_CORE)


class Place:
    def __init__(self):
        fsdp = lax.axis_index("fsdp")
        self.tp = lax.axis_index("tp")
        self.core = fsdp & 1
        self.side = (fsdp >> 1) & 1
        self.low = (fsdp >> 2) & 1
        self.high = fsdp >> 3
        self.quarter = 2 * self.tp + self.low


def run_kernel(body, outs, *operands, scratch=(), sems=0, apart=False, us=1.0, name=None):
    def space(operand):
        if operand.dtype == jnp.int32:
            return pltpu.SMEM
        return pltpu.HBM if apart else pltpu.VMEM

    scratches = [pltpu.VMEM(shape, kind) for shape, kind in scratch]
    if sems:
        scratches.append(pltpu.SemaphoreType.DMA((sems,)))
    return pl.pallas_call(
        body,
        out_shape=[jax.ShapeDtypeStruct(shape, kind) for shape, kind in outs],
        in_specs=[pl.BlockSpec(memory_space=space(operand)) for operand in operands],
        out_specs=[pl.BlockSpec(memory_space=pltpu.VMEM)] * len(outs),
        scratch_shapes=scratches,
        compiler_params=pltpu.CompilerParams(vmem_limit_bytes=8 << 20),
        cost_estimate=pl.CostEstimate(
            flops=int(us * 1.0e7), transcendentals=0, bytes_accessed=int(us * 1.0e4)
        ),
        name=name,
    )(*[pltpu.with_memory_space_constraint(op, pltpu.HBM) if apart else op for op in operands])


def tie(value, *others):
    return lax.optimization_barrier((value, others))[0]


def mul(left, right, left_dim=1, right_dim=0):
    return lax.dot_general(
        left, right, (((left_dim,), (right_dim,)), ((), ())), preferred_element_type=wide
    )


def bit_of(index, stride):
    return (index // stride) & 1


def place_of(index, parts, shard_pos):
    here = Place()
    shard = index & (shard_pos - 1)
    high = here.high ^ bit_of(index, shard_pos)
    tp = here.tp ^ bit_of(index, 2 * shard_pos)
    low = here.low ^ bit_of(index, 4 * shard_pos)
    side, core = here.side, here.core
    if parts:
        side = side ^ bit_of(index, 8 * shard_pos)
        core = core ^ bit_of(index, 16 * shard_pos)
    block = (high * 2 + low) * 4 + side * 2 + core
    return (block * 2 + tp) * shard_pos + shard


def live_rows_of(lengths_ref, index, parts, shard_pos):
    return place_of(index, parts, shard_pos) < lengths_ref[Place().high]


def row_of(chip, core, rows):
    return pl.ds(pl.multiple_of((2 * chip + core) * rows, 16), rows)


def join_pieces(piece_refs, full_ref, rows, cols):
    here = Place()
    for which, ref in enumerate(piece_refs):
        side, core = here.side ^ ((which >> 1) & 1), here.core ^ (which >> 2)
        for inner in range(2):
            block = (here.high ^ (which & 1)) * 2 + (here.low ^ inner)
            full_ref[row_of(block * 2 + side, core, rows), :] = ref[inner, 0:rows, cols]


def split_rows(full_ref, keep_ref, send_ref, begin, cols):
    core = Place().core
    rows = keep_ref.shape[1]
    for chip in range(keep_ref.shape[0]):
        keep_ref[chip, :, begin : begin + cols] = full_ref[row_of(chip, core, rows), 0:cols]
        send_ref[chip] = full_ref[row_of(chip, 1 - core, rows), 0:cols]


def rows_kernel(hidden_hbm, cot_hbm, hidden_ref, cot_ref, other_ref, held0, held1, sems):
    copies = [
        pltpu.make_async_copy(source, target, sems.at[i])
        for i, (source, target) in enumerate(((hidden_hbm, held0), (cot_hbm, held1)))
    ]
    for copy in copies:
        copy.start()
    near = Place().high == 0
    shard = hidden_ref.shape[0]
    for i, (held, out_ref) in enumerate(((held0, hidden_ref), (held1, cot_ref))):
        copies[i].wait()
        first, second = held[:, 0, :], held[:, 1, :]
        out_ref[...] = jnp.where(near, first, second)
        other_ref[i * shard : (i + 1) * shard, :] = jnp.where(near, second, first)


def pack_kernel(count, *refs):
    sources, refs = refs[:count], refs[count:]
    outs, held, sems = refs[:4], refs[4:-1], refs[-1]
    copies = [
        pltpu.make_async_copy(source, target, sems.at[i])
        for i, (source, target) in enumerate(zip(sources, held))
    ]
    for copy in copies:
        copy.start()
    wq_ref, wk_ref, wv_ref, wo_ref, wu_ref, wd_ref = held[:6]
    own_ref, send_ref, later_own_ref, later_send_ref = outs
    rows = wq_ref.shape[0]
    head_cols = wq_ref.shape[1] // 2
    unit_cols = wu_ref.shape[1] // 2
    low = Place().low
    for copy in copies[6:]:
        copy.wait()
    vectors = [ref[...].astype(wide).reshape(1, rows) for ref in held[6:14]]
    block = jnp.concatenate(
        [
            jnp.pad(jnp.concatenate(vectors, 0), ((0, 0), (0, 4 * rows - rows))),
            held[14][...].astype(wide).reshape(1, 4 * rows),
            jnp.zeros((7, 4 * rows), wide),
        ],
        0,
    ).astype(low_type)
    for out_ref in (own_ref, send_ref):
        out_ref[rows : rows + 16, 0 : 4 * rows] = block
        out_ref[rows : rows + 16, 4 * rows :] = jnp.zeros(
            (16, out_ref.shape[1] - 4 * rows), low_type
        )
    for copy in copies[:6]:
        copy.wait()
    for half in range(2):
        heads = slice(half * head_cols, (half + 1) * head_cols)
        units = slice(half * unit_cols, (half + 1) * unit_cols)

        def put(first_ref, later_ref):
            for i, ref in enumerate((wq_ref, wk_ref, wv_ref, wo_ref)):
                first_ref[0:rows, i * head_cols : (i + 1) * head_cols] = ref[:, heads]
            later_ref[:, 0:unit_cols] = wu_ref[:, units]
            later_ref[:, unit_cols:] = wd_ref[:, units]

        @pl.when(low == half)
        def _():
            put(own_ref, later_own_ref)

        @pl.when(low != half)
        def _():
            put(send_ref, later_send_ref)


def by_chip_row(here, refs, high, low, rows, cols):
    near = high == 0
    p0, p1, p2, p3 = [
        jnp.where(
            near,
            refs[2 * part][low, rows : rows + 16, 0:cols].astype(wide),
            refs[2 * part + 1][low, rows : rows + 16, 0:cols].astype(wide),
        )
        for part in range(4)
    ]
    left = here.side == 0
    own = jnp.where(left, p0, p1), jnp.where(left, p1, p0)
    other = jnp.where(left, p2, p3), jnp.where(left, p3, p2)
    even = here.core == 0
    result = []
    for side in range(2):
        result.append(jnp.where(even, own[side], other[side]))
        result.append(jnp.where(even, other[side], own[side]))
    return result


def project_kernel(
    keep_ref, got_ref, tp_ref, low_ref, both_ref, *refs
):
    parts, outs = refs[:8], refs[8:]
    rows_ref, query_ref, pair_ref, rest_ref, weight_ref, out_weight_ref = outs
    rows = parts[0].shape[1] - 16
    head_cols = query_ref.shape[1]
    join_pieces(parts, weight_ref, rows, slice(0, 3 * head_cols))
    join_pieces(parts, out_weight_ref, rows, slice(3 * head_cols, 4 * head_cols))
    shard = keep_ref.shape[0]
    rows_ref[0:shard, :] = keep_ref[...]
    rows_ref[shard : 2 * shard, :] = got_ref[0:shard, :]
    for i, ref in enumerate((tp_ref, low_ref, both_ref)):
        rows_ref[2 * shard * (i + 1) : 2 * shard * (i + 2), :] = ref[...]
    here = Place()
    biases = jnp.concatenate(by_chip_row(here, parts, here.high ^ here.tp, 0, rows, rows), 1)
    query_bias, value_bias = biases[0:1], biases[1:2]
    made = mul(rows_ref[...], weight_ref[...])
    query_ref[...] = (made[:, 0:head_cols] + query_bias).astype(low_type)
    values = made[:, 2 * head_cols :] + value_bias
    split = pair_ref.shape[1] - head_cols
    pair_ref[:, 0:head_cols] = made[:, head_cols : 2 * head_cols].astype(low_type)
    pair_ref[:, head_cols:] = values[:, 0:split].astype(low_type)
    rest_ref[...] = values[:, split:].astype(low_type)


def joined_pair(pairs, rests, head_cols):
    pair = jnp.concatenate([ref[...] for ref in pairs], 0)
    rest = jnp.concatenate([ref[...] for ref in rests], 0)
    return pair[:, 0:head_cols], jnp.concatenate([pair[:, head_cols:], rest], 1)


def head_of(array, head):
    return array[:, head * HD : (head + 1) * HD]


def attend_kernel(
    shard_pos, lengths_ref, query_ref, *refs
):
    pieces, (weight_ref, low_ref, stats_ref, keep_ref, *sends) = refs[:8], refs[8:]
    head_cols = query_ref.shape[1]
    count = query_ref.shape[0]
    keys, values = joined_pair(pieces[:4], pieces[4:], head_cols)
    queries = query_ref[...] * HD ** (-0.5)
    lanes = lax.broadcasted_iota(jnp.int32, (1, keys.shape[0]), 1)
    live = live_rows_of(lengths_ref, lanes, True, shard_pos)
    column = lax.broadcasted_iota(jnp.int32, (count, 128), 1)
    stats = jnp.zeros((count, 128), wide)
    parts = []
    for head in range(head_cols // HD):
        scores = mul(head_of(queries, head), head_of(keys, head), 1, 1)
        scores = jnp.where(live, scores, masked_score)
        top = jnp.max(scores, axis=1, keepdims=True)
        grown = jnp.exp(scores - top)
        total = jnp.sum(grown, axis=1, keepdims=True)
        weights = (grown * (1.0 / total)).astype(low_type)
        parts.append(mul(weights, head_of(values, head)))
        stats = jnp.where(column == head, top + jnp.log(total), stats)
    attended = jnp.concatenate(parts, 1).astype(low_type)
    low_ref[...] = attended
    stats_ref[...] = stats
    give_out(mul(attended, weight_ref[...], 1, 1), keep_ref, sends)


def full_kernel(cols, *refs):
    pieces, outs = refs[:8], refs[8:]
    for out_ref, (begin, end) in zip(outs, cols):
        join_pieces(pieces, out_ref, pieces[0].shape[1], slice(begin, end))


def lines_kernel(*refs):
    parts, (vector_ref, bias_ref) = refs[:8], refs[8:]
    here = Place()
    rows = parts[0].shape[1] - 16
    vectors = []
    for block in range(4):
        high, low = (block >> 1) ^ here.high, (block & 1) ^ here.low
        vectors += by_chip_row(here, parts, high, low, rows, rows)
    vector_ref[...] = jnp.concatenate(vectors, 1)[0:8]
    bias = by_chip_row(here, parts, here.high ^ here.tp, 0, rows, 4 * rows)
    bias_ref[...] = jnp.concatenate(bias, 1)[8:9]


def give_out(partial, keep_ref, sends):
    count = keep_ref.shape[0]
    keep_ref[...] = partial[0:count]
    for i, ref in enumerate(sends):
        ref[...] = partial[(i + 1) * count : (i + 2) * count].astype(low_type)


def collect(keep_ref, *got):
    total = keep_ref[...]
    for ref in got:
        total = total + ref[...].astype(wide)
    return total


def vector_row(vector_ref, row):
    return vector_ref[row : row + 1, :]


def first_norm_kernel(
    keep_ref, got1_ref, got2_ref, got3_ref, own_ref, vector_ref,
    out_ref, low_ref, normed_ref, scale_ref,
):
    branch = collect(keep_ref, got1_ref, got2_ref, got3_ref)
    rows = own_ref[0 : branch.shape[0], :].astype(wide)
    normed, scale = norm_parts(rows + branch + vector_row(vector_ref, 2))
    out = normed * vector_row(vector_ref, 3) + vector_row(vector_ref, 4)
    out_ref[...] = out
    low_ref[...] = out.astype(low_type)
    normed_ref[...] = normed
    scale_ref[...] = jnp.broadcast_to(scale, scale_ref.shape)


def spread_of(values):
    scaled = jnp.clip(values * (0.5**0.5), -3.832506856900711, 3.832506856900711)
    square = scaled * scaled
    top = jnp.full_like(values, 0.00022905065861350646)
    for term in (0.0034082910107109506, 0.050955695062380861, 0.18520832239976145, 1.128379143519084):
        top = top * square + term
    under = jnp.full_like(values, -1.1791602954361697e-7)
    for term in (
        0.000023547966471313185,
        0.0010179625278914885,
        0.014070470171167667,
        0.11098505178285362,
        0.49746925110067538,
        1.0,
    ):
        under = under * square + term
    return 0.5 + 0.5 * (scaled * top / under)


def hidden_kernel(
    own_ref, got1_ref, got2_ref, got3_ref, up_ref, down_ref, bias_ref,
    keep_ref, send1_ref, send2_ref, send3_ref, active_ref, slope_ref, rows_ref,
):
    rows = jnp.concatenate([r[...] for r in (own_ref, got1_ref, got2_ref, got3_ref)], 0)
    rows_ref[...] = rows
    preact = mul(rows, up_ref[...]) + bias_ref[...]
    spread = spread_of(preact)
    active = (preact * spread).astype(low_type)
    active_ref[...] = active
    slope_ref[...] = spread + preact * jnp.exp(-0.5 * preact * preact) * (2.0 * math.pi) ** (-0.5)
    give_out(mul(active, down_ref[...], 1, 1), keep_ref, (send1_ref, send2_ref, send3_ref))


def second_norm_kernel(
    lengths_ref, keep_ref, got1_ref, got2_ref, got3_ref, first_ref, own_ref, slot_ref, vector_ref,
    output_ref, grad_ref, low_ref, sums_ref,
):
    shard_pos = own_ref.shape[0]
    branch = collect(keep_ref, got1_ref, got2_ref, got3_ref)
    normed, scale = norm_parts(first_ref[...] + branch + vector_row(vector_ref, 5))
    gain = vector_row(vector_ref, 6)
    output_ref[...] = (normed * gain + vector_row(vector_ref, 7)).astype(low_type)
    index = lax.broadcasted_iota(jnp.int32, (2 * shard_pos, 1), 0)
    live = live_rows_of(lengths_ref, index, False, shard_pos)
    grad = jnp.concatenate([own_ref[...], slot_ref[shard_pos:, :]], 0).astype(wide)
    grad = jnp.where(live, grad, 0.0)
    second = norm_back(grad, normed, scale, gain)
    grad_ref[...] = second
    low = second.astype(low_type)
    low_ref[...] = low
    sums_ref[0:1, :] = jnp.sum(low.astype(wide), axis=0, keepdims=True)
    sums_ref[1:2, :] = jnp.sum(grad * normed, axis=0, keepdims=True)
    sums_ref[2:3, :] = jnp.sum(grad, axis=0, keepdims=True)


def hidden_back_kernel(
    own_ref, got1_ref, got2_ref, got3_ref, slope_ref, up_ref, down_ref,
    keep_ref, send1_ref, send2_ref, send3_ref, pre_ref, rows_ref, sums_ref,
):
    rows = jnp.concatenate([r[...] for r in (own_ref, got1_ref, got2_ref, got3_ref)], 0)
    rows_ref[...] = rows
    pre = (mul(rows, down_ref[...]) * slope_ref[...]).astype(low_type)
    pre_ref[...] = pre
    sums_ref[...] = jnp.sum(pre.astype(wide), axis=0, keepdims=True)
    give_out(mul(pre, up_ref[...], 1, 1), keep_ref, (send1_ref, send2_ref, send3_ref))


def weight_kernel(pairs, extra, *refs):
    operands = refs[: 2 * pairs + extra]
    keep_ref, *sends, full_ref = refs[2 * pairs + extra :]
    begin = 0
    for i, send_ref in enumerate(sends):
        left, right = operands[2 * i], operands[2 * i + 1]
        cols = right.shape[1]
        full_ref[:, 0:cols] = mul(left[...], right[...], 0, 0).astype(low_type)
        if extra and i == pairs - 1:
            total = operands[-2][...] + operands[-1][...]
            blank = jnp.zeros((128 - total.shape[0], total.shape[1]), wide)
            total = jnp.transpose(jnp.concatenate([total, blank], 0))
            full_ref[:, cols : cols + 128] = total.astype(low_type)
            cols += 128
        split_rows(full_ref, keep_ref, send_ref, begin, cols)
        begin += cols


def fold_kernel(count, bit, stride, *refs):
    keeps, got, outs = refs[:count], refs[count:-2], refs[-2:]
    own = getattr(Place(), bit)
    for choice, out_ref in enumerate(outs):
        for block in range(out_ref.shape[0]):
            index = block * stride[0] + (own ^ choice) * stride[1]
            begin = 0
            for i, got_ref in enumerate(got):
                end = begin + got_ref.shape[2]
                if count == 1:
                    total = keeps[0][index, :, begin:end].astype(wide)
                else:
                    total = keeps[i][index].astype(wide)
                out_ref[block, :, begin:end] = (total + got_ref[index].astype(wide)).astype(
                    out_ref.dtype
                )
                begin = end


def block_fold_kernel(keep_ref, got_ref, *outs):
    here = Place()
    for choice, out_ref in enumerate(outs):
        index = (here.high ^ (choice >> 1)) * 2 + (here.low ^ (choice & 1))
        out_ref[...] = (keep_ref[index] + got_ref[index].astype(wide)).astype(out_ref.dtype)


def final_fold_kernel(*refs):
    inputs, (own_ref, send_ref) = refs[:-2], refs[-2:]
    low = Place().low
    for choice, out_ref in ((low, own_ref), (1 - low, send_ref)):
        total = inputs[0][choice].astype(wide)
        for ref in inputs[1:]:
            total = total + ref[choice].astype(wide)
        out_ref[...] = total.astype(out_ref.dtype)


def total_kernel(spans, count, *refs):
    sources, outs = refs[:count], refs[count:]
    even = Place().low == 0
    own, got = sources[0][...], sources[1][...].astype(wide)
    if count == 4:
        own = own + sources[2][...].astype(wide)
        got = got + sources[3][...].astype(wide)
    for out_ref, (begin, end) in zip(outs, spans):
        cols = end - begin
        mine, other = own[:, begin:end], got[:, begin:end]
        out_ref[:, 0:cols] = jnp.where(even, mine, other)
        out_ref[:, cols:] = jnp.where(even, other, mine)
    vectors = outs[len(spans) :]
    if vectors:
        end = own.shape[1]
        rows = jnp.transpose(own[:, end - 128 :] + got[:, end - 128 :])
        for i, out_ref in enumerate(vectors[:-1]):
            out_ref[...] = rows[i : i + 1, :].reshape(out_ref.shape)
        first = len(vectors) - 1
        parts = [rows[first + i : first + i + 1, :] for i in range(4)]
        vectors[-1][...] = jnp.concatenate(parts, 1).reshape(vectors[-1].shape)


def first_back_kernel(
    keep_ref, got1_ref, got2_ref, got3_ref, second_ref, normed_ref, scale_ref, vector_ref,
    grad_ref, low_ref, sums_ref,
):
    grad = second_ref[...] + collect(keep_ref, got1_ref, got2_ref, got3_ref)
    normed = normed_ref[...]
    first = norm_back(grad, normed, scale_ref[:, 0:1], vector_row(vector_ref, 3))
    grad_ref[...] = first
    low = first.astype(low_type)
    low_ref[...] = low
    sums_ref[0:1, :] = jnp.sum(low.astype(wide), axis=0, keepdims=True)
    sums_ref[1:2, :] = jnp.sum(grad * normed, axis=0, keepdims=True)
    sums_ref[2:3, :] = jnp.sum(grad, axis=0, keepdims=True)


def attended_back_kernel(
    own_ref, got1_ref, got2_ref, got3_ref, weight_ref, low_ref, stats_ref, query_ref,
    packet_ref, rows_ref, sums_ref,
):
    rows = jnp.concatenate([r[...] for r in (own_ref, got1_ref, got2_ref, got3_ref)], 0)
    rows_ref[...] = rows
    made = mul(rows, weight_ref[...])
    head_cols = made.shape[1]
    sums_ref[...] = jnp.sum(made, axis=0, keepdims=True)
    grad = made.astype(low_type)
    packet_ref[:, 0:head_cols] = grad
    packet_ref[:, head_cols : 2 * head_cols] = query_ref[...]
    both = grad.astype(wide) * low_ref[...].astype(wide)
    column = lax.broadcasted_iota(jnp.int32, (made.shape[0], 128), 1)
    stats = stats_ref[...]
    levels = jnp.zeros_like(stats)
    heads = head_cols // HD
    for head in range(heads):
        delta = jnp.sum(head_of(both, head), axis=1, keepdims=True)
        for place, left in ((head, stats[:, head : head + 1]), (heads + head, delta)):
            for level in range(2):
                piece = left.astype(low_type).astype(wide)
                left = left - piece
                levels = jnp.where(column == 2 * place + level, piece, levels)
    packet_ref[:, 2 * head_cols :] = levels.astype(low_type)


def stat_of(packet, head_cols, place):
    base = 2 * head_cols + 2 * place
    first, second = packet[:, base : base + 1], packet[:, base + 1 : base + 2]
    return first.astype(wide) + second.astype(wide)


def query_back_kernel(shard_pos, lengths_ref, packet_ref, *refs):
    pieces, (out_ref, sums_ref) = refs[:8], refs[8:]
    head_cols = out_ref.shape[1]
    heads = head_cols // HD
    keys, values = joined_pair(pieces[:4], pieces[4:], head_cols)
    packet = packet_ref[...]
    grad = packet[:, 0:head_cols]
    queries = packet[:, head_cols : 2 * head_cols] * HD ** (-0.5)
    lanes = lax.broadcasted_iota(jnp.int32, (1, keys.shape[0]), 1)
    live = live_rows_of(lengths_ref, lanes, True, shard_pos)
    parts = []
    for head in range(heads):
        scores = mul(head_of(queries, head), head_of(keys, head), 1, 1)
        scores = jnp.where(live, scores, masked_score)
        weights = jnp.exp(scores - stat_of(packet, head_cols, head))
        weight_grad = mul(head_of(grad, head), head_of(values, head), 1, 1)
        weight_grad = weight_grad - stat_of(packet, head_cols, heads + head)
        parts.append(mul((weights * weight_grad).astype(low_type), head_of(keys, head)))
    made = (jnp.concatenate(parts, 1) * HD ** (-0.5)).astype(low_type)
    out_ref[...] = made
    sums_ref[...] = jnp.sum(made.astype(wide), axis=0, keepdims=True)


def pair_back_kernel(
    shard_pos, lengths_ref, pair_ref, rest_ref, query_grad_ref, weight_ref,
    g0_ref, g1_ref, g2_ref, g3_ref,
    keep_ref, send1_ref, send2_ref, send3_ref, made_ref,
):
    head_cols = query_grad_ref.shape[1]
    heads = head_cols // HD
    keys, values = joined_pair((pair_ref,), (rest_ref,), head_cols)
    packet = jnp.concatenate([ref[...] for ref in (g0_ref, g1_ref, g2_ref, g3_ref)], 0)
    grad = packet[:, 0:head_cols]
    queries = packet[:, head_cols : 2 * head_cols] * HD ** (-0.5)
    index = lax.broadcasted_iota(jnp.int32, (keys.shape[0], 1), 0)
    live = live_rows_of(lengths_ref, index, False, shard_pos)
    stats = jnp.transpose(packet[:, 2 * head_cols :].astype(wide))
    key_parts, value_parts = [], []
    for head in range(heads):
        log_total = stats[2 * head : 2 * head + 1] + stats[2 * head + 1 : 2 * head + 2]
        at = 2 * (heads + head)
        delta = stats[at : at + 1] + stats[at + 1 : at + 2]
        scores = mul(head_of(keys, head), head_of(queries, head), 1, 1)
        scores = jnp.where(live, scores, masked_score)
        weights = jnp.exp(scores - log_total)
        weight_grad = mul(head_of(values, head), head_of(grad, head), 1, 1)
        score_grad = (weights * (weight_grad - delta)).astype(low_type)
        key_parts.append(mul(score_grad, head_of(queries, head)))
        value_parts.append(mul(weights.astype(low_type), head_of(grad, head)))
    made = jnp.concatenate(
        [query_grad_ref[...]] + [part.astype(low_type) for part in key_parts + value_parts], 1
    )
    made_ref[...] = made
    give_out(mul(made, weight_ref[...], 1, 1), keep_ref, (send1_ref, send2_ref, send3_ref))


def slots_kernel(grad_ref, out_ref, got_ref, output_ref, hidden_grad_ref):
    near = Place().high == 0
    count, width = grad_ref.shape
    for target, own, got in (
        (hidden_grad_ref, grad_ref[...], got_ref[:, 0:width].astype(wide)),
        (output_ref, out_ref[0:count, :], got_ref[:, width:]),
    ):
        target[:, 0, :] = jnp.where(near, own, got)
        target[:, 1, :] = jnp.where(near, got, own)


def last_kernel(keep_ref, got1_ref, got2_ref, got3_ref, first_ref, output_ref, own_ref, send_ref):
    total = first_ref[...] + collect(keep_ref, got1_ref, got2_ref, got3_ref)
    count, width = own_ref.shape
    own_ref[...] = total[0:count]
    send_ref[:, 0:width] = total[count:].astype(send_ref.dtype)
    send_ref[:, width:] = output_ref[count:, :]


def vectors_kernel(shards, query_ref, value_ref, first_ref, second_ref, unit_ref, out_ref):
    width = out_ref.shape[1] // shards
    per = shards // 4
    quarter = Place().quarter
    out_ref[...] = jnp.zeros_like(out_ref)
    out_ref[2:5, :] = first_ref[0:3, :]
    out_ref[5:8, :] = second_ref[0:3, :]
    for which in range(4):

        @pl.when(quarter == which)
        def _():
            span = slice(which * per * width, (which + 1) * per * width)
            out_ref[0:1, span] = query_ref[...]
            out_ref[1:2, span] = value_ref[...]
            for i in range(4):
                parts = []
                for local in range(per):
                    begin = (4 * local + i) * width
                    parts.append(unit_ref[:, begin : begin + width])
                out_ref[8 + i : 9 + i, span] = jnp.concatenate(parts, 1)


def send_team(parts):
    return tuple(swap(parts[i], TEAM_BITS[i]) for i in (1, 0, 2))


def gather_team(rows):
    return tuple(swap(rows, bit) for bit in TEAM_BITS[::-1])[::-1]


def gather_parts(rows):
    side = swap(rows, BIT_SIDE)
    return rows, side, swap(rows, BIT_CORE), swap(side, BIT_CORE)


def local_32(
    hidden_in,
    cotangent,
    lengths,
    w_query,
    b_query,
    w_key,
    w_value,
    b_value,
    w_out,
    b_out,
    first_gain,
    first_shift,
    w_up,
    b_up,
    w_down,
    b_down,
    second_gain,
    second_shift,
):
    shard_pos, seq_count, width = hidden_in.shape
    rows_here = 2 * shard_pos
    group = 4 * rows_here
    shard_rows = w_query.shape[0]
    head_cols = w_query.shape[1] // 2
    unit_cols = w_up.shape[1] // 2
    chips = lax.axis_size("fsdp") // 2
    pair_cols = -(-head_cols // 128) * 128

    sources = (
        w_query, w_key, w_value, jnp.transpose(w_out), w_up, jnp.transpose(w_down),
        b_query, b_value, b_out, first_gain, first_shift, b_down, second_gain, second_shift, b_up,
    )
    first = ((shard_rows + 16, 4 * head_cols), low_type)
    later = ((shard_rows, 2 * unit_cols), low_type)
    shard = ((shard_pos, width), low_type)
    hidden_own, cot_own, other = run_kernel(
        rows_kernel,
        [shard, shard, ((rows_here, width), low_type)],
        hidden_in, cotangent,
        scratch=[(hidden_in.shape, low_type)] * 2,
        sems=2,
        apart=True,
        name="rows",
    )
    slot_rows = swap(other, BIT_HIGH)
    packs = run_kernel(
        functools.partial(pack_kernel, len(sources)),
        [first, first, later, later],
        *tie(sources, other),
        scratch=[(source.shape, source.dtype) for source in sources],
        sems=len(sources),
        apart=True,
        us=3.0,
        name="pack",
    )

    def over_blocks_of(own, send):
        return own, swap(send, BIT_LOW), swap(own, BIT_HIGH), swap(send, BIT_HIGH | BIT_LOW)

    first_own, first_send, later_own, later_send = tuple(packs)
    f0, f1, f2, f3 = over_blocks_of(first_own, first_send)
    first_near = jnp.stack([f0, f1])
    first_near_side = swap(first_near, BIT_SIDE)
    team_rows = gather_team(
        tie(jnp.concatenate([hidden_own, slot_rows[:shard_pos]], 0), packs)
    )
    first_far = tie(jnp.stack([f2, f3]), first_near_side)
    first_far_side = swap(first_far, BIT_SIDE)
    later_near = jnp.stack([later_own, swap(tie(later_send, first_near), BIT_LOW)])
    later_far = swap(tie(later_near, first_far), BIT_HIGH)
    first_pieces = (
        first_near,
        first_far,
        first_near_side,
        first_far_side,
        swap(first_near, BIT_CORE),
        swap(first_far, BIT_CORE),
        swap(first_near_side, BIT_CORE),
        swap(tie(first_far_side, team_rows, later_near), BIT_CORE),
    )

    group_rows, queries, pair, rest, qkv_weight, out_weight = run_kernel(
        project_kernel,
        [
            ((group, width), low_type),
            ((group, head_cols), low_type),
            ((group, pair_cols), low_type),
            ((group, 2 * head_cols - pair_cols), low_type),
            ((width, 3 * head_cols), low_type),
            ((width, head_cols), low_type),
        ],
        hidden_own, slot_rows, *team_rows, *first_pieces,
        name="project",
    )
    pair_parts, rest_parts = gather_parts(pair), gather_parts(rest)
    later_near_side = swap(tie(later_near, pair_parts[1]), BIT_SIDE)
    vectors, up_bias = run_kernel(
        lines_kernel,
        [((8, width), wide), ((1, unit_cols), wide)],
        *tie(first_pieces, pair),
        us=0.5,
        name="lines",
    )
    rows_shape = (rows_here, width)
    given = [(rows_shape, wide)] + [(rows_shape, low_type)] * 3
    attended_low, stats, keep, *sends = run_kernel(
        functools.partial(attend_kernel, shard_pos),
        [((group, head_cols), low_type), ((group, 128), wide)] + given,
        lengths, tie(queries, vectors), *pair_parts, *rest_parts, out_weight,
        us=3.0,
        name="attend",
    )
    sends = send_team(sends)
    later_far_side = swap(tie(later_far, attended_low), BIT_SIDE)
    first_out, first_low, normed, scale = run_kernel(
        first_norm_kernel,
        [(rows_shape, wide), (rows_shape, low_type), (rows_shape, wide), ((rows_here, 128), wide)],
        keep, *sends, group_rows, vectors,
        us=0.5,
        name="first_norm",
    )
    first_team = gather_team(first_low)
    later_sides = tie((later_near, later_far, later_near_side, later_far_side), first_low)
    later_pieces = later_sides + tuple(swap(part, BIT_CORE) for part in later_sides)
    up_weight, down_weight = run_kernel(
        functools.partial(full_kernel, ((0, unit_cols), (unit_cols, 2 * unit_cols))),
        [((width, unit_cols), low_type)] * 2,
        *later_pieces,
        us=1.0,
        name="full_units",
    )
    keep, s1, s2, s3, active, slope, first_rows = run_kernel(
        hidden_kernel,
        given
        + [((group, unit_cols), low_type), ((group, unit_cols), wide), ((group, width), low_type)],
        first_low, *first_team, up_weight, down_weight, up_bias,
        us=2.0,
        name="hidden",
    )
    sends = send_team((s1, s2, s3))
    output, second_grad, second_low, second_sums = run_kernel(
        second_norm_kernel,
        [(rows_shape, low_type), (rows_shape, wide), (rows_shape, low_type), ((8, width), wide)],
        lengths, keep, *sends, first_out, cot_own, slot_rows, vectors,
        name="second_norm",
    )
    second_team = gather_team(second_low)
    def weight_parts(operands, name, extra=()):
        parts = [right.shape[1] for right in operands[1::2]]
        parts[-1] += 128 if extra else 0
        shapes = [(chips, shard_rows, cols) for cols in [sum(parts)] + parts]
        kept, *sent = run_kernel(
            functools.partial(weight_kernel, len(parts), len(extra)),
            [(shape, low_type) for shape in shapes],
            *operands, *extra,
            scratch=[((width, max(parts)), low_type)],
            name=name,
        )
        return kept, sent

    def finish(sources, spans, name, vectors=()):
        outs = [(shard_rows, 2 * (end - begin)) for begin, end in spans] + list(vectors)
        return run_kernel(
            functools.partial(total_kernel, spans, len(sources)),
            [(shape, wide) for shape in outs],
            *sources,
            us=0.7,
            name=name,
        )

    def fold(bit, stride, kept, got, name):
        cols = sum(part.shape[2] for part in kept)
        shape = (kept[0].shape[0] // 2, shard_rows, cols)
        return run_kernel(
            functools.partial(fold_kernel, len(kept), bit, stride),
            [(shape, wide), (shape, low_type)],
            *kept, *got,
            us=0.7,
            name=name + "_fold_" + bit,
        )

    keep, s1, s2, s3, pre_grad, second_rows, unit_sums = run_kernel(
        hidden_back_kernel,
        given
        + [((group, unit_cols), low_type), ((group, width), low_type), ((1, unit_cols), wide)],
        second_low, *second_team, slope, up_weight, down_weight,
        us=1.5,
        name="hidden_back",
    )
    unit_kept, unit_sent = weight_parts(
        (second_rows, active, first_rows, pre_grad), "unit_weights"
    )
    unit_got = [swap(part, BIT_CORE) for part in unit_sent]
    unit_kept, unit_sent = fold("side", (2, 1), [unit_kept], unit_got, "unit")
    unit_got = swap(unit_sent, BIT_SIDE)
    sends = send_team(tie((s1, s2, s3), unit_sent))
    first_grad, one_low, first_sums = run_kernel(
        first_back_kernel,
        [(rows_shape, wide), (rows_shape, low_type), ((8, width), wide)],
        keep, *sends, second_grad, normed, scale, vectors,
        us=0.7,
        name="first_back",
    )
    one_team = gather_team(one_low)
    packet, one_rows, value_sums = run_kernel(
        attended_back_kernel,
        [
            ((group, 2 * head_cols + 128), low_type),
            ((group, width), low_type),
            ((1, head_cols), wide),
        ],
        one_low, *one_team, out_weight, attended_low, stats, queries,
        us=0.7,
        name="attended_back",
    )
    packet_side = swap(packet, BIT_SIDE)
    query_grad, query_sums = run_kernel(
        functools.partial(query_back_kernel, shard_pos),
        [((group, head_cols), low_type), ((1, head_cols), wide)],
        lengths, packet, *pair_parts, *rest_parts,
        us=3.0,
        name="query_back",
    )
    packets = (
        packet,
        packet_side,
        swap(packet, BIT_CORE),
        swap(tie(packet_side, query_grad), BIT_CORE),
    )
    (sums,) = run_kernel(
        functools.partial(vectors_kernel, 2 * chips),
        [((16, width), wide)],
        query_sums, value_sums, first_sums, second_sums, unit_sums,
        us=0.5,
        name="vectors",
    )
    sums_got = swap(sums, BIT_TP)
    unit_kept, unit_sent = fold("high", (1, 2), [tie(unit_kept, packet)], [unit_got], "unit")
    unit_got = swap(unit_sent, BIT_HIGH)
    keep, s1, s2, s3, qkv_grad = run_kernel(
        functools.partial(pair_back_kernel, shard_pos),
        given + [((group, 3 * head_cols), low_type)],
        lengths, tie(pair, unit_kept), rest, query_grad, qkv_weight, *packets,
        us=4.0,
        name="pair_back",
    )
    late_kept, late_sent = weight_parts(
        (one_rows, attended_low, group_rows, tie(qkv_grad, unit_got)),
        "head_weights",
        (sums, sums_got),
    )
    late_got = [swap(part, BIT_CORE) for part in late_sent]
    lasts = send_team((s1, s2, s3))
    late_kept, late_sent = fold("side", (2, 1), [late_kept], late_got, "late")
    late_got = swap(late_sent, BIT_SIDE)
    late_shape = late_kept.shape[1:]
    late_own, s1, s2, s3 = run_kernel(
        block_fold_kernel,
        [(late_shape, wide)] + [(late_shape, low_type)] * 3,
        late_kept, late_got,
        us=0.5,
        name="late_block",
    )
    late_sums = (
        late_own, swap(s1, BIT_LOW), swap(s2, BIT_HIGH), swap(s3, BIT_HIGH | BIT_LOW)
    )
    grad_own, grad_send = run_kernel(
        last_kernel,
        [((shard_pos, width), wide), ((shard_pos, 2 * width), low_type)],
        tie(keep, late_kept), *lasts, first_grad, output,
        us=0.5,
        name="last",
    )
    grad_got = swap(grad_send, BIT_HIGH)
    unit_own, unit_sent = run_kernel(
        final_fold_kernel,
        [(unit_kept.shape[1:], wide), (unit_kept.shape[1:], low_type)],
        unit_kept, unit_got,
        us=0.5,
        name="unit_low",
    )
    down_grad, up_grad = finish(
        (unit_own, swap(unit_sent, BIT_LOW)), ((0, unit_cols), (unit_cols, 2 * unit_cols)), "unit_total"
    )
    out_grad, query_total, key_total, value_total, *shares = finish(
        tie(late_sums, down_grad, up_grad),
        [(i * head_cols, (i + 1) * head_cols) for i in range(4)],
        "late_total",
        [(shard_rows,)] * 8 + [b_up.shape],
    )
    whole_output, hidden_grad = run_kernel(
        slots_kernel,
        [(hidden_in.shape, low_type), (hidden_in.shape, wide)],
        grad_own, output, grad_got,
        us=0.5,
        name="slots",
    )
    return (
        whole_output,
        hidden_grad,
        query_total,
        shares[0],
        key_total,
        value_total,
        shares[1],
        jnp.transpose(out_grad),
        shares[2],
        shares[3],
        shares[4],
        up_grad,
        shares[8],
        jnp.transpose(down_grad),
        shares[5],
        shares[6],
        shares[7],
    )


def solution(mesh):
    in_specs = (
        P(("fsdp", "tp"), None, None),
        P(("fsdp", "tp"), None, None),
        P(),
        P("fsdp", "tp"),
        P("fsdp"),
        P("fsdp", "tp"),
        P("fsdp", "tp"),
        P("fsdp"),
        P("tp", "fsdp"),
        P("fsdp"),
        P("fsdp"),
        P("fsdp"),
        P("fsdp", "tp"),
        P("fsdp"),
        P("tp", "fsdp"),
        P("fsdp"),
        P("fsdp"),
        P("fsdp"),
    )
    out_specs = (
        P(("fsdp", "tp"), None, None),
        P(("fsdp", "tp"), None, None),
        P("fsdp", "tp"),
        P("fsdp"),
        P("fsdp", "tp"),
        P("fsdp", "tp"),
        P("fsdp"),
        P("tp", "fsdp"),
        P("fsdp"),
        P("fsdp"),
        P("fsdp"),
        P("fsdp", "tp"),
        P("fsdp"),
        P("tp", "fsdp"),
        P("fsdp"),
        P("fsdp"),
        P("fsdp"),
    )
    program = local_32 if mesh.shape["fsdp"] == 16 else local
    return jax.shard_map(program, mesh=mesh, in_specs=in_specs, out_specs=out_specs, check_vma=False)
```

```python
import functools
import math

import jax
import jax.numpy as jnp
from jax import lax
from jax.experimental import pallas as pl
from jax.experimental.pallas import tpu as pltpu
from jax.sharding import PartitionSpec as P

HD = 64
layer_eps = 1e-12
masked_score = -1e30
AXES = ("fsdp", "tp")
low_type = jnp.bfloat16
wide = jnp.float32

TP_BIT, CORE_BIT, SLOT_BIT, GROUP = 1, 2, 4, 8


def device_count():
    return lax.axis_size("fsdp") * lax.axis_size("tp")


def swap(values, bit):
    return lax.ppermute(values, AXES, [(i, i ^ bit) for i in range(device_count())])


def over_blocks(values):
    total = device_count()
    groups = [list(range(first, total, GROUP)) for first in range(GROUP)]
    return lax.all_to_all(values, AXES, 0, 0, axis_index_groups=groups)


def gather_blocks(values):
    blocks = device_count() // GROUP
    return over_blocks(jnp.broadcast_to(values[None], (blocks,) + values.shape))


def in_order(first_bit, own, other, axis):
    return jnp.where(
        first_bit == 0, jnp.stack([own, other], axis), jnp.stack([other, own], axis)
    )


def gather_group(rows):
    pair = jnp.concatenate([rows, swap(rows, TP_BIT)], 0)
    return jnp.concatenate([pair, swap(pair, CORE_BIT)], 0)


def sum_group(partial):
    half = partial.shape[0] // 2
    kept = partial[:half] + swap(partial[half:].astype(low_type), CORE_BIT).astype(wide)
    quarter = half // 2
    return kept[:quarter] + swap(kept[quarter:].astype(low_type), TP_BIT).astype(wide)


def norm_parts(values):
    centre = values - jnp.mean(values, axis=-1, keepdims=True)
    spread = jnp.mean(centre * centre, axis=-1, keepdims=True)
    scale = lax.rsqrt(spread + layer_eps)
    return centre * scale, scale


def norm_back(grad, normed, scale, gain):
    scaled = grad * gain
    mean_one = jnp.mean(scaled, axis=-1, keepdims=True)
    mean_two = jnp.mean(scaled * normed, axis=-1, keepdims=True)
    return scale * (scaled - mean_one - normed * mean_two)


def local(
    hidden_in,
    cotangent,
    lengths,
    w_query,
    b_query,
    w_key,
    w_value,
    b_value,
    w_out,
    b_out,
    first_gain,
    first_shift,
    w_up,
    b_up,
    w_down,
    b_down,
    second_gain,
    second_shift,
):
    fsdp_index = lax.axis_index("fsdp")
    tp_bit = lax.axis_index("tp")
    core_bit = fsdp_index % 2
    slot_bit = (fsdp_index // 2) % 2
    block = fsdp_index // 4
    blocks = lax.axis_size("fsdp") // 4
    shard_pos, seq_count, width = hidden_in.shape
    rows_here = 2 * shard_pos
    shard_rows = w_query.shape[0]
    head_cols = w_query.shape[1] // 2
    unit_cols = w_up.shape[1] // 2
    heads = head_cols // HD
    score_scale = HD ** (-0.5)

    def halves(weight):
        return weight.reshape(shard_rows, 2, weight.shape[1] // 2)

    def for_core(parts, which):
        return jnp.concatenate(
            [lax.dynamic_index_in_dim(part, which, 1, keepdims=False) for part in parts], 1
        )

    vectors = jnp.concatenate(
        [
            vector.reshape(shard_rows, -1)
            for vector in (
                b_query,
                b_value,
                b_out,
                first_gain,
                first_shift,
                b_down,
                second_gain,
                second_shift,
                b_up,
            )
        ],
        1,
    )
    vectors = jnp.pad(vectors, ((0, 0), (0, 128 - vectors.shape[1])))
    first_parts = [halves(w_query), halves(w_key), halves(w_value)]
    later_parts = [halves(jnp.transpose(w_out)), halves(w_up), halves(jnp.transpose(w_down))]

    def to_core(parts, shared):
        own, other = for_core(parts, core_bit), for_core(parts, 1 - core_bit)
        if shared is not None:
            own = jnp.concatenate([own, shared], 1)
            other = jnp.concatenate([other, shared], 1)
        return in_order(core_bit, own, swap(other, CORE_BIT), 0)

    def full_rows(pieces):
        stacked = in_order(slot_bit, pieces, swap(pieces, SLOT_BIT), 1)
        return stacked.reshape(width, pieces.shape[-1])

    def to_slot(values):
        own = lax.dynamic_index_in_dim(values, slot_bit, 1, keepdims=False)
        other = lax.dynamic_index_in_dim(values, 1 - slot_bit, 1, keepdims=False)
        return jnp.concatenate([own, swap(other, SLOT_BIT)], 0)

    def from_slot(rows):
        returned = swap(rows[shard_pos:], SLOT_BIT)
        return in_order(slot_bit, rows[:shard_pos], returned, 1)

    rows_low = to_slot(hidden_in)
    first_pack = to_core(first_parts, vectors)
    gathered_rows = gather_blocks(rows_low)
    gathered_first = gather_blocks(first_pack.reshape(2 * shard_rows, -1))
    pair_rows = jnp.stack([gathered_rows, swap(gathered_rows, TP_BIT)], 1)
    slot_rows = jnp.stack([pair_rows, swap(pair_rows, CORE_BIT)], 1)
    slot_rows = slot_rows.reshape(-1, width)
    first_full = full_rows(gathered_first)
    later_pack = to_core(later_parts, None).reshape(2 * shard_rows, -1)
    out_piece = gather_blocks(later_pack[:, :head_cols])
    up_piece = gather_blocks(later_pack[:, head_cols : head_cols + unit_cols])
    down_piece = gather_blocks(later_pack[:, head_cols + unit_cols :])
    out_weight = full_rows(out_piece)
    up_weight = full_rows(up_piece)
    down_weight = full_rows(down_piece)
    qkv_weight = first_full[:, : 3 * head_cols]
    vector_cols = first_full[:, 3 * head_cols :].astype(wide)
    (
        query_bias_all,
        value_bias_all,
        out_bias,
        gain_one,
        shift_one,
        down_bias,
        gain_two,
        shift_two,
    ) = [vector_cols[:, i] for i in range(8)]
    up_bias_all = vector_cols[:, 8 : 8 + b_up.shape[0] // shard_rows].reshape(-1)
    quarter = 2 * tp_bit + core_bit
    query_bias = lax.dynamic_slice_in_dim(query_bias_all, quarter * head_cols, head_cols)
    value_bias = lax.dynamic_slice_in_dim(value_bias_all, quarter * head_cols, head_cols)
    up_bias = lax.dynamic_slice_in_dim(up_bias_all, quarter * unit_cols, unit_cols)

    def positions_of(block_ids):
        shape = (block_ids.shape[0], 2, 2, 2, shard_pos)
        iota = lambda dim: lax.broadcasted_iota(jnp.int32, shape, dim)
        place = block_ids.reshape(-1, 1, 1, 1, 1) * 2 + (iota(3) ^ slot_bit)
        place = (place * 2 + (iota(1) ^ core_bit)) * 2 + (iota(2) ^ tp_bit)
        return (place * shard_pos + iota(4)).reshape(-1)

    length = lax.dynamic_index_in_dim(lengths, slot_bit, 0, keepdims=False)
    slot_live = positions_of(jnp.arange(blocks)) < length
    group_live = positions_of(block.reshape(1)) < length
    row_live = group_live[:rows_here]

    group_count = 4 * rows_here
    own_rows = lax.dynamic_slice_in_dim(slot_rows, block * group_count, group_count, 0)

    def as_heads(values):
        return values.reshape(values.shape[0], heads, HD)

    queries = (
        jnp.dot(slot_rows, qkv_weight[:, :head_cols], preferred_element_type=wide) + query_bias
    ).astype(low_type)
    keys = jnp.dot(
        slot_rows, qkv_weight[:, head_cols : 2 * head_cols], preferred_element_type=wide
    ).astype(low_type)
    values = (
        jnp.dot(slot_rows, qkv_weight[:, 2 * head_cols :], preferred_element_type=wide)
        + value_bias
    ).astype(low_type)
    query_all, key_all, value_all = as_heads(queries), as_heads(keys), as_heads(values)

    def own_of(array):
        return lax.dynamic_slice_in_dim(array, block * group_count, group_count, 0)

    query_own, key_own, value_own = own_of(query_all), own_of(key_all), own_of(value_all)
    scores = (
        jnp.einsum("qhd,khd->hqk", query_own, key_all, preferred_element_type=wide) * score_scale
    )
    masked = jnp.where(slot_live[None, None, :], scores, masked_score)
    top = jnp.max(masked, axis=2, keepdims=True)
    total = jnp.sum(jnp.exp(masked - top), axis=2, keepdims=True)
    log_total = top + jnp.log(total)
    weights = jnp.exp(masked - log_total)
    attended = jnp.einsum(
        "hqk,khd->qhd", weights.astype(low_type), value_all, preferred_element_type=wide
    )
    attended_low = attended.reshape(group_count, head_cols).astype(low_type)

    branch_one = sum_group(
        jnp.einsum("th,dh->td", attended_low, out_weight, preferred_element_type=wide)
    )
    first_sum = rows_low.astype(wide) + branch_one + out_bias
    normed_one, scale_one = norm_parts(first_sum)
    first_out = normed_one * gain_one + shift_one
    group_first = gather_group(first_out.astype(low_type))
    preact = jnp.dot(group_first, up_weight, preferred_element_type=wide) + up_bias
    spread = 0.5 * (1.0 + lax.erf(preact * (0.5**0.5)))
    active_low = (preact * spread).astype(low_type)
    branch_two = sum_group(
        jnp.einsum("tf,df->td", active_low, down_weight, preferred_element_type=wide)
    )
    normed_two, scale_two = norm_parts(first_out + branch_two + down_bias)
    output = normed_two * gain_two + shift_two
    grad_out = to_slot(cotangent).astype(wide) * row_live[:, None].astype(wide)
    second_grad = norm_back(grad_out, normed_two, scale_two, gain_two)
    gain_two_grad = jnp.sum(grad_out * normed_two, axis=0)
    shift_two_grad = jnp.sum(grad_out, axis=0)
    branch_two_grad = second_grad.astype(low_type)
    down_bias_grad = jnp.sum(branch_two_grad.astype(wide), axis=0)
    group_two = gather_group(branch_two_grad)
    active_grad = jnp.einsum("td,df->tf", group_two, down_weight, preferred_element_type=wide)
    slope = spread + preact * jnp.exp(-0.5 * preact * preact) * (2.0 * jnp.pi) ** (-0.5)
    preact_grad = (active_grad * slope).astype(low_type)
    up_bias_grad = jnp.sum(preact_grad.astype(wide), axis=0)
    first_out_grad = second_grad + sum_group(
        jnp.einsum("tf,df->td", preact_grad, up_weight, preferred_element_type=wide)
    )

    def sum_weight(partial):
        cols = partial.shape[1]
        split = partial.astype(low_type).reshape(blocks, 2, 2 * shard_rows, cols)
        own = lax.dynamic_index_in_dim(split, slot_bit, 1, keepdims=False)
        other = lax.dynamic_index_in_dim(split, 1 - slot_bit, 1, keepdims=False)
        half = own.astype(wide) + swap(other, SLOT_BIT).astype(wide)
        pieces = over_blocks(half.astype(low_type))
        summed = jnp.sum(pieces.astype(wide), axis=0).reshape(2, shard_rows, cols)
        mine = lax.dynamic_index_in_dim(summed, core_bit, 0, keepdims=False)
        theirs = lax.dynamic_index_in_dim(summed, 1 - core_bit, 0, keepdims=False)
        return in_order(core_bit, mine, swap(theirs, CORE_BIT), 1)

    up_grad = sum_weight(
        jnp.einsum("td,tf->df", group_first, preact_grad, preferred_element_type=wide)
    )
    down_grad = sum_weight(
        jnp.einsum("td,tf->df", group_two, active_low, preferred_element_type=wide)
    )
    gain_one_grad = jnp.sum(first_out_grad * normed_one, axis=0)
    shift_one_grad = jnp.sum(first_out_grad, axis=0)
    first_grad = norm_back(first_out_grad, normed_one, scale_one, gain_one)
    branch_one_grad = first_grad.astype(low_type)
    out_bias_grad = jnp.sum(branch_one_grad.astype(wide), axis=0)
    group_one = gather_group(branch_one_grad)
    attended_grad = jnp.dot(group_one, out_weight, preferred_element_type=wide).astype(low_type)
    grad_all = as_heads(gather_blocks(attended_grad).reshape(-1, head_cols))
    grad_own = as_heads(attended_grad)
    delta = jnp.einsum("qhd,qhd->hq", grad_own.astype(wide), attended)
    row_stats = gather_blocks(jnp.stack([log_total[:, :, 0], delta]))
    row_stats = jnp.moveaxis(row_stats, 0, 2).reshape(2, heads, -1)
    out_grad = sum_weight(
        jnp.einsum("td,th->dh", group_one, attended_low, preferred_element_type=wide)
    )

    weight_grad = jnp.einsum("qhd,khd->hqk", grad_own, value_all, preferred_element_type=wide)
    score_grad = (weights * (weight_grad - delta[:, :, None])).astype(low_type)
    query_grad = (
        jnp.einsum("hqk,khd->qhd", score_grad, key_all, preferred_element_type=wide) * score_scale
    )
    scores_back = (
        jnp.einsum("qhd,khd->hqk", query_all, key_own, preferred_element_type=wide) * score_scale
    )
    weights_back = jnp.where(
        group_live[None, None, :], jnp.exp(scores_back - row_stats[0][:, :, None]), 0.0
    )
    value_grad = jnp.einsum(
        "hqk,qhd->khd", weights_back.astype(low_type), grad_all, preferred_element_type=wide
    )
    back_grad = jnp.einsum("qhd,khd->hqk", grad_all, value_own, preferred_element_type=wide)
    back_score = (weights_back * (back_grad - row_stats[1][:, :, None])).astype(low_type)
    key_grad = (
        jnp.einsum("hqk,qhd->khd", back_score, query_all, preferred_element_type=wide)
        * score_scale
    )
    qkv_grad = jnp.concatenate(
        [
            grad.reshape(group_count, head_cols).astype(low_type)
            for grad in (query_grad, key_grad, value_grad)
        ],
        1,
    )
    qkv_sums = sum_weight(
        jnp.einsum("td,te->de", own_rows, qkv_grad, preferred_element_type=wide)
    )
    hidden_grad = first_grad + sum_group(
        jnp.einsum("te,de->td", qkv_grad, qkv_weight, preferred_element_type=wide)
    )
    bias_sums = jnp.sum(qkv_grad.astype(wide), axis=0)

    def widen(part):
        full = jnp.zeros((4 * part.shape[0],), wide)
        return lax.dynamic_update_slice_in_dim(full, part, quarter * part.shape[0], 0)

    fsdp_count = lax.axis_size("fsdp")
    all_vectors = jnp.concatenate(
        [
            vector.reshape(fsdp_count, -1)
            for vector in (
                widen(bias_sums[:head_cols]),
                widen(bias_sums[2 * head_cols :]),
                out_bias_grad,
                gain_one_grad,
                shift_one_grad,
                down_bias_grad,
                gain_two_grad,
                shift_two_grad,
                widen(up_bias_grad),
            )
        ],
        1,
    )
    vector_sum = jnp.sum(lax.all_to_all(all_vectors, "fsdp", 0, 0, tiled=True), axis=0)
    vector_sum = vector_sum + swap(vector_sum, TP_BIT)
    vector_grads = [
        vector_sum[i * shard_rows : (i + 1) * shard_rows] for i in range(8)
    ] + [vector_sum[8 * shard_rows :]]

    def columns(array):
        return array.reshape(shard_rows, -1)

    query_sum, key_sum, value_sum = [
        columns(qkv_sums[:, :, i * head_cols : (i + 1) * head_cols]) for i in range(3)
    ]
    return (
        from_slot(output.astype(low_type)),
        from_slot(hidden_grad),
        query_sum,
        vector_grads[0],
        key_sum,
        value_sum,
        vector_grads[1],
        jnp.transpose(columns(out_grad)),
        vector_grads[2],
        vector_grads[3],
        vector_grads[4],
        columns(up_grad),
        vector_grads[8],
        jnp.transpose(columns(down_grad)),
        vector_grads[5],
        vector_grads[6],
        vector_grads[7],
    )

BIT_TP, BIT_CORE, BIT_SIDE, BIT_LOW, BIT_HIGH = 1, 2, 4, 8, 16
TEAM_BITS = (BIT_TP, BIT_LOW, BIT_TP | BIT_LOW)
PART_BITS = (BIT_SIDE, BIT_CORE, BIT_SIDE | BIT_CORE)


class Place:
    def __init__(self):
        fsdp = lax.axis_index("fsdp")
        self.tp = lax.axis_index("tp")
        self.core = fsdp & 1
        self.side = (fsdp >> 1) & 1
        self.low = (fsdp >> 2) & 1
        self.high = fsdp >> 3
        self.quarter = 2 * self.tp + self.low


def run_kernel(body, outs, *operands, scratch=(), sems=0, apart=False, us=1.0, name=None):
    def space(operand):
        if operand.dtype == jnp.int32:
            return pltpu.SMEM
        return pltpu.HBM if apart else pltpu.VMEM

    scratches = [pltpu.VMEM(shape, kind) for shape, kind in scratch]
    if sems:
        scratches.append(pltpu.SemaphoreType.DMA((sems,)))
    return pl.pallas_call(
        body,
        out_shape=[jax.ShapeDtypeStruct(shape, kind) for shape, kind in outs],
        in_specs=[pl.BlockSpec(memory_space=space(operand)) for operand in operands],
        out_specs=[pl.BlockSpec(memory_space=pltpu.VMEM)] * len(outs),
        scratch_shapes=scratches,
        compiler_params=pltpu.CompilerParams(vmem_limit_bytes=8 << 20),
        cost_estimate=pl.CostEstimate(
            flops=int(us * 1.0e7), transcendentals=0, bytes_accessed=int(us * 1.0e4)
        ),
        name=name,
    )(*[pltpu.with_memory_space_constraint(op, pltpu.HBM) if apart else op for op in operands])


def tie(value, *others):
    return lax.optimization_barrier((value, others))[0]


def mul(left, right, left_dim=1, right_dim=0):
    return lax.dot_general(
        left, right, (((left_dim,), (right_dim,)), ((), ())), preferred_element_type=wide
    )


def bit_of(index, stride):
    return (index // stride) & 1


def place_of(index, parts, shard_pos):
    here = Place()
    shard = index & (shard_pos - 1)
    high = here.high ^ bit_of(index, shard_pos)
    tp = here.tp ^ bit_of(index, 2 * shard_pos)
    low = here.low ^ bit_of(index, 4 * shard_pos)
    side, core = here.side, here.core
    if parts:
        side = side ^ bit_of(index, 8 * shard_pos)
        core = core ^ bit_of(index, 16 * shard_pos)
    block = (high * 2 + low) * 4 + side * 2 + core
    return (block * 2 + tp) * shard_pos + shard


def live_rows_of(lengths_ref, index, parts, shard_pos):
    return place_of(index, parts, shard_pos) < lengths_ref[Place().high]


def row_of(chip, core, rows):
    return pl.ds(pl.multiple_of((2 * chip + core) * rows, 16), rows)


def join_pieces(piece_refs, full_ref, rows, begin, cols=slice(None)):
    here = Place()
    for which, ref in enumerate(piece_refs):
        side, core = here.side ^ ((which >> 1) & 1), here.core ^ (which >> 2)
        for inner in range(2):
            block = (here.high ^ (which & 1)) * 2 + (here.low ^ inner)
            piece = ref[inner, begin : begin + rows, cols]
            full_ref[row_of(block * 2 + side, core, rows), :] = piece


def split_rows(full_ref, keep_ref, send_ref, begin, cols):
    core = Place().core
    rows = keep_ref.shape[1]
    for chip in range(keep_ref.shape[0]):
        keep_ref[chip, :, begin : begin + cols] = full_ref[row_of(chip, core, rows), 0:cols]
        send_ref[chip] = full_ref[row_of(chip, 1 - core, rows), 0:cols]


def rows_kernel(hidden_hbm, cot_hbm, hidden_ref, cot_ref, other_ref, held0, held1, sems):
    copies = [
        pltpu.make_async_copy(source, target, sems.at[i])
        for i, (source, target) in enumerate(((hidden_hbm, held0), (cot_hbm, held1)))
    ]
    for copy in copies:
        copy.start()
    near = Place().high == 0
    shard = hidden_ref.shape[0]
    for i, (held, out_ref) in enumerate(((held0, hidden_ref), (held1, cot_ref))):
        copies[i].wait()
        first, second = held[:, 0, :], held[:, 1, :]
        out_ref[...] = jnp.where(near, first, second)
        other_ref[i * shard : (i + 1) * shard, :] = jnp.where(near, second, first)


def pack_kernel(count, *refs):
    sources, refs = refs[:count], refs[count:]
    outs, held, sems = refs[:4], refs[4:-1], refs[-1]
    copies = [
        pltpu.make_async_copy(source, target, sems.at[i])
        for i, (source, target) in enumerate(zip(sources, held))
    ]
    for copy in copies:
        copy.start()
    wq_ref, wk_ref, wv_ref, wo_ref, wu_ref, wd_ref = held[:6]
    own_ref, send_ref, later_own_ref, near_ref = outs
    size = send_ref.shape[0]
    rows = wq_ref.shape[0]
    head_cols = wq_ref.shape[1] // 2
    unit_cols = wu_ref.shape[1] // 2
    low = Place().low
    for copy in copies[6:]:
        copy.wait()
    vectors = [ref[...].astype(wide).reshape(1, rows) for ref in held[6:14]]
    block = jnp.concatenate(
        [
            jnp.pad(jnp.concatenate(vectors, 0), ((0, 0), (0, 4 * rows - rows))),
            held[14][...].astype(wide).reshape(1, 4 * rows),
            jnp.zeros((7, 4 * rows), wide),
        ],
        0,
    ).astype(low_type)
    for out_ref in (own_ref, send_ref, near_ref):
        out_ref[rows : rows + 16, 0 : 4 * rows] = block
        out_ref[rows : rows + 16, 4 * rows :] = jnp.zeros(
            (16, out_ref.shape[1] - 4 * rows), low_type
        )
    for copy in copies[:6]:
        copy.wait()
    for half in range(2):
        heads = slice(half * head_cols, (half + 1) * head_cols)
        units = slice(half * unit_cols, (half + 1) * unit_cols)

        def put_first(first_ref):
            for i, ref in enumerate((wq_ref, wk_ref, wv_ref, wo_ref)):
                first_ref[0:rows, i * head_cols : (i + 1) * head_cols] = ref[:, heads]

        def put_later(later_ref, begin):
            later_ref[begin : begin + rows, :] = wu_ref[:, units]
            later_ref[begin + rows : begin + 2 * rows, :] = wd_ref[:, units]

        @pl.when(low == half)
        def _():
            put_first(own_ref)
            put_later(later_own_ref, 0)

        @pl.when(low != half)
        def _():
            put_first(send_ref)
            put_first(near_ref)
            put_later(near_ref, size)


def by_chip_row(here, refs, high, low, rows, cols):
    near = high == 0
    p0, p1, p2, p3 = [
        jnp.where(
            near,
            refs[2 * part][low, rows : rows + 16, 0:cols].astype(wide),
            refs[2 * part + 1][low, rows : rows + 16, 0:cols].astype(wide),
        )
        for part in range(4)
    ]
    left = here.side == 0
    own = jnp.where(left, p0, p1), jnp.where(left, p1, p0)
    other = jnp.where(left, p2, p3), jnp.where(left, p3, p2)
    even = here.core == 0
    result = []
    for side in range(2):
        result.append(jnp.where(even, own[side], other[side]))
        result.append(jnp.where(even, other[side], own[side]))
    return result


def project_kernel(
    keep_ref, got_ref, tp_ref, low_ref, both_ref, *refs
):
    parts, outs = refs[:8], refs[8:]
    rows_ref, query_ref, pair_ref, rest_ref, weight_ref, out_weight_ref = outs
    rows = parts[0].shape[1] - 16
    head_cols = query_ref.shape[1]
    join_pieces(parts, weight_ref, rows, 0, slice(0, 3 * head_cols))
    join_pieces(parts, out_weight_ref, rows, 0, slice(3 * head_cols, 4 * head_cols))
    shard = keep_ref.shape[0]
    rows_ref[0:shard, :] = keep_ref[...]
    rows_ref[shard : 2 * shard, :] = got_ref[0:shard, :]
    for i, ref in enumerate((tp_ref, low_ref, both_ref)):
        rows_ref[2 * shard * (i + 1) : 2 * shard * (i + 2), :] = ref[...]
    here = Place()
    biases = jnp.concatenate(by_chip_row(here, parts, here.high ^ here.tp, 0, rows, rows), 1)
    query_bias, value_bias = biases[0:1], biases[1:2]
    made = mul(rows_ref[...], weight_ref[...])
    query_ref[...] = (made[:, 0:head_cols] + query_bias).astype(low_type)
    values = made[:, 2 * head_cols :] + value_bias
    split = pair_ref.shape[1] - head_cols
    pair_ref[:, 0:head_cols] = made[:, head_cols : 2 * head_cols].astype(low_type)
    pair_ref[:, head_cols:] = values[:, 0:split].astype(low_type)
    rest_ref[...] = values[:, split:].astype(low_type)


def joined_pair(pairs, rests, head_cols):
    pair = jnp.concatenate([ref[...] for ref in pairs], 0)
    rest = jnp.concatenate([ref[...] for ref in rests], 0)
    return pair[:, 0:head_cols], jnp.concatenate([pair[:, head_cols:], rest], 1)


def head_of(array, head):
    return array[:, head * HD : (head + 1) * HD]


def attend_kernel(
    shard_pos, lengths_ref, query_ref, *refs
):
    pieces, (weight_ref, low_ref, stats_ref, keep_ref, *sends) = refs[:8], refs[8:]
    head_cols = query_ref.shape[1]
    count = query_ref.shape[0]
    keys, values = joined_pair(pieces[:4], pieces[4:], head_cols)
    queries = query_ref[...] * HD ** (-0.5)
    lanes = lax.broadcasted_iota(jnp.int32, (1, keys.shape[0]), 1)
    live = live_rows_of(lengths_ref, lanes, True, shard_pos)
    column = lax.broadcasted_iota(jnp.int32, (count, 128), 1)
    stats = jnp.zeros((count, 128), wide)
    parts = []
    for head in range(head_cols // HD):
        scores = mul(head_of(queries, head), head_of(keys, head), 1, 1)
        scores = jnp.where(live, scores, masked_score)
        top = jnp.max(scores, axis=1, keepdims=True)
        grown = jnp.exp(scores - top)
        total = jnp.sum(grown, axis=1, keepdims=True)
        weights = (grown * (1.0 / total)).astype(low_type)
        parts.append(mul(weights, head_of(values, head)))
        stats = jnp.where(column == head, top + jnp.log(total), stats)
    attended = jnp.concatenate(parts, 1).astype(low_type)
    low_ref[...] = attended
    stats_ref[...] = stats
    give_out(mul(attended, weight_ref[...], 1, 1), keep_ref, sends)


def full_kernel(*refs):
    pieces, outs = refs[:8], refs[8:]
    rows = pieces[0].shape[1] // 2
    for i, out_ref in enumerate(outs):
        join_pieces(pieces, out_ref, rows, i * rows)


def lines_kernel(*refs):
    parts, (vector_ref, bias_ref) = refs[:8], refs[8:]
    here = Place()
    rows = parts[0].shape[1] - 16
    vectors = []
    for block in range(4):
        high, low = (block >> 1) ^ here.high, (block & 1) ^ here.low
        vectors += by_chip_row(here, parts, high, low, rows, rows)
    vector_ref[...] = jnp.concatenate(vectors, 1)[0:8]
    bias = by_chip_row(here, parts, here.high ^ here.tp, 0, rows, 4 * rows)
    bias_ref[...] = jnp.concatenate(bias, 1)[8:9]


def give_out(partial, keep_ref, sends):
    count = keep_ref.shape[0]
    keep_ref[...] = partial[0:count]
    for i, ref in enumerate(sends):
        ref[...] = partial[(i + 1) * count : (i + 2) * count].astype(low_type)


def collect(keep_ref, *got):
    total = keep_ref[...]
    for ref in got:
        total = total + ref[...].astype(wide)
    return total


def vector_row(vector_ref, row):
    return vector_ref[row : row + 1, :]


def first_norm_kernel(
    keep_ref, got1_ref, got2_ref, got3_ref, own_ref, vector_ref,
    out_ref, low_ref, normed_ref, scale_ref,
):
    branch = collect(keep_ref, got1_ref, got2_ref, got3_ref)
    rows = own_ref[0 : branch.shape[0], :].astype(wide)
    normed, scale = norm_parts(rows + branch + vector_row(vector_ref, 2))
    out = normed * vector_row(vector_ref, 3) + vector_row(vector_ref, 4)
    out_ref[...] = out
    low_ref[...] = out.astype(low_type)
    normed_ref[...] = normed
    scale_ref[...] = jnp.broadcast_to(scale, scale_ref.shape)


def spread_of(values):
    scaled = jnp.clip(values * (0.5**0.5), -3.832506856900711, 3.832506856900711)
    square = scaled * scaled
    top = jnp.full_like(values, 0.00022905065861350646)
    for term in (0.0034082910107109506, 0.050955695062380861, 0.18520832239976145, 1.128379143519084):
        top = top * square + term
    under = jnp.full_like(values, -1.1791602954361697e-7)
    for term in (
        0.000023547966471313185,
        0.0010179625278914885,
        0.014070470171167667,
        0.11098505178285362,
        0.49746925110067538,
        1.0,
    ):
        under = under * square + term
    return 0.5 + 0.5 * (scaled * top / under)


def hidden_kernel(
    own_ref, got1_ref, got2_ref, got3_ref, up_ref, down_ref, bias_ref,
    keep_ref, send1_ref, send2_ref, send3_ref, active_ref, slope_ref, rows_ref,
):
    rows = jnp.concatenate([r[...] for r in (own_ref, got1_ref, got2_ref, got3_ref)], 0)
    rows_ref[...] = rows
    preact = mul(rows, up_ref[...]) + bias_ref[...]
    spread = spread_of(preact)
    active = (preact * spread).astype(low_type)
    active_ref[...] = active
    slope_ref[...] = spread + preact * jnp.exp(-0.5 * preact * preact) * (2.0 * math.pi) ** (-0.5)
    give_out(mul(active, down_ref[...], 1, 1), keep_ref, (send1_ref, send2_ref, send3_ref))


def second_norm_kernel(
    lengths_ref, keep_ref, got1_ref, got2_ref, got3_ref, first_ref, own_ref, slot_ref, vector_ref,
    output_ref, grad_ref, low_ref, sums_ref,
):
    shard_pos = own_ref.shape[0]
    branch = collect(keep_ref, got1_ref, got2_ref, got3_ref)
    normed, scale = norm_parts(first_ref[...] + branch + vector_row(vector_ref, 5))
    gain = vector_row(vector_ref, 6)
    output_ref[...] = (normed * gain + vector_row(vector_ref, 7)).astype(low_type)
    index = lax.broadcasted_iota(jnp.int32, (2 * shard_pos, 1), 0)
    live = live_rows_of(lengths_ref, index, False, shard_pos)
    grad = jnp.concatenate([own_ref[...], slot_ref[shard_pos:, :]], 0).astype(wide)
    grad = jnp.where(live, grad, 0.0)
    second = norm_back(grad, normed, scale, gain)
    grad_ref[...] = second
    low = second.astype(low_type)
    low_ref[...] = low
    sums_ref[0:1, :] = jnp.sum(low.astype(wide), axis=0, keepdims=True)
    sums_ref[1:2, :] = jnp.sum(grad * normed, axis=0, keepdims=True)
    sums_ref[2:3, :] = jnp.sum(grad, axis=0, keepdims=True)


def hidden_back_kernel(
    own_ref, got1_ref, got2_ref, got3_ref, slope_ref, up_ref, down_ref,
    keep_ref, send1_ref, send2_ref, send3_ref, pre_ref, rows_ref, sums_ref,
):
    rows = jnp.concatenate([r[...] for r in (own_ref, got1_ref, got2_ref, got3_ref)], 0)
    rows_ref[...] = rows
    pre = (mul(rows, down_ref[...]) * slope_ref[...]).astype(low_type)
    pre_ref[...] = pre
    sums_ref[...] = jnp.sum(pre.astype(wide), axis=0, keepdims=True)
    give_out(mul(pre, up_ref[...], 1, 1), keep_ref, (send1_ref, send2_ref, send3_ref))


def weight_kernel(pairs, extra, *refs):
    operands = refs[: 2 * pairs + extra]
    keep_ref, *sends, full_ref = refs[2 * pairs + extra :]
    begin = 0
    for i, send_ref in enumerate(sends):
        left, right = operands[2 * i], operands[2 * i + 1]
        cols = right.shape[1]
        full_ref[:, 0:cols] = mul(left[...], right[...], 0, 0).astype(low_type)
        if extra and i == pairs - 1:
            total = operands[-2][...] + operands[-1][...]
            blank = jnp.zeros((128 - total.shape[0], total.shape[1]), wide)
            total = jnp.transpose(jnp.concatenate([total, blank], 0))
            full_ref[:, cols : cols + 128] = total.astype(low_type)
            cols += 128
        split_rows(full_ref, keep_ref, send_ref, begin, cols)
        begin += cols


def fold_kernel(count, bit, stride, *refs):
    keeps, got, outs = refs[:count], refs[count:-2], refs[-2:]
    own = getattr(Place(), bit)
    for choice, out_ref in enumerate(outs):
        for block in range(out_ref.shape[0]):
            index = block * stride[0] + (own ^ choice) * stride[1]
            begin = 0
            for i, got_ref in enumerate(got):
                end = begin + got_ref.shape[2]
                if count == 1:
                    total = keeps[0][index, :, begin:end].astype(wide)
                else:
                    total = keeps[i][index].astype(wide)
                out_ref[block, :, begin:end] = (total + got_ref[index].astype(wide)).astype(
                    out_ref.dtype
                )
                begin = end


def block_fold_kernel(keep_ref, got_ref, *outs):
    here = Place()
    for choice, out_ref in enumerate(outs):
        index = (here.high ^ (choice >> 1)) * 2 + (here.low ^ (choice & 1))
        out_ref[...] = (keep_ref[index] + got_ref[index].astype(wide)).astype(out_ref.dtype)


def final_fold_kernel(*refs):
    inputs, (own_ref, send_ref) = refs[:-2], refs[-2:]
    low = Place().low
    for choice, out_ref in ((low, own_ref), (1 - low, send_ref)):
        total = inputs[0][choice].astype(wide)
        for ref in inputs[1:]:
            total = total + ref[choice].astype(wide)
        out_ref[...] = total.astype(out_ref.dtype)


def total_kernel(spans, count, *refs):
    sources, outs = refs[:count], refs[count:]
    even = Place().low == 0
    own, got = sources[0][...], sources[1][...].astype(wide)
    if count == 4:
        own = own + sources[2][...].astype(wide)
        got = got + sources[3][...].astype(wide)
    for out_ref, (begin, end) in zip(outs, spans):
        cols = end - begin
        mine, other = own[:, begin:end], got[:, begin:end]
        out_ref[:, 0:cols] = jnp.where(even, mine, other)
        out_ref[:, cols:] = jnp.where(even, other, mine)
    vectors = outs[len(spans) :]
    if vectors:
        end = own.shape[1]
        rows = jnp.transpose(own[:, end - 128 :] + got[:, end - 128 :])
        for i, out_ref in enumerate(vectors[:-1]):
            out_ref[...] = rows[i : i + 1, :].reshape(out_ref.shape)
        first = len(vectors) - 1
        parts = [rows[first + i : first + i + 1, :] for i in range(4)]
        vectors[-1][...] = jnp.concatenate(parts, 1).reshape(vectors[-1].shape)


def first_back_kernel(
    keep_ref, got1_ref, got2_ref, got3_ref, second_ref, normed_ref, scale_ref, vector_ref,
    grad_ref, low_ref, sums_ref,
):
    grad = second_ref[...] + collect(keep_ref, got1_ref, got2_ref, got3_ref)
    normed = normed_ref[...]
    first = norm_back(grad, normed, scale_ref[:, 0:1], vector_row(vector_ref, 3))
    grad_ref[...] = first
    low = first.astype(low_type)
    low_ref[...] = low
    sums_ref[0:1, :] = jnp.sum(low.astype(wide), axis=0, keepdims=True)
    sums_ref[1:2, :] = jnp.sum(grad * normed, axis=0, keepdims=True)
    sums_ref[2:3, :] = jnp.sum(grad, axis=0, keepdims=True)


def attended_back_kernel(
    own_ref, got1_ref, got2_ref, got3_ref, weight_ref, low_ref, stats_ref, query_ref,
    packet_ref, rows_ref, sums_ref,
):
    rows = jnp.concatenate([r[...] for r in (own_ref, got1_ref, got2_ref, got3_ref)], 0)
    rows_ref[...] = rows
    made = mul(rows, weight_ref[...])
    head_cols = made.shape[1]
    sums_ref[...] = jnp.sum(made, axis=0, keepdims=True)
    grad = made.astype(low_type)
    packet_ref[:, 0:head_cols] = grad
    packet_ref[:, head_cols : 2 * head_cols] = query_ref[...]
    both = grad.astype(wide) * low_ref[...].astype(wide)
    column = lax.broadcasted_iota(jnp.int32, (made.shape[0], 128), 1)
    stats = stats_ref[...]
    levels = jnp.zeros_like(stats)
    heads = head_cols // HD
    for head in range(heads):
        delta = jnp.sum(head_of(both, head), axis=1, keepdims=True)
        for place, left in ((head, stats[:, head : head + 1]), (heads + head, delta)):
            for level in range(2):
                piece = left.astype(low_type).astype(wide)
                left = left - piece
                levels = jnp.where(column == 2 * place + level, piece, levels)
    packet_ref[:, 2 * head_cols :] = levels.astype(low_type)


def stat_of(packet, head_cols, place):
    base = 2 * head_cols + 2 * place
    first, second = packet[:, base : base + 1], packet[:, base + 1 : base + 2]
    return first.astype(wide) + second.astype(wide)


def query_back_kernel(shard_pos, lengths_ref, packet_ref, *refs):
    pieces, (out_ref, sums_ref) = refs[:8], refs[8:]
    head_cols = out_ref.shape[1]
    heads = head_cols // HD
    keys, values = joined_pair(pieces[:4], pieces[4:], head_cols)
    packet = packet_ref[...]
    grad = packet[:, 0:head_cols]
    queries = packet[:, head_cols : 2 * head_cols] * HD ** (-0.5)
    lanes = lax.broadcasted_iota(jnp.int32, (1, keys.shape[0]), 1)
    live = live_rows_of(lengths_ref, lanes, True, shard_pos)
    parts = []
    for head in range(heads):
        scores = mul(head_of(queries, head), head_of(keys, head), 1, 1)
        scores = jnp.where(live, scores, masked_score)
        weights = jnp.exp(scores - stat_of(packet, head_cols, head))
        weight_grad = mul(head_of(grad, head), head_of(values, head), 1, 1)
        weight_grad = weight_grad - stat_of(packet, head_cols, heads + head)
        parts.append(mul((weights * weight_grad).astype(low_type), head_of(keys, head)))
    made = (jnp.concatenate(parts, 1) * HD ** (-0.5)).astype(low_type)
    out_ref[...] = made
    sums_ref[...] = jnp.sum(made.astype(wide), axis=0, keepdims=True)


def pair_back_kernel(
    shard_pos, lengths_ref, pair_ref, rest_ref, query_grad_ref, weight_ref,
    g0_ref, g1_ref, g2_ref, g3_ref,
    keep_ref, send1_ref, send2_ref, send3_ref, made_ref,
):
    head_cols = query_grad_ref.shape[1]
    heads = head_cols // HD
    keys, values = joined_pair((pair_ref,), (rest_ref,), head_cols)
    packet = jnp.concatenate([ref[...] for ref in (g0_ref, g1_ref, g2_ref, g3_ref)], 0)
    grad = packet[:, 0:head_cols]
    queries = packet[:, head_cols : 2 * head_cols] * HD ** (-0.5)
    index = lax.broadcasted_iota(jnp.int32, (keys.shape[0], 1), 0)
    live = live_rows_of(lengths_ref, index, False, shard_pos)
    stats = jnp.transpose(packet[:, 2 * head_cols :].astype(wide))
    key_parts, value_parts = [], []
    for head in range(heads):
        log_total = stats[2 * head : 2 * head + 1] + stats[2 * head + 1 : 2 * head + 2]
        at = 2 * (heads + head)
        delta = stats[at : at + 1] + stats[at + 1 : at + 2]
        scores = mul(head_of(keys, head), head_of(queries, head), 1, 1)
        scores = jnp.where(live, scores, masked_score)
        weights = jnp.exp(scores - log_total)
        weight_grad = mul(head_of(values, head), head_of(grad, head), 1, 1)
        score_grad = (weights * (weight_grad - delta)).astype(low_type)
        key_parts.append(mul(score_grad, head_of(queries, head)))
        value_parts.append(mul(weights.astype(low_type), head_of(grad, head)))
    made = jnp.concatenate(
        [query_grad_ref[...]] + [part.astype(low_type) for part in key_parts + value_parts], 1
    )
    made_ref[...] = made
    give_out(mul(made, weight_ref[...], 1, 1), keep_ref, (send1_ref, send2_ref, send3_ref))


def slots_kernel(grad_ref, out_ref, got_ref, output_ref, hidden_grad_ref):
    near = Place().high == 0
    count, width = grad_ref.shape
    for target, own, got in (
        (hidden_grad_ref, grad_ref[...], got_ref[:, 0:width].astype(wide)),
        (output_ref, out_ref[0:count, :], got_ref[:, width:]),
    ):
        target[:, 0, :] = jnp.where(near, own, got)
        target[:, 1, :] = jnp.where(near, got, own)


def last_kernel(keep_ref, got1_ref, got2_ref, got3_ref, first_ref, output_ref, own_ref, send_ref):
    total = first_ref[...] + collect(keep_ref, got1_ref, got2_ref, got3_ref)
    count, width = own_ref.shape
    own_ref[...] = total[0:count]
    send_ref[:, 0:width] = total[count:].astype(send_ref.dtype)
    send_ref[:, width:] = output_ref[count:, :]


def vectors_kernel(shards, query_ref, value_ref, first_ref, second_ref, unit_ref, out_ref):
    width = out_ref.shape[1] // shards
    per = shards // 4
    quarter = Place().quarter
    out_ref[...] = jnp.zeros_like(out_ref)
    out_ref[2:5, :] = first_ref[0:3, :]
    out_ref[5:8, :] = second_ref[0:3, :]
    for which in range(4):

        @pl.when(quarter == which)
        def _():
            span = slice(which * per * width, (which + 1) * per * width)
            out_ref[0:1, span] = query_ref[...]
            out_ref[1:2, span] = value_ref[...]
            for i in range(4):
                parts = []
                for local in range(per):
                    begin = (4 * local + i) * width
                    parts.append(unit_ref[:, begin : begin + width])
                out_ref[8 + i : 9 + i, span] = jnp.concatenate(parts, 1)


def send_team(parts):
    return tuple(swap(parts[i], TEAM_BITS[i]) for i in (1, 0, 2))


def gather_team(rows):
    return tuple(swap(rows, bit) for bit in TEAM_BITS[::-1])[::-1]


def gather_parts(rows):
    side = swap(rows, BIT_SIDE)
    return rows, side, swap(rows, BIT_CORE), swap(side, BIT_CORE)


def local_32(
    hidden_in,
    cotangent,
    lengths,
    w_query,
    b_query,
    w_key,
    w_value,
    b_value,
    w_out,
    b_out,
    first_gain,
    first_shift,
    w_up,
    b_up,
    w_down,
    b_down,
    second_gain,
    second_shift,
):
    shard_pos, seq_count, width = hidden_in.shape
    rows_here = 2 * shard_pos
    group = 4 * rows_here
    shard_rows = w_query.shape[0]
    head_cols = w_query.shape[1] // 2
    unit_cols = w_up.shape[1] // 2
    chips = lax.axis_size("fsdp") // 2
    pair_cols = -(-head_cols // 128) * 128

    sources = (
        w_query, w_key, w_value, jnp.transpose(w_out), w_up, jnp.transpose(w_down),
        b_query, b_value, b_out, first_gain, first_shift, b_down, second_gain, second_shift, b_up,
    )
    first = ((shard_rows + 16, 4 * head_cols), low_type)
    later = ((2 * shard_rows, unit_cols), low_type)
    near = ((3 * shard_rows + 16, unit_cols), low_type)
    shard = ((shard_pos, width), low_type)
    hidden_own, cot_own, other = run_kernel(
        rows_kernel,
        [shard, shard, ((rows_here, width), low_type)],
        hidden_in, cotangent,
        scratch=[(hidden_in.shape, low_type)] * 2,
        sems=2,
        apart=True,
        name="rows",
    )
    slot_rows = swap(other, BIT_HIGH)
    packs = run_kernel(
        functools.partial(pack_kernel, len(sources)),
        [first, first, later, near],
        *tie(sources, other),
        scratch=[(source.shape, source.dtype) for source in sources],
        sems=len(sources),
        apart=True,
        us=3.0,
        name="pack",
    )

    first_own, first_send, later_own, near_send = tuple(packs)
    near_got = swap(near_send, BIT_LOW)
    size = first_own.shape[0]
    f2, f3 = swap(first_own, BIT_HIGH), swap(first_send, BIT_HIGH | BIT_LOW)
    first_near = jnp.stack([first_own, near_got[:size]])
    first_near_side = swap(first_near, BIT_SIDE)
    team_rows = gather_team(
        tie(jnp.concatenate([hidden_own, slot_rows[:shard_pos]], 0), packs)
    )
    first_far = tie(jnp.stack([f2, f3]), first_near_side)
    first_far_side = swap(first_far, BIT_SIDE)
    later_near = jnp.stack([later_own, near_got[size:]])
    later_far = swap(tie(later_near, first_far), BIT_HIGH)
    first_pieces = (
        first_near,
        first_far,
        first_near_side,
        first_far_side,
        swap(first_near, BIT_CORE),
        swap(first_far, BIT_CORE),
        swap(first_near_side, BIT_CORE),
        swap(tie(first_far_side, team_rows, later_near), BIT_CORE),
    )

    group_rows, queries, pair, rest, qkv_weight, out_weight = run_kernel(
        project_kernel,
        [
            ((group, width), low_type),
            ((group, head_cols), low_type),
            ((group, pair_cols), low_type),
            ((group, 2 * head_cols - pair_cols), low_type),
            ((width, 3 * head_cols), low_type),
            ((width, head_cols), low_type),
        ],
        hidden_own, slot_rows, *team_rows, *first_pieces,
        name="project",
    )
    pair_parts, rest_parts = gather_parts(pair), gather_parts(rest)
    later_near_side = swap(tie(later_near, pair_parts[1]), BIT_SIDE)
    vectors, up_bias = run_kernel(
        lines_kernel,
        [((8, width), wide), ((1, unit_cols), wide)],
        *tie(first_pieces, pair),
        us=0.5,
        name="lines",
    )
    rows_shape = (rows_here, width)
    given = [(rows_shape, wide)] + [(rows_shape, low_type)] * 3
    attended_low, stats, keep, *sends = run_kernel(
        functools.partial(attend_kernel, shard_pos),
        [((group, head_cols), low_type), ((group, 128), wide)] + given,
        lengths, tie(queries, vectors), *pair_parts, *rest_parts, out_weight,
        us=3.0,
        name="attend",
    )
    sends = send_team(sends)
    later_far_side = swap(tie(later_far, attended_low), BIT_SIDE)
    first_out, first_low, normed, scale = run_kernel(
        first_norm_kernel,
        [(rows_shape, wide), (rows_shape, low_type), (rows_shape, wide), ((rows_here, 128), wide)],
        keep, *sends, group_rows, vectors,
        us=0.5,
        name="first_norm",
    )
    first_team = gather_team(first_low)
    later_sides = tie((later_near, later_far, later_near_side, later_far_side), first_low)
    later_pieces = later_sides + tuple(swap(part, BIT_CORE) for part in later_sides)
    up_weight, down_weight = run_kernel(
        full_kernel,
        [((width, unit_cols), low_type)] * 2,
        *later_pieces,
        us=1.0,
        name="full_units",
    )
    keep, s1, s2, s3, active, slope, first_rows = run_kernel(
        hidden_kernel,
        given
        + [((group, unit_cols), low_type), ((group, unit_cols), wide), ((group, width), low_type)],
        first_low, *first_team, up_weight, down_weight, up_bias,
        us=2.0,
        name="hidden",
    )
    sends = send_team((s1, s2, s3))
    output, second_grad, second_low, second_sums = run_kernel(
        second_norm_kernel,
        [(rows_shape, low_type), (rows_shape, wide), (rows_shape, low_type), ((8, width), wide)],
        lengths, keep, *sends, first_out, cot_own, slot_rows, vectors,
        name="second_norm",
    )
    second_team = gather_team(second_low)
    def weight_parts(operands, name, extra=()):
        parts = [right.shape[1] for right in operands[1::2]]
        parts[-1] += 128 if extra else 0
        shapes = [(chips, shard_rows, cols) for cols in [sum(parts)] + parts]
        kept, *sent = run_kernel(
            functools.partial(weight_kernel, len(parts), len(extra)),
            [(shape, low_type) for shape in shapes],
            *operands, *extra,
            scratch=[((width, max(parts)), low_type)],
            name=name,
        )
        return kept, sent

    def finish(sources, spans, name, vectors=()):
        outs = [(shard_rows, 2 * (end - begin)) for begin, end in spans] + list(vectors)
        return run_kernel(
            functools.partial(total_kernel, spans, len(sources)),
            [(shape, wide) for shape in outs],
            *sources,
            us=0.7,
            name=name,
        )

    def fold(bit, stride, kept, got, name):
        cols = sum(part.shape[2] for part in kept)
        shape = (kept[0].shape[0] // 2, shard_rows, cols)
        return run_kernel(
            functools.partial(fold_kernel, len(kept), bit, stride),
            [(shape, wide), (shape, low_type)],
            *kept, *got,
            us=0.7,
            name=name + "_fold_" + bit,
        )

    keep, s1, s2, s3, pre_grad, second_rows, unit_sums = run_kernel(
        hidden_back_kernel,
        given
        + [((group, unit_cols), low_type), ((group, width), low_type), ((1, unit_cols), wide)],
        second_low, *second_team, slope, up_weight, down_weight,
        us=1.5,
        name="hidden_back",
    )
    unit_kept, unit_sent = weight_parts(
        (second_rows, active, first_rows, pre_grad), "unit_weights"
    )
    unit_got = [swap(part, BIT_CORE) for part in unit_sent]
    unit_kept, unit_sent = fold("side", (2, 1), [unit_kept], unit_got, "unit")
    unit_got = swap(unit_sent, BIT_SIDE)
    sends = send_team(tie((s1, s2, s3), unit_sent))
    first_grad, one_low, first_sums = run_kernel(
        first_back_kernel,
        [(rows_shape, wide), (rows_shape, low_type), ((8, width), wide)],
        keep, *sends, second_grad, normed, scale, vectors,
        us=0.7,
        name="first_back",
    )
    one_team = gather_team(one_low)
    packet, one_rows, value_sums = run_kernel(
        attended_back_kernel,
        [
            ((group, 2 * head_cols + 128), low_type),
            ((group, width), low_type),
            ((1, head_cols), wide),
        ],
        one_low, *one_team, out_weight, attended_low, stats, queries,
        us=0.7,
        name="attended_back",
    )
    packet_side = swap(packet, BIT_SIDE)
    query_grad, query_sums = run_kernel(
        functools.partial(query_back_kernel, shard_pos),
        [((group, head_cols), low_type), ((1, head_cols), wide)],
        lengths, packet, *pair_parts, *rest_parts,
        us=3.0,
        name="query_back",
    )
    packets = (
        packet,
        packet_side,
        swap(packet, BIT_CORE),
        swap(tie(packet_side, query_grad), BIT_CORE),
    )
    (sums,) = run_kernel(
        functools.partial(vectors_kernel, 2 * chips),
        [((16, width), wide)],
        query_sums, value_sums, first_sums, second_sums, unit_sums,
        us=0.5,
        name="vectors",
    )
    sums_got = swap(sums, BIT_TP)
    unit_kept, unit_sent = fold("high", (1, 2), [tie(unit_kept, packet)], [unit_got], "unit")
    unit_got = swap(unit_sent, BIT_HIGH)
    keep, s1, s2, s3, qkv_grad = run_kernel(
        functools.partial(pair_back_kernel, shard_pos),
        given + [((group, 3 * head_cols), low_type)],
        lengths, tie(pair, unit_kept), rest, query_grad, qkv_weight, *packets,
        us=4.0,
        name="pair_back",
    )
    late_kept, late_sent = weight_parts(
        (one_rows, attended_low, group_rows, tie(qkv_grad, unit_got)),
        "head_weights",
        (sums, sums_got),
    )
    late_got = [swap(part, BIT_CORE) for part in late_sent]
    lasts = send_team((s1, s2, s3))
    late_kept, late_sent = fold("side", (2, 1), [late_kept], late_got, "late")
    late_got = swap(late_sent, BIT_SIDE)
    late_shape = late_kept.shape[1:]
    late_own, s1, s2, s3 = run_kernel(
        block_fold_kernel,
        [(late_shape, wide)] + [(late_shape, low_type)] * 3,
        late_kept, late_got,
        us=0.5,
        name="late_block",
    )
    late_sums = (
        late_own, swap(s1, BIT_LOW), swap(s2, BIT_HIGH), swap(s3, BIT_HIGH | BIT_LOW)
    )
    grad_own, grad_send = run_kernel(
        last_kernel,
        [((shard_pos, width), wide), ((shard_pos, 2 * width), low_type)],
        tie(keep, late_kept), *lasts, first_grad, output,
        us=0.5,
        name="last",
    )
    grad_got = swap(grad_send, BIT_HIGH)
    unit_own, unit_sent = run_kernel(
        final_fold_kernel,
        [(unit_kept.shape[1:], wide), (unit_kept.shape[1:], low_type)],
        unit_kept, unit_got,
        us=0.5,
        name="unit_low",
    )
    down_grad, up_grad = finish(
        (unit_own, swap(unit_sent, BIT_LOW)), ((0, unit_cols), (unit_cols, 2 * unit_cols)), "unit_total"
    )
    out_grad, query_total, key_total, value_total, *shares = finish(
        tie(late_sums, down_grad, up_grad),
        [(i * head_cols, (i + 1) * head_cols) for i in range(4)],
        "late_total",
        [(shard_rows,)] * 8 + [b_up.shape],
    )
    whole_output, hidden_grad = run_kernel(
        slots_kernel,
        [(hidden_in.shape, low_type), (hidden_in.shape, wide)],
        grad_own, output, grad_got,
        us=0.5,
        name="slots",
    )
    return (
        whole_output,
        hidden_grad,
        query_total,
        shares[0],
        key_total,
        value_total,
        shares[1],
        jnp.transpose(out_grad),
        shares[2],
        shares[3],
        shares[4],
        up_grad,
        shares[8],
        jnp.transpose(down_grad),
        shares[5],
        shares[6],
        shares[7],
    )


def solution(mesh):
    in_specs = (
        P(("fsdp", "tp"), None, None),
        P(("fsdp", "tp"), None, None),
        P(),
        P("fsdp", "tp"),
        P("fsdp"),
        P("fsdp", "tp"),
        P("fsdp", "tp"),
        P("fsdp"),
        P("tp", "fsdp"),
        P("fsdp"),
        P("fsdp"),
        P("fsdp"),
        P("fsdp", "tp"),
        P("fsdp"),
        P("tp", "fsdp"),
        P("fsdp"),
        P("fsdp"),
        P("fsdp"),
    )
    out_specs = (
        P(("fsdp", "tp"), None, None),
        P(("fsdp", "tp"), None, None),
        P("fsdp", "tp"),
        P("fsdp"),
        P("fsdp", "tp"),
        P("fsdp", "tp"),
        P("fsdp"),
        P("tp", "fsdp"),
        P("fsdp"),
        P("fsdp"),
        P("fsdp"),
        P("fsdp", "tp"),
        P("fsdp"),
        P("tp", "fsdp"),
        P("fsdp"),
        P("fsdp"),
        P("fsdp"),
    )
    program = local_32 if mesh.shape["fsdp"] == 16 else local
    return jax.shard_map(program, mesh=mesh, in_specs=in_specs, out_specs=out_specs, check_vma=False)
```

```python
import functools
import math

import jax
import jax.numpy as jnp
from jax import lax
from jax.experimental import pallas as pl
from jax.experimental.pallas import tpu as pltpu
from jax.sharding import PartitionSpec as P

HD = 64
layer_eps = 1e-12
masked_score = -1e30
AXES = ("fsdp", "tp")
low_type = jnp.bfloat16
wide = jnp.float32

TP_BIT, CORE_BIT, SLOT_BIT, GROUP = 1, 2, 4, 8


def device_count():
    return lax.axis_size("fsdp") * lax.axis_size("tp")


def swap(values, bit):
    return lax.ppermute(values, AXES, [(i, i ^ bit) for i in range(device_count())])


def over_blocks(values):
    total = device_count()
    groups = [list(range(first, total, GROUP)) for first in range(GROUP)]
    return lax.all_to_all(values, AXES, 0, 0, axis_index_groups=groups)


def gather_blocks(values):
    blocks = device_count() // GROUP
    return over_blocks(jnp.broadcast_to(values[None], (blocks,) + values.shape))


def in_order(first_bit, own, other, axis):
    return jnp.where(
        first_bit == 0, jnp.stack([own, other], axis), jnp.stack([other, own], axis)
    )


def gather_group(rows):
    pair = jnp.concatenate([rows, swap(rows, TP_BIT)], 0)
    return jnp.concatenate([pair, swap(pair, CORE_BIT)], 0)


def sum_group(partial):
    half = partial.shape[0] // 2
    kept = partial[:half] + swap(partial[half:].astype(low_type), CORE_BIT).astype(wide)
    quarter = half // 2
    return kept[:quarter] + swap(kept[quarter:].astype(low_type), TP_BIT).astype(wide)


def norm_parts(values):
    centre = values - jnp.mean(values, axis=-1, keepdims=True)
    spread = jnp.mean(centre * centre, axis=-1, keepdims=True)
    scale = lax.rsqrt(spread + layer_eps)
    return centre * scale, scale


def norm_back(grad, normed, scale, gain):
    scaled = grad * gain
    mean_one = jnp.mean(scaled, axis=-1, keepdims=True)
    mean_two = jnp.mean(scaled * normed, axis=-1, keepdims=True)
    return scale * (scaled - mean_one - normed * mean_two)


def local(
    hidden_in,
    cotangent,
    lengths,
    w_query,
    b_query,
    w_key,
    w_value,
    b_value,
    w_out,
    b_out,
    first_gain,
    first_shift,
    w_up,
    b_up,
    w_down,
    b_down,
    second_gain,
    second_shift,
):
    fsdp_index = lax.axis_index("fsdp")
    tp_bit = lax.axis_index("tp")
    core_bit = fsdp_index % 2
    slot_bit = (fsdp_index // 2) % 2
    block = fsdp_index // 4
    blocks = lax.axis_size("fsdp") // 4
    shard_pos, seq_count, width = hidden_in.shape
    rows_here = 2 * shard_pos
    shard_rows = w_query.shape[0]
    head_cols = w_query.shape[1] // 2
    unit_cols = w_up.shape[1] // 2
    heads = head_cols // HD
    score_scale = HD ** (-0.5)

    def halves(weight):
        return weight.reshape(shard_rows, 2, weight.shape[1] // 2)

    def for_core(parts, which):
        return jnp.concatenate(
            [lax.dynamic_index_in_dim(part, which, 1, keepdims=False) for part in parts], 1
        )

    vectors = jnp.concatenate(
        [
            vector.reshape(shard_rows, -1)
            for vector in (
                b_query,
                b_value,
                b_out,
                first_gain,
                first_shift,
                b_down,
                second_gain,
                second_shift,
                b_up,
            )
        ],
        1,
    )
    vectors = jnp.pad(vectors, ((0, 0), (0, 128 - vectors.shape[1])))
    first_parts = [halves(w_query), halves(w_key), halves(w_value)]
    later_parts = [halves(jnp.transpose(w_out)), halves(w_up), halves(jnp.transpose(w_down))]

    def to_core(parts, shared):
        own, other = for_core(parts, core_bit), for_core(parts, 1 - core_bit)
        if shared is not None:
            own = jnp.concatenate([own, shared], 1)
            other = jnp.concatenate([other, shared], 1)
        return in_order(core_bit, own, swap(other, CORE_BIT), 0)

    def full_rows(pieces):
        stacked = in_order(slot_bit, pieces, swap(pieces, SLOT_BIT), 1)
        return stacked.reshape(width, pieces.shape[-1])

    def to_slot(values):
        own = lax.dynamic_index_in_dim(values, slot_bit, 1, keepdims=False)
        other = lax.dynamic_index_in_dim(values, 1 - slot_bit, 1, keepdims=False)
        return jnp.concatenate([own, swap(other, SLOT_BIT)], 0)

    def from_slot(rows):
        returned = swap(rows[shard_pos:], SLOT_BIT)
        return in_order(slot_bit, rows[:shard_pos], returned, 1)

    rows_low = to_slot(hidden_in)
    first_pack = to_core(first_parts, vectors)
    gathered_rows = gather_blocks(rows_low)
    gathered_first = gather_blocks(first_pack.reshape(2 * shard_rows, -1))
    pair_rows = jnp.stack([gathered_rows, swap(gathered_rows, TP_BIT)], 1)
    slot_rows = jnp.stack([pair_rows, swap(pair_rows, CORE_BIT)], 1)
    slot_rows = slot_rows.reshape(-1, width)
    first_full = full_rows(gathered_first)
    later_pack = to_core(later_parts, None).reshape(2 * shard_rows, -1)
    out_piece = gather_blocks(later_pack[:, :head_cols])
    up_piece = gather_blocks(later_pack[:, head_cols : head_cols + unit_cols])
    down_piece = gather_blocks(later_pack[:, head_cols + unit_cols :])
    out_weight = full_rows(out_piece)
    up_weight = full_rows(up_piece)
    down_weight = full_rows(down_piece)
    qkv_weight = first_full[:, : 3 * head_cols]
    vector_cols = first_full[:, 3 * head_cols :].astype(wide)
    (
        query_bias_all,
        value_bias_all,
        out_bias,
        gain_one,
        shift_one,
        down_bias,
        gain_two,
        shift_two,
    ) = [vector_cols[:, i] for i in range(8)]
    up_bias_all = vector_cols[:, 8 : 8 + b_up.shape[0] // shard_rows].reshape(-1)
    quarter = 2 * tp_bit + core_bit
    query_bias = lax.dynamic_slice_in_dim(query_bias_all, quarter * head_cols, head_cols)
    value_bias = lax.dynamic_slice_in_dim(value_bias_all, quarter * head_cols, head_cols)
    up_bias = lax.dynamic_slice_in_dim(up_bias_all, quarter * unit_cols, unit_cols)

    def positions_of(block_ids):
        shape = (block_ids.shape[0], 2, 2, 2, shard_pos)
        iota = lambda dim: lax.broadcasted_iota(jnp.int32, shape, dim)
        place = block_ids.reshape(-1, 1, 1, 1, 1) * 2 + (iota(3) ^ slot_bit)
        place = (place * 2 + (iota(1) ^ core_bit)) * 2 + (iota(2) ^ tp_bit)
        return (place * shard_pos + iota(4)).reshape(-1)

    length = lax.dynamic_index_in_dim(lengths, slot_bit, 0, keepdims=False)
    slot_live = positions_of(jnp.arange(blocks)) < length
    group_live = positions_of(block.reshape(1)) < length
    row_live = group_live[:rows_here]

    group_count = 4 * rows_here
    own_rows = lax.dynamic_slice_in_dim(slot_rows, block * group_count, group_count, 0)

    def as_heads(values):
        return values.reshape(values.shape[0], heads, HD)

    queries = (
        jnp.dot(slot_rows, qkv_weight[:, :head_cols], preferred_element_type=wide) + query_bias
    ).astype(low_type)
    keys = jnp.dot(
        slot_rows, qkv_weight[:, head_cols : 2 * head_cols], preferred_element_type=wide
    ).astype(low_type)
    values = (
        jnp.dot(slot_rows, qkv_weight[:, 2 * head_cols :], preferred_element_type=wide)
        + value_bias
    ).astype(low_type)
    query_all, key_all, value_all = as_heads(queries), as_heads(keys), as_heads(values)

    def own_of(array):
        return lax.dynamic_slice_in_dim(array, block * group_count, group_count, 0)

    query_own, key_own, value_own = own_of(query_all), own_of(key_all), own_of(value_all)
    scores = (
        jnp.einsum("qhd,khd->hqk", query_own, key_all, preferred_element_type=wide) * score_scale
    )
    masked = jnp.where(slot_live[None, None, :], scores, masked_score)
    top = jnp.max(masked, axis=2, keepdims=True)
    total = jnp.sum(jnp.exp(masked - top), axis=2, keepdims=True)
    log_total = top + jnp.log(total)
    weights = jnp.exp(masked - log_total)
    attended = jnp.einsum(
        "hqk,khd->qhd", weights.astype(low_type), value_all, preferred_element_type=wide
    )
    attended_low = attended.reshape(group_count, head_cols).astype(low_type)

    branch_one = sum_group(
        jnp.einsum("th,dh->td", attended_low, out_weight, preferred_element_type=wide)
    )
    first_sum = rows_low.astype(wide) + branch_one + out_bias
    normed_one, scale_one = norm_parts(first_sum)
    first_out = normed_one * gain_one + shift_one
    group_first = gather_group(first_out.astype(low_type))
    preact = jnp.dot(group_first, up_weight, preferred_element_type=wide) + up_bias
    spread = 0.5 * (1.0 + lax.erf(preact * (0.5**0.5)))
    active_low = (preact * spread).astype(low_type)
    branch_two = sum_group(
        jnp.einsum("tf,df->td", active_low, down_weight, preferred_element_type=wide)
    )
    normed_two, scale_two = norm_parts(first_out + branch_two + down_bias)
    output = normed_two * gain_two + shift_two
    grad_out = to_slot(cotangent).astype(wide) * row_live[:, None].astype(wide)
    second_grad = norm_back(grad_out, normed_two, scale_two, gain_two)
    gain_two_grad = jnp.sum(grad_out * normed_two, axis=0)
    shift_two_grad = jnp.sum(grad_out, axis=0)
    branch_two_grad = second_grad.astype(low_type)
    down_bias_grad = jnp.sum(branch_two_grad.astype(wide), axis=0)
    group_two = gather_group(branch_two_grad)
    active_grad = jnp.einsum("td,df->tf", group_two, down_weight, preferred_element_type=wide)
    slope = spread + preact * jnp.exp(-0.5 * preact * preact) * (2.0 * jnp.pi) ** (-0.5)
    preact_grad = (active_grad * slope).astype(low_type)
    up_bias_grad = jnp.sum(preact_grad.astype(wide), axis=0)
    first_out_grad = second_grad + sum_group(
        jnp.einsum("tf,df->td", preact_grad, up_weight, preferred_element_type=wide)
    )

    def sum_weight(partial):
        cols = partial.shape[1]
        split = partial.astype(low_type).reshape(blocks, 2, 2 * shard_rows, cols)
        own = lax.dynamic_index_in_dim(split, slot_bit, 1, keepdims=False)
        other = lax.dynamic_index_in_dim(split, 1 - slot_bit, 1, keepdims=False)
        half = own.astype(wide) + swap(other, SLOT_BIT).astype(wide)
        pieces = over_blocks(half.astype(low_type))
        summed = jnp.sum(pieces.astype(wide), axis=0).reshape(2, shard_rows, cols)
        mine = lax.dynamic_index_in_dim(summed, core_bit, 0, keepdims=False)
        theirs = lax.dynamic_index_in_dim(summed, 1 - core_bit, 0, keepdims=False)
        return in_order(core_bit, mine, swap(theirs, CORE_BIT), 1)

    up_grad = sum_weight(
        jnp.einsum("td,tf->df", group_first, preact_grad, preferred_element_type=wide)
    )
    down_grad = sum_weight(
        jnp.einsum("td,tf->df", group_two, active_low, preferred_element_type=wide)
    )
    gain_one_grad = jnp.sum(first_out_grad * normed_one, axis=0)
    shift_one_grad = jnp.sum(first_out_grad, axis=0)
    first_grad = norm_back(first_out_grad, normed_one, scale_one, gain_one)
    branch_one_grad = first_grad.astype(low_type)
    out_bias_grad = jnp.sum(branch_one_grad.astype(wide), axis=0)
    group_one = gather_group(branch_one_grad)
    attended_grad = jnp.dot(group_one, out_weight, preferred_element_type=wide).astype(low_type)
    grad_all = as_heads(gather_blocks(attended_grad).reshape(-1, head_cols))
    grad_own = as_heads(attended_grad)
    delta = jnp.einsum("qhd,qhd->hq", grad_own.astype(wide), attended)
    row_stats = gather_blocks(jnp.stack([log_total[:, :, 0], delta]))
    row_stats = jnp.moveaxis(row_stats, 0, 2).reshape(2, heads, -1)
    out_grad = sum_weight(
        jnp.einsum("td,th->dh", group_one, attended_low, preferred_element_type=wide)
    )

    weight_grad = jnp.einsum("qhd,khd->hqk", grad_own, value_all, preferred_element_type=wide)
    score_grad = (weights * (weight_grad - delta[:, :, None])).astype(low_type)
    query_grad = (
        jnp.einsum("hqk,khd->qhd", score_grad, key_all, preferred_element_type=wide) * score_scale
    )
    scores_back = (
        jnp.einsum("qhd,khd->hqk", query_all, key_own, preferred_element_type=wide) * score_scale
    )
    weights_back = jnp.where(
        group_live[None, None, :], jnp.exp(scores_back - row_stats[0][:, :, None]), 0.0
    )
    value_grad = jnp.einsum(
        "hqk,qhd->khd", weights_back.astype(low_type), grad_all, preferred_element_type=wide
    )
    back_grad = jnp.einsum("qhd,khd->hqk", grad_all, value_own, preferred_element_type=wide)
    back_score = (weights_back * (back_grad - row_stats[1][:, :, None])).astype(low_type)
    key_grad = (
        jnp.einsum("hqk,qhd->khd", back_score, query_all, preferred_element_type=wide)
        * score_scale
    )
    qkv_grad = jnp.concatenate(
        [
            grad.reshape(group_count, head_cols).astype(low_type)
            for grad in (query_grad, key_grad, value_grad)
        ],
        1,
    )
    qkv_sums = sum_weight(
        jnp.einsum("td,te->de", own_rows, qkv_grad, preferred_element_type=wide)
    )
    hidden_grad = first_grad + sum_group(
        jnp.einsum("te,de->td", qkv_grad, qkv_weight, preferred_element_type=wide)
    )
    bias_sums = jnp.sum(qkv_grad.astype(wide), axis=0)

    def widen(part):
        full = jnp.zeros((4 * part.shape[0],), wide)
        return lax.dynamic_update_slice_in_dim(full, part, quarter * part.shape[0], 0)

    fsdp_count = lax.axis_size("fsdp")
    all_vectors = jnp.concatenate(
        [
            vector.reshape(fsdp_count, -1)
            for vector in (
                widen(bias_sums[:head_cols]),
                widen(bias_sums[2 * head_cols :]),
                out_bias_grad,
                gain_one_grad,
                shift_one_grad,
                down_bias_grad,
                gain_two_grad,
                shift_two_grad,
                widen(up_bias_grad),
            )
        ],
        1,
    )
    vector_sum = jnp.sum(lax.all_to_all(all_vectors, "fsdp", 0, 0, tiled=True), axis=0)
    vector_sum = vector_sum + swap(vector_sum, TP_BIT)
    vector_grads = [
        vector_sum[i * shard_rows : (i + 1) * shard_rows] for i in range(8)
    ] + [vector_sum[8 * shard_rows :]]

    def columns(array):
        return array.reshape(shard_rows, -1)

    query_sum, key_sum, value_sum = [
        columns(qkv_sums[:, :, i * head_cols : (i + 1) * head_cols]) for i in range(3)
    ]
    return (
        from_slot(output.astype(low_type)),
        from_slot(hidden_grad),
        query_sum,
        vector_grads[0],
        key_sum,
        value_sum,
        vector_grads[1],
        jnp.transpose(columns(out_grad)),
        vector_grads[2],
        vector_grads[3],
        vector_grads[4],
        columns(up_grad),
        vector_grads[8],
        jnp.transpose(columns(down_grad)),
        vector_grads[5],
        vector_grads[6],
        vector_grads[7],
    )

BIT_TP, BIT_CORE, BIT_SIDE, BIT_LOW, BIT_HIGH = 1, 2, 4, 8, 16
TEAM_BITS = (BIT_TP, BIT_LOW, BIT_TP | BIT_LOW)
PART_BITS = (BIT_SIDE, BIT_CORE, BIT_SIDE | BIT_CORE)


class Place:
    def __init__(self):
        fsdp = lax.axis_index("fsdp")
        self.tp = lax.axis_index("tp")
        self.core = fsdp & 1
        self.side = (fsdp >> 1) & 1
        self.low = (fsdp >> 2) & 1
        self.high = fsdp >> 3
        self.quarter = 2 * self.tp + self.low


def run_kernel(body, outs, *operands, scratch=(), sems=0, apart=False, us=1.0, name=None):
    def space(operand):
        if operand.dtype == jnp.int32:
            return pltpu.SMEM
        return pltpu.HBM if apart else pltpu.VMEM

    scratches = [pltpu.VMEM(shape, kind) for shape, kind in scratch]
    if sems:
        scratches.append(pltpu.SemaphoreType.DMA((sems,)))
    return pl.pallas_call(
        body,
        out_shape=[jax.ShapeDtypeStruct(shape, kind) for shape, kind in outs],
        in_specs=[pl.BlockSpec(memory_space=space(operand)) for operand in operands],
        out_specs=[pl.BlockSpec(memory_space=pltpu.VMEM)] * len(outs),
        scratch_shapes=scratches,
        compiler_params=pltpu.CompilerParams(vmem_limit_bytes=8 << 20),
        cost_estimate=pl.CostEstimate(
            flops=int(us * 1.0e7), transcendentals=0, bytes_accessed=int(us * 1.0e4)
        ),
        name=name,
    )(*[pltpu.with_memory_space_constraint(op, pltpu.HBM) if apart else op for op in operands])


def tie(value, *others):
    return lax.optimization_barrier((value, others))[0]


def mul(left, right, left_dim=1, right_dim=0):
    return lax.dot_general(
        left, right, (((left_dim,), (right_dim,)), ((), ())), preferred_element_type=wide
    )


def bit_of(index, stride):
    return (index // stride) & 1


def place_of(index, parts, shard_pos):
    here = Place()
    shard = index & (shard_pos - 1)
    high = here.high ^ bit_of(index, shard_pos)
    tp = here.tp ^ bit_of(index, 2 * shard_pos)
    low = here.low ^ bit_of(index, 4 * shard_pos)
    side, core = here.side, here.core
    if parts:
        side = side ^ bit_of(index, 8 * shard_pos)
        core = core ^ bit_of(index, 16 * shard_pos)
    block = (high * 2 + low) * 4 + side * 2 + core
    return (block * 2 + tp) * shard_pos + shard


def live_rows_of(lengths_ref, index, parts, shard_pos):
    return place_of(index, parts, shard_pos) < lengths_ref[Place().high]


def row_of(chip, core, rows):
    return pl.ds(pl.multiple_of((2 * chip + core) * rows, 16), rows)


def join_pieces(piece_refs, full_ref, rows, begin, cols=slice(None)):
    here = Place()
    for which, ref in enumerate(piece_refs):
        side, core = here.side ^ ((which >> 1) & 1), here.core ^ (which >> 2)
        for inner in range(2):
            block = (here.high ^ (which & 1)) * 2 + (here.low ^ inner)
            piece = ref[inner, begin : begin + rows, cols]
            full_ref[row_of(block * 2 + side, core, rows), :] = piece


def split_rows(full_ref, keep_ref, send_ref, begin, cols):
    core = Place().core
    rows = keep_ref.shape[1]
    for chip in range(keep_ref.shape[0]):
        keep_ref[chip, :, begin : begin + cols] = full_ref[row_of(chip, core, rows), 0:cols]
        send_ref[chip] = full_ref[row_of(chip, 1 - core, rows), 0:cols]


def pack_kernel(count, *refs):
    sources, refs = refs[:count], refs[count:]
    outs, held, sems = refs[:7], refs[7:-1], refs[-1]
    copies = [
        pltpu.make_async_copy(source, target, sems.at[i])
        for i, (source, target) in enumerate(zip(sources, held))
    ]
    for copy in copies:
        copy.start()
    wq_ref, wk_ref, wv_ref, wo_ref, wu_ref, wd_ref = held[:6]
    own_ref, send_ref, later_own_ref, near_ref, hidden_ref, cot_ref, other_ref = outs
    size, shard = send_ref.shape[0], hidden_ref.shape[0]
    rows = wq_ref.shape[0]
    head_cols = wq_ref.shape[1] // 2
    unit_cols = wu_ref.shape[1] // 2
    low = Place().low
    near = Place().high == 0
    for i, out_ref in ((15, hidden_ref), (16, cot_ref)):
        copies[i].wait()
        first, second = held[i][:, 0, :], held[i][:, 1, :]
        out_ref[...] = jnp.where(near, first, second)
        other_ref[(i - 15) * shard : (i - 14) * shard, :] = jnp.where(near, second, first)
    for copy in copies[6:15]:
        copy.wait()
    vectors = [ref[...].astype(wide).reshape(1, rows) for ref in held[6:14]]
    block = jnp.concatenate(
        [
            jnp.pad(jnp.concatenate(vectors, 0), ((0, 0), (0, 4 * rows - rows))),
            held[14][...].astype(wide).reshape(1, 4 * rows),
            jnp.zeros((7, 4 * rows), wide),
        ],
        0,
    ).astype(low_type)
    for out_ref in (own_ref, send_ref, near_ref):
        out_ref[rows : rows + 16, 0 : 4 * rows] = block
        out_ref[rows : rows + 16, 4 * rows :] = jnp.zeros(
            (16, out_ref.shape[1] - 4 * rows), low_type
        )
    for copy in copies[:6]:
        copy.wait()
    for half in range(2):
        heads = slice(half * head_cols, (half + 1) * head_cols)
        units = slice(half * unit_cols, (half + 1) * unit_cols)

        def put_first(first_ref):
            for i, ref in enumerate((wq_ref, wk_ref, wv_ref, wo_ref)):
                first_ref[0:rows, i * head_cols : (i + 1) * head_cols] = ref[:, heads]

        def put_later(later_ref, begin):
            later_ref[begin : begin + rows, :] = wu_ref[:, units]
            later_ref[begin + rows : begin + 2 * rows, :] = wd_ref[:, units]

        @pl.when(low == half)
        def _():
            put_first(own_ref)
            put_later(later_own_ref, 0)

        @pl.when(low != half)
        def _():
            put_first(send_ref)
            put_first(near_ref)
            put_later(near_ref, size)


def by_chip_row(here, refs, high, low, rows, cols):
    near = high == 0
    p0, p1, p2, p3 = [
        jnp.where(
            near,
            refs[2 * part][low, rows : rows + 16, 0:cols].astype(wide),
            refs[2 * part + 1][low, rows : rows + 16, 0:cols].astype(wide),
        )
        for part in range(4)
    ]
    left = here.side == 0
    own = jnp.where(left, p0, p1), jnp.where(left, p1, p0)
    other = jnp.where(left, p2, p3), jnp.where(left, p3, p2)
    even = here.core == 0
    result = []
    for side in range(2):
        result.append(jnp.where(even, own[side], other[side]))
        result.append(jnp.where(even, other[side], own[side]))
    return result


def project_kernel(
    keep_ref, got_ref, tp_ref, low_ref, both_ref, *refs
):
    parts, outs = refs[:8], refs[8:]
    rows_ref, query_ref, pair_ref, rest_ref, weight_ref, out_weight_ref = outs
    rows = parts[0].shape[1] - 16
    head_cols = query_ref.shape[1]
    join_pieces(parts, weight_ref, rows, 0, slice(0, 3 * head_cols))
    join_pieces(parts, out_weight_ref, rows, 0, slice(3 * head_cols, 4 * head_cols))
    shard = keep_ref.shape[0]
    rows_ref[0:shard, :] = keep_ref[...]
    rows_ref[shard : 2 * shard, :] = got_ref[0:shard, :]
    for i, ref in enumerate((tp_ref, low_ref, both_ref)):
        rows_ref[2 * shard * (i + 1) : 2 * shard * (i + 2), :] = ref[...]
    here = Place()
    biases = jnp.concatenate(by_chip_row(here, parts, here.high ^ here.tp, 0, rows, rows), 1)
    query_bias, value_bias = biases[0:1], biases[1:2]
    made = mul(rows_ref[...], weight_ref[...])
    query_ref[...] = (made[:, 0:head_cols] + query_bias).astype(low_type)
    values = made[:, 2 * head_cols :] + value_bias
    split = pair_ref.shape[1] - head_cols
    pair_ref[:, 0:head_cols] = made[:, head_cols : 2 * head_cols].astype(low_type)
    pair_ref[:, head_cols:] = values[:, 0:split].astype(low_type)
    rest_ref[...] = values[:, split:].astype(low_type)


def joined_pair(pairs, rests, head_cols):
    pair = jnp.concatenate([ref[...] for ref in pairs], 0)
    rest = jnp.concatenate([ref[...] for ref in rests], 0)
    return pair[:, 0:head_cols], jnp.concatenate([pair[:, head_cols:], rest], 1)


def head_of(array, head):
    return array[:, head * HD : (head + 1) * HD]


def attend_kernel(
    shard_pos, lengths_ref, query_ref, *refs
):
    pieces, (weight_ref, low_ref, stats_ref, keep_ref, *sends) = refs[:8], refs[8:]
    head_cols = query_ref.shape[1]
    count = query_ref.shape[0]
    keys, values = joined_pair(pieces[:4], pieces[4:], head_cols)
    queries = query_ref[...] * HD ** (-0.5)
    lanes = lax.broadcasted_iota(jnp.int32, (1, keys.shape[0]), 1)
    live = live_rows_of(lengths_ref, lanes, True, shard_pos)
    column = lax.broadcasted_iota(jnp.int32, (count, 128), 1)
    stats = jnp.zeros((count, 128), wide)
    parts = []
    for head in range(head_cols // HD):
        scores = mul(head_of(queries, head), head_of(keys, head), 1, 1)
        scores = jnp.where(live, scores, masked_score)
        top = jnp.max(scores, axis=1, keepdims=True)
        grown = jnp.exp(scores - top)
        total = jnp.sum(grown, axis=1, keepdims=True)
        weights = (grown * (1.0 / total)).astype(low_type)
        parts.append(mul(weights, head_of(values, head)))
        stats = jnp.where(column == head, top + jnp.log(total), stats)
    attended = jnp.concatenate(parts, 1).astype(low_type)
    low_ref[...] = attended
    stats_ref[...] = stats
    give_out(mul(attended, weight_ref[...], 1, 1), keep_ref, sends)


def full_kernel(*refs):
    pieces, outs = refs[:8], refs[8:]
    rows = pieces[0].shape[1] // 2
    for i, out_ref in enumerate(outs):
        join_pieces(pieces, out_ref, rows, i * rows)


def lines_kernel(*refs):
    parts, (vector_ref, bias_ref) = refs[:8], refs[8:]
    here = Place()
    rows = parts[0].shape[1] - 16
    vectors = []
    for block in range(4):
        high, low = (block >> 1) ^ here.high, (block & 1) ^ here.low
        vectors += by_chip_row(here, parts, high, low, rows, rows)
    vector_ref[...] = jnp.concatenate(vectors, 1)[0:8]
    bias = by_chip_row(here, parts, here.high ^ here.tp, 0, rows, 4 * rows)
    bias_ref[...] = jnp.concatenate(bias, 1)[8:9]


def give_out(partial, keep_ref, sends):
    count = keep_ref.shape[0]
    keep_ref[...] = partial[0:count]
    for i, ref in enumerate(sends):
        ref[...] = partial[(i + 1) * count : (i + 2) * count].astype(low_type)


def collect(keep_ref, *got):
    total = keep_ref[...]
    for ref in got:
        total = total + ref[...].astype(wide)
    return total


def vector_row(vector_ref, row):
    return vector_ref[row : row + 1, :]


def first_norm_kernel(
    keep_ref, got1_ref, got2_ref, got3_ref, own_ref, vector_ref,
    out_ref, low_ref, normed_ref, scale_ref,
):
    branch = collect(keep_ref, got1_ref, got2_ref, got3_ref)
    rows = own_ref[0 : branch.shape[0], :].astype(wide)
    normed, scale = norm_parts(rows + branch + vector_row(vector_ref, 2))
    out = normed * vector_row(vector_ref, 3) + vector_row(vector_ref, 4)
    out_ref[...] = out
    low_ref[...] = out.astype(low_type)
    normed_ref[...] = normed
    scale_ref[...] = jnp.broadcast_to(scale, scale_ref.shape)


def spread_of(values):
    scaled = jnp.clip(values * (0.5**0.5), -3.832506856900711, 3.832506856900711)
    square = scaled * scaled
    top = jnp.full_like(values, 0.00022905065861350646)
    for term in (0.0034082910107109506, 0.050955695062380861, 0.18520832239976145, 1.128379143519084):
        top = top * square + term
    under = jnp.full_like(values, -1.1791602954361697e-7)
    for term in (
        0.000023547966471313185,
        0.0010179625278914885,
        0.014070470171167667,
        0.11098505178285362,
        0.49746925110067538,
        1.0,
    ):
        under = under * square + term
    return 0.5 + 0.5 * (scaled * top / under)


def hidden_kernel(
    own_ref, got1_ref, got2_ref, got3_ref, up_ref, down_ref, bias_ref,
    keep_ref, send1_ref, send2_ref, send3_ref, active_ref, slope_ref, rows_ref,
):
    rows = jnp.concatenate([r[...] for r in (own_ref, got1_ref, got2_ref, got3_ref)], 0)
    rows_ref[...] = rows
    preact = mul(rows, up_ref[...]) + bias_ref[...]
    spread = spread_of(preact)
    active = (preact * spread).astype(low_type)
    active_ref[...] = active
    slope_ref[...] = spread + preact * jnp.exp(-0.5 * preact * preact) * (2.0 * math.pi) ** (-0.5)
    give_out(mul(active, down_ref[...], 1, 1), keep_ref, (send1_ref, send2_ref, send3_ref))


def second_norm_kernel(
    lengths_ref, keep_ref, got1_ref, got2_ref, got3_ref, first_ref, own_ref, slot_ref, vector_ref,
    output_ref, grad_ref, low_ref, sums_ref,
):
    shard_pos = own_ref.shape[0]
    branch = collect(keep_ref, got1_ref, got2_ref, got3_ref)
    normed, scale = norm_parts(first_ref[...] + branch + vector_row(vector_ref, 5))
    gain = vector_row(vector_ref, 6)
    output_ref[...] = (normed * gain + vector_row(vector_ref, 7)).astype(low_type)
    index = lax.broadcasted_iota(jnp.int32, (2 * shard_pos, 1), 0)
    live = live_rows_of(lengths_ref, index, False, shard_pos)
    grad = jnp.concatenate([own_ref[...], slot_ref[shard_pos:, :]], 0).astype(wide)
    grad = jnp.where(live, grad, 0.0)
    second = norm_back(grad, normed, scale, gain)
    grad_ref[...] = second
    low = second.astype(low_type)
    low_ref[...] = low
    sums_ref[0:1, :] = jnp.sum(low.astype(wide), axis=0, keepdims=True)
    sums_ref[1:2, :] = jnp.sum(grad * normed, axis=0, keepdims=True)
    sums_ref[2:3, :] = jnp.sum(grad, axis=0, keepdims=True)


def hidden_back_kernel(
    own_ref, got1_ref, got2_ref, got3_ref, slope_ref, up_ref, down_ref,
    keep_ref, send1_ref, send2_ref, send3_ref, pre_ref, rows_ref, sums_ref,
):
    rows = jnp.concatenate([r[...] for r in (own_ref, got1_ref, got2_ref, got3_ref)], 0)
    rows_ref[...] = rows
    pre = (mul(rows, down_ref[...]) * slope_ref[...]).astype(low_type)
    pre_ref[...] = pre
    sums_ref[...] = jnp.sum(pre.astype(wide), axis=0, keepdims=True)
    give_out(mul(pre, up_ref[...], 1, 1), keep_ref, (send1_ref, send2_ref, send3_ref))


def weight_kernel(pairs, extra, *refs):
    operands = refs[: 2 * pairs + extra]
    keep_ref, *sends, full_ref = refs[2 * pairs + extra :]
    begin = 0
    for i, send_ref in enumerate(sends):
        left, right = operands[2 * i], operands[2 * i + 1]
        cols = right.shape[1]
        full_ref[:, 0:cols] = mul(left[...], right[...], 0, 0).astype(low_type)
        if extra and i == pairs - 1:
            total = operands[-2][...] + operands[-1][...]
            blank = jnp.zeros((128 - total.shape[0], total.shape[1]), wide)
            total = jnp.transpose(jnp.concatenate([total, blank], 0))
            full_ref[:, cols : cols + 128] = total.astype(low_type)
            cols += 128
        split_rows(full_ref, keep_ref, send_ref, begin, cols)
        begin += cols


def fold_kernel(count, bit, stride, *refs):
    keeps, got, outs = refs[:count], refs[count:-2], refs[-2:]
    own = getattr(Place(), bit)
    for choice, out_ref in enumerate(outs):
        for block in range(out_ref.shape[0]):
            index = block * stride[0] + (own ^ choice) * stride[1]
            begin = 0
            for i, got_ref in enumerate(got):
                end = begin + got_ref.shape[2]
                if count == 1:
                    total = keeps[0][index, :, begin:end].astype(wide)
                else:
                    total = keeps[i][index].astype(wide)
                out_ref[block, :, begin:end] = (total + got_ref[index].astype(wide)).astype(
                    out_ref.dtype
                )
                begin = end


def block_fold_kernel(keep_ref, got_ref, *outs):
    here = Place()
    for choice, out_ref in enumerate(outs):
        index = (here.high ^ (choice >> 1)) * 2 + (here.low ^ (choice & 1))
        out_ref[...] = (keep_ref[index] + got_ref[index].astype(wide)).astype(out_ref.dtype)


def final_fold_kernel(*refs):
    inputs, (own_ref, send_ref) = refs[:-2], refs[-2:]
    low = Place().low
    for choice, out_ref in ((low, own_ref), (1 - low, send_ref)):
        total = inputs[0][choice].astype(wide)
        for ref in inputs[1:]:
            total = total + ref[choice].astype(wide)
        out_ref[...] = total.astype(out_ref.dtype)


def total_kernel(spans, count, *refs):
    sources, outs = refs[:count], refs[count:]
    even = Place().low == 0
    own, got = sources[0][...], sources[1][...].astype(wide)
    if count == 4:
        own = own + sources[2][...].astype(wide)
        got = got + sources[3][...].astype(wide)
    for out_ref, (begin, end) in zip(outs, spans):
        cols = end - begin
        mine, other = own[:, begin:end], got[:, begin:end]
        out_ref[:, 0:cols] = jnp.where(even, mine, other)
        out_ref[:, cols:] = jnp.where(even, other, mine)
    vectors = outs[len(spans) :]
    if vectors:
        end = own.shape[1]
        rows = jnp.transpose(own[:, end - 128 :] + got[:, end - 128 :])
        for i, out_ref in enumerate(vectors[:-1]):
            out_ref[...] = rows[i : i + 1, :].reshape(out_ref.shape)
        first = len(vectors) - 1
        parts = [rows[first + i : first + i + 1, :] for i in range(4)]
        vectors[-1][...] = jnp.concatenate(parts, 1).reshape(vectors[-1].shape)


def first_back_kernel(
    keep_ref, got1_ref, got2_ref, got3_ref, second_ref, normed_ref, scale_ref, vector_ref,
    grad_ref, low_ref, sums_ref,
):
    grad = second_ref[...] + collect(keep_ref, got1_ref, got2_ref, got3_ref)
    normed = normed_ref[...]
    first = norm_back(grad, normed, scale_ref[:, 0:1], vector_row(vector_ref, 3))
    grad_ref[...] = first
    low = first.astype(low_type)
    low_ref[...] = low
    sums_ref[0:1, :] = jnp.sum(low.astype(wide), axis=0, keepdims=True)
    sums_ref[1:2, :] = jnp.sum(grad * normed, axis=0, keepdims=True)
    sums_ref[2:3, :] = jnp.sum(grad, axis=0, keepdims=True)


def attended_back_kernel(
    own_ref, got1_ref, got2_ref, got3_ref, weight_ref, low_ref, stats_ref, query_ref,
    packet_ref, rows_ref, sums_ref,
):
    rows = jnp.concatenate([r[...] for r in (own_ref, got1_ref, got2_ref, got3_ref)], 0)
    rows_ref[...] = rows
    made = mul(rows, weight_ref[...])
    head_cols = made.shape[1]
    sums_ref[...] = jnp.sum(made, axis=0, keepdims=True)
    grad = made.astype(low_type)
    packet_ref[:, 0:head_cols] = grad
    packet_ref[:, head_cols : 2 * head_cols] = query_ref[...]
    both = grad.astype(wide) * low_ref[...].astype(wide)
    column = lax.broadcasted_iota(jnp.int32, (made.shape[0], 128), 1)
    stats = stats_ref[...]
    levels = jnp.zeros_like(stats)
    heads = head_cols // HD
    for head in range(heads):
        delta = jnp.sum(head_of(both, head), axis=1, keepdims=True)
        for place, left in ((head, stats[:, head : head + 1]), (heads + head, delta)):
            for level in range(2):
                piece = left.astype(low_type).astype(wide)
                left = left - piece
                levels = jnp.where(column == 2 * place + level, piece, levels)
    packet_ref[:, 2 * head_cols :] = levels.astype(low_type)


def stat_of(packet, head_cols, place):
    base = 2 * head_cols + 2 * place
    first, second = packet[:, base : base + 1], packet[:, base + 1 : base + 2]
    return first.astype(wide) + second.astype(wide)


def query_back_kernel(shard_pos, lengths_ref, packet_ref, *refs):
    pieces, (out_ref, sums_ref) = refs[:8], refs[8:]
    head_cols = out_ref.shape[1]
    heads = head_cols // HD
    keys, values = joined_pair(pieces[:4], pieces[4:], head_cols)
    packet = packet_ref[...]
    grad = packet[:, 0:head_cols]
    queries = packet[:, head_cols : 2 * head_cols] * HD ** (-0.5)
    lanes = lax.broadcasted_iota(jnp.int32, (1, keys.shape[0]), 1)
    live = live_rows_of(lengths_ref, lanes, True, shard_pos)
    parts = []
    for head in range(heads):
        scores = mul(head_of(queries, head), head_of(keys, head), 1, 1)
        scores = jnp.where(live, scores, masked_score)
        weights = jnp.exp(scores - stat_of(packet, head_cols, head))
        weight_grad = mul(head_of(grad, head), head_of(values, head), 1, 1)
        weight_grad = weight_grad - stat_of(packet, head_cols, heads + head)
        parts.append(mul((weights * weight_grad).astype(low_type), head_of(keys, head)))
    made = (jnp.concatenate(parts, 1) * HD ** (-0.5)).astype(low_type)
    out_ref[...] = made
    sums_ref[...] = jnp.sum(made.astype(wide), axis=0, keepdims=True)


def pair_back_kernel(
    shard_pos, lengths_ref, pair_ref, rest_ref, query_grad_ref, weight_ref,
    g0_ref, g1_ref, g2_ref, g3_ref,
    keep_ref, send1_ref, send2_ref, send3_ref, made_ref,
):
    head_cols = query_grad_ref.shape[1]
    heads = head_cols // HD
    keys, values = joined_pair((pair_ref,), (rest_ref,), head_cols)
    packet = jnp.concatenate([ref[...] for ref in (g0_ref, g1_ref, g2_ref, g3_ref)], 0)
    grad = packet[:, 0:head_cols]
    queries = packet[:, head_cols : 2 * head_cols] * HD ** (-0.5)
    index = lax.broadcasted_iota(jnp.int32, (keys.shape[0], 1), 0)
    live = live_rows_of(lengths_ref, index, False, shard_pos)
    stats = jnp.transpose(packet[:, 2 * head_cols :].astype(wide))
    key_parts, value_parts = [], []
    for head in range(heads):
        log_total = stats[2 * head : 2 * head + 1] + stats[2 * head + 1 : 2 * head + 2]
        at = 2 * (heads + head)
        delta = stats[at : at + 1] + stats[at + 1 : at + 2]
        scores = mul(head_of(keys, head), head_of(queries, head), 1, 1)
        scores = jnp.where(live, scores, masked_score)
        weights = jnp.exp(scores - log_total)
        weight_grad = mul(head_of(values, head), head_of(grad, head), 1, 1)
        score_grad = (weights * (weight_grad - delta)).astype(low_type)
        key_parts.append(mul(score_grad, head_of(queries, head)))
        value_parts.append(mul(weights.astype(low_type), head_of(grad, head)))
    made = jnp.concatenate(
        [query_grad_ref[...]] + [part.astype(low_type) for part in key_parts + value_parts], 1
    )
    made_ref[...] = made
    give_out(mul(made, weight_ref[...], 1, 1), keep_ref, (send1_ref, send2_ref, send3_ref))


def slots_kernel(grad_ref, out_ref, got_ref, output_ref, hidden_grad_ref):
    near = Place().high == 0
    count, width = grad_ref.shape
    for target, own, got in (
        (hidden_grad_ref, grad_ref[...], got_ref[:, 0:width].astype(wide)),
        (output_ref, out_ref[0:count, :], got_ref[:, width:]),
    ):
        target[:, 0, :] = jnp.where(near, own, got)
        target[:, 1, :] = jnp.where(near, got, own)


def last_kernel(keep_ref, got1_ref, got2_ref, got3_ref, first_ref, output_ref, own_ref, send_ref):
    total = first_ref[...] + collect(keep_ref, got1_ref, got2_ref, got3_ref)
    count, width = own_ref.shape
    own_ref[...] = total[0:count]
    send_ref[:, 0:width] = total[count:].astype(send_ref.dtype)
    send_ref[:, width:] = output_ref[count:, :]


def vectors_kernel(shards, query_ref, value_ref, first_ref, second_ref, unit_ref, out_ref):
    width = out_ref.shape[1] // shards
    per = shards // 4
    quarter = Place().quarter
    out_ref[...] = jnp.zeros_like(out_ref)
    out_ref[2:5, :] = first_ref[0:3, :]
    out_ref[5:8, :] = second_ref[0:3, :]
    for which in range(4):

        @pl.when(quarter == which)
        def _():
            span = slice(which * per * width, (which + 1) * per * width)
            out_ref[0:1, span] = query_ref[...]
            out_ref[1:2, span] = value_ref[...]
            for i in range(4):
                parts = []
                for local in range(per):
                    begin = (4 * local + i) * width
                    parts.append(unit_ref[:, begin : begin + width])
                out_ref[8 + i : 9 + i, span] = jnp.concatenate(parts, 1)


def send_team(parts):
    return tuple(swap(parts[i], TEAM_BITS[i]) for i in (1, 0, 2))


def gather_team(rows):
    return tuple(swap(rows, bit) for bit in TEAM_BITS[::-1])[::-1]


def gather_parts(rows):
    side = swap(rows, BIT_SIDE)
    return rows, side, swap(rows, BIT_CORE), swap(side, BIT_CORE)


def local_32(
    hidden_in,
    cotangent,
    lengths,
    w_query,
    b_query,
    w_key,
    w_value,
    b_value,
    w_out,
    b_out,
    first_gain,
    first_shift,
    w_up,
    b_up,
    w_down,
    b_down,
    second_gain,
    second_shift,
):
    shard_pos, seq_count, width = hidden_in.shape
    rows_here = 2 * shard_pos
    group = 4 * rows_here
    shard_rows = w_query.shape[0]
    head_cols = w_query.shape[1] // 2
    unit_cols = w_up.shape[1] // 2
    chips = lax.axis_size("fsdp") // 2
    pair_cols = -(-head_cols // 128) * 128

    sources = (
        w_query, w_key, w_value, jnp.transpose(w_out), w_up, jnp.transpose(w_down),
        b_query, b_value, b_out, first_gain, first_shift, b_down, second_gain, second_shift, b_up,
        hidden_in, cotangent,
    )
    first = ((shard_rows + 16, 4 * head_cols), low_type)
    later = ((2 * shard_rows, unit_cols), low_type)
    near = ((3 * shard_rows + 16, unit_cols), low_type)
    shard = ((shard_pos, width), low_type)
    *packs, hidden_own, cot_own, other = run_kernel(
        functools.partial(pack_kernel, len(sources)),
        [first, first, later, near, shard, shard, ((rows_here, width), low_type)],
        *sources,
        scratch=[(source.shape, source.dtype) for source in sources],
        sems=len(sources),
        apart=True,
        us=3.0,
        name="pack",
    )

    slot_rows = swap(other, BIT_HIGH)
    first_own, first_send, later_own, near_send = tuple(packs)
    near_got = swap(near_send, BIT_LOW)
    size = first_own.shape[0]
    f2, f3 = swap(first_own, BIT_HIGH), swap(first_send, BIT_HIGH | BIT_LOW)
    first_near = jnp.stack([first_own, near_got[:size]])
    first_near_side = swap(first_near, BIT_SIDE)
    team_rows = gather_team(
        tie(jnp.concatenate([hidden_own, slot_rows[:shard_pos]], 0), packs)
    )
    first_far = tie(jnp.stack([f2, f3]), first_near_side)
    first_far_side = swap(first_far, BIT_SIDE)
    later_near = jnp.stack([later_own, near_got[size:]])
    later_far = swap(tie(later_near, first_far), BIT_HIGH)
    first_pieces = (
        first_near,
        first_far,
        first_near_side,
        first_far_side,
        swap(first_near, BIT_CORE),
        swap(first_far, BIT_CORE),
        swap(first_near_side, BIT_CORE),
        swap(tie(first_far_side, team_rows, later_near), BIT_CORE),
    )

    group_rows, queries, pair, rest, qkv_weight, out_weight = run_kernel(
        project_kernel,
        [
            ((group, width), low_type),
            ((group, head_cols), low_type),
            ((group, pair_cols), low_type),
            ((group, 2 * head_cols - pair_cols), low_type),
            ((width, 3 * head_cols), low_type),
            ((width, head_cols), low_type),
        ],
        hidden_own, slot_rows, *team_rows, *first_pieces,
        name="project",
    )
    pair_parts, rest_parts = gather_parts(pair), gather_parts(rest)
    later_near_side = swap(tie(later_near, pair_parts[1]), BIT_SIDE)
    vectors, up_bias = run_kernel(
        lines_kernel,
        [((8, width), wide), ((1, unit_cols), wide)],
        *tie(first_pieces, pair),
        us=0.5,
        name="lines",
    )
    rows_shape = (rows_here, width)
    given = [(rows_shape, wide)] + [(rows_shape, low_type)] * 3
    attended_low, stats, keep, *sends = run_kernel(
        functools.partial(attend_kernel, shard_pos),
        [((group, head_cols), low_type), ((group, 128), wide)] + given,
        lengths, tie(queries, vectors), *pair_parts, *rest_parts, out_weight,
        us=3.0,
        name="attend",
    )
    sends = send_team(sends)
    later_far_side = swap(tie(later_far, attended_low), BIT_SIDE)
    first_out, first_low, normed, scale = run_kernel(
        first_norm_kernel,
        [(rows_shape, wide), (rows_shape, low_type), (rows_shape, wide), ((rows_here, 128), wide)],
        keep, *sends, group_rows, vectors,
        us=0.5,
        name="first_norm",
    )
    first_team = gather_team(first_low)
    later_sides = tie((later_near, later_far, later_near_side, later_far_side), first_low)
    later_pieces = later_sides + tuple(swap(part, BIT_CORE) for part in later_sides)
    up_weight, down_weight = run_kernel(
        full_kernel,
        [((width, unit_cols), low_type)] * 2,
        *later_pieces,
        us=1.0,
        name="full_units",
    )
    keep, s1, s2, s3, active, slope, first_rows = run_kernel(
        hidden_kernel,
        given
        + [((group, unit_cols), low_type), ((group, unit_cols), wide), ((group, width), low_type)],
        first_low, *first_team, up_weight, down_weight, up_bias,
        us=2.0,
        name="hidden",
    )
    sends = send_team((s1, s2, s3))
    output, second_grad, second_low, second_sums = run_kernel(
        second_norm_kernel,
        [(rows_shape, low_type), (rows_shape, wide), (rows_shape, low_type), ((8, width), wide)],
        lengths, keep, *sends, first_out, cot_own, slot_rows, vectors,
        name="second_norm",
    )
    second_team = gather_team(second_low)
    def weight_parts(operands, name, extra=()):
        parts = [right.shape[1] for right in operands[1::2]]
        parts[-1] += 128 if extra else 0
        shapes = [(chips, shard_rows, cols) for cols in [sum(parts)] + parts]
        kept, *sent = run_kernel(
            functools.partial(weight_kernel, len(parts), len(extra)),
            [(shape, low_type) for shape in shapes],
            *operands, *extra,
            scratch=[((width, max(parts)), low_type)],
            name=name,
        )
        return kept, sent

    def finish(sources, spans, name, vectors=()):
        outs = [(shard_rows, 2 * (end - begin)) for begin, end in spans] + list(vectors)
        return run_kernel(
            functools.partial(total_kernel, spans, len(sources)),
            [(shape, wide) for shape in outs],
            *sources,
            us=0.7,
            name=name,
        )

    def fold(bit, stride, kept, got, name):
        cols = sum(part.shape[2] for part in kept)
        shape = (kept[0].shape[0] // 2, shard_rows, cols)
        return run_kernel(
            functools.partial(fold_kernel, len(kept), bit, stride),
            [(shape, wide), (shape, low_type)],
            *kept, *got,
            us=0.7,
            name=name + "_fold_" + bit,
        )

    keep, s1, s2, s3, pre_grad, second_rows, unit_sums = run_kernel(
        hidden_back_kernel,
        given
        + [((group, unit_cols), low_type), ((group, width), low_type), ((1, unit_cols), wide)],
        second_low, *second_team, slope, up_weight, down_weight,
        us=1.5,
        name="hidden_back",
    )
    unit_kept, unit_sent = weight_parts(
        (second_rows, active, first_rows, pre_grad), "unit_weights"
    )
    unit_got = [swap(part, BIT_CORE) for part in unit_sent]
    unit_kept, unit_sent = fold("side", (2, 1), [unit_kept], unit_got, "unit")
    unit_got = swap(unit_sent, BIT_SIDE)
    sends = send_team(tie((s1, s2, s3), unit_sent))
    first_grad, one_low, first_sums = run_kernel(
        first_back_kernel,
        [(rows_shape, wide), (rows_shape, low_type), ((8, width), wide)],
        keep, *sends, second_grad, normed, scale, vectors,
        us=0.7,
        name="first_back",
    )
    one_team = gather_team(one_low)
    packet, one_rows, value_sums = run_kernel(
        attended_back_kernel,
        [
            ((group, 2 * head_cols + 128), low_type),
            ((group, width), low_type),
            ((1, head_cols), wide),
        ],
        one_low, *one_team, out_weight, attended_low, stats, queries,
        us=0.7,
        name="attended_back",
    )
    packet_side = swap(packet, BIT_SIDE)
    query_grad, query_sums = run_kernel(
        functools.partial(query_back_kernel, shard_pos),
        [((group, head_cols), low_type), ((1, head_cols), wide)],
        lengths, packet, *pair_parts, *rest_parts,
        us=3.0,
        name="query_back",
    )
    packets = (
        packet,
        packet_side,
        swap(packet, BIT_CORE),
        swap(tie(packet_side, query_grad), BIT_CORE),
    )
    (sums,) = run_kernel(
        functools.partial(vectors_kernel, 2 * chips),
        [((16, width), wide)],
        query_sums, value_sums, first_sums, second_sums, unit_sums,
        us=0.5,
        name="vectors",
    )
    sums_got = swap(sums, BIT_TP)
    unit_kept, unit_sent = fold("high", (1, 2), [tie(unit_kept, packet)], [unit_got], "unit")
    unit_got = swap(unit_sent, BIT_HIGH)
    keep, s1, s2, s3, qkv_grad = run_kernel(
        functools.partial(pair_back_kernel, shard_pos),
        given + [((group, 3 * head_cols), low_type)],
        lengths, tie(pair, unit_kept), rest, query_grad, qkv_weight, *packets,
        us=4.0,
        name="pair_back",
    )
    late_kept, late_sent = weight_parts(
        (one_rows, attended_low, group_rows, tie(qkv_grad, unit_got)),
        "head_weights",
        (sums, sums_got),
    )
    late_got = [swap(part, BIT_CORE) for part in late_sent]
    lasts = send_team((s1, s2, s3))
    late_kept, late_sent = fold("side", (2, 1), [late_kept], late_got, "late")
    late_got = swap(late_sent, BIT_SIDE)
    late_shape = late_kept.shape[1:]
    late_own, s1, s2, s3 = run_kernel(
        block_fold_kernel,
        [(late_shape, wide)] + [(late_shape, low_type)] * 3,
        late_kept, late_got,
        us=0.5,
        name="late_block",
    )
    late_sums = (
        late_own, swap(s1, BIT_LOW), swap(s2, BIT_HIGH), swap(s3, BIT_HIGH | BIT_LOW)
    )
    grad_own, grad_send = run_kernel(
        last_kernel,
        [((shard_pos, width), wide), ((shard_pos, 2 * width), low_type)],
        tie(keep, late_kept), *lasts, first_grad, output,
        us=0.5,
        name="last",
    )
    grad_got = swap(grad_send, BIT_HIGH)
    unit_own, unit_sent = run_kernel(
        final_fold_kernel,
        [(unit_kept.shape[1:], wide), (unit_kept.shape[1:], low_type)],
        unit_kept, unit_got,
        us=0.5,
        name="unit_low",
    )
    down_grad, up_grad = finish(
        (unit_own, swap(unit_sent, BIT_LOW)), ((0, unit_cols), (unit_cols, 2 * unit_cols)), "unit_total"
    )
    out_grad, query_total, key_total, value_total, *shares = finish(
        tie(late_sums, down_grad, up_grad),
        [(i * head_cols, (i + 1) * head_cols) for i in range(4)],
        "late_total",
        [(shard_rows,)] * 8 + [b_up.shape],
    )
    whole_output, hidden_grad = run_kernel(
        slots_kernel,
        [(hidden_in.shape, low_type), (hidden_in.shape, wide)],
        grad_own, output, grad_got,
        us=0.5,
        name="slots",
    )
    return (
        whole_output,
        hidden_grad,
        query_total,
        shares[0],
        key_total,
        value_total,
        shares[1],
        jnp.transpose(out_grad),
        shares[2],
        shares[3],
        shares[4],
        up_grad,
        shares[8],
        jnp.transpose(down_grad),
        shares[5],
        shares[6],
        shares[7],
    )


def solution(mesh):
    in_specs = (
        P(("fsdp", "tp"), None, None),
        P(("fsdp", "tp"), None, None),
        P(),
        P("fsdp", "tp"),
        P("fsdp"),
        P("fsdp", "tp"),
        P("fsdp", "tp"),
        P("fsdp"),
        P("tp", "fsdp"),
        P("fsdp"),
        P("fsdp"),
        P("fsdp"),
        P("fsdp", "tp"),
        P("fsdp"),
        P("tp", "fsdp"),
        P("fsdp"),
        P("fsdp"),
        P("fsdp"),
    )
    out_specs = (
        P(("fsdp", "tp"), None, None),
        P(("fsdp", "tp"), None, None),
        P("fsdp", "tp"),
        P("fsdp"),
        P("fsdp", "tp"),
        P("fsdp", "tp"),
        P("fsdp"),
        P("tp", "fsdp"),
        P("fsdp"),
        P("fsdp"),
        P("fsdp"),
        P("fsdp", "tp"),
        P("fsdp"),
        P("tp", "fsdp"),
        P("fsdp"),
        P("fsdp"),
        P("fsdp"),
    )
    program = local_32 if mesh.shape["fsdp"] == 16 else local
    return jax.shard_map(program, mesh=mesh, in_specs=in_specs, out_specs=out_specs, check_vma=False)
```

```python
import functools
import math

import jax
import jax.numpy as jnp
from jax import lax
from jax.experimental import pallas as pl
from jax.experimental.pallas import tpu as pltpu
from jax.sharding import PartitionSpec as P

HD = 64
layer_eps = 1e-12
masked_score = -1e30
AXES = ("fsdp", "tp")
low_type = jnp.bfloat16
wide = jnp.float32

TP_BIT, CORE_BIT, SLOT_BIT, GROUP = 1, 2, 4, 8


def device_count():
    return lax.axis_size("fsdp") * lax.axis_size("tp")


def swap(values, bit):
    return lax.ppermute(values, AXES, [(i, i ^ bit) for i in range(device_count())])


def over_blocks(values):
    total = device_count()
    groups = [list(range(first, total, GROUP)) for first in range(GROUP)]
    return lax.all_to_all(values, AXES, 0, 0, axis_index_groups=groups)


def gather_blocks(values):
    blocks = device_count() // GROUP
    return over_blocks(jnp.broadcast_to(values[None], (blocks,) + values.shape))


def in_order(first_bit, own, other, axis):
    return jnp.where(
        first_bit == 0, jnp.stack([own, other], axis), jnp.stack([other, own], axis)
    )


def gather_group(rows):
    pair = jnp.concatenate([rows, swap(rows, TP_BIT)], 0)
    return jnp.concatenate([pair, swap(pair, CORE_BIT)], 0)


def sum_group(partial):
    half = partial.shape[0] // 2
    kept = partial[:half] + swap(partial[half:].astype(low_type), CORE_BIT).astype(wide)
    quarter = half // 2
    return kept[:quarter] + swap(kept[quarter:].astype(low_type), TP_BIT).astype(wide)


def norm_parts(values):
    centre = values - jnp.mean(values, axis=-1, keepdims=True)
    spread = jnp.mean(centre * centre, axis=-1, keepdims=True)
    scale = lax.rsqrt(spread + layer_eps)
    return centre * scale, scale


def norm_back(grad, normed, scale, gain):
    scaled = grad * gain
    mean_one = jnp.mean(scaled, axis=-1, keepdims=True)
    mean_two = jnp.mean(scaled * normed, axis=-1, keepdims=True)
    return scale * (scaled - mean_one - normed * mean_two)


def local(
    hidden_in,
    cotangent,
    lengths,
    w_query,
    b_query,
    w_key,
    w_value,
    b_value,
    w_out,
    b_out,
    first_gain,
    first_shift,
    w_up,
    b_up,
    w_down,
    b_down,
    second_gain,
    second_shift,
):
    fsdp_index = lax.axis_index("fsdp")
    tp_bit = lax.axis_index("tp")
    core_bit = fsdp_index % 2
    slot_bit = (fsdp_index // 2) % 2
    block = fsdp_index // 4
    blocks = lax.axis_size("fsdp") // 4
    shard_pos, seq_count, width = hidden_in.shape
    rows_here = 2 * shard_pos
    shard_rows = w_query.shape[0]
    head_cols = w_query.shape[1] // 2
    unit_cols = w_up.shape[1] // 2
    heads = head_cols // HD
    score_scale = HD ** (-0.5)

    def halves(weight):
        return weight.reshape(shard_rows, 2, weight.shape[1] // 2)

    def for_core(parts, which):
        return jnp.concatenate(
            [lax.dynamic_index_in_dim(part, which, 1, keepdims=False) for part in parts], 1
        )

    vectors = jnp.concatenate(
        [
            vector.reshape(shard_rows, -1)
            for vector in (
                b_query,
                b_value,
                b_out,
                first_gain,
                first_shift,
                b_down,
                second_gain,
                second_shift,
                b_up,
            )
        ],
        1,
    )
    vectors = jnp.pad(vectors, ((0, 0), (0, 128 - vectors.shape[1])))
    first_parts = [halves(w_query), halves(w_key), halves(w_value)]
    later_parts = [halves(jnp.transpose(w_out)), halves(w_up), halves(jnp.transpose(w_down))]

    def to_core(parts, shared):
        own, other = for_core(parts, core_bit), for_core(parts, 1 - core_bit)
        if shared is not None:
            own = jnp.concatenate([own, shared], 1)
            other = jnp.concatenate([other, shared], 1)
        return in_order(core_bit, own, swap(other, CORE_BIT), 0)

    def full_rows(pieces):
        stacked = in_order(slot_bit, pieces, swap(pieces, SLOT_BIT), 1)
        return stacked.reshape(width, pieces.shape[-1])

    def to_slot(values):
        own = lax.dynamic_index_in_dim(values, slot_bit, 1, keepdims=False)
        other = lax.dynamic_index_in_dim(values, 1 - slot_bit, 1, keepdims=False)
        return jnp.concatenate([own, swap(other, SLOT_BIT)], 0)

    def from_slot(rows):
        returned = swap(rows[shard_pos:], SLOT_BIT)
        return in_order(slot_bit, rows[:shard_pos], returned, 1)

    rows_low = to_slot(hidden_in)
    first_pack = to_core(first_parts, vectors)
    gathered_rows = gather_blocks(rows_low)
    gathered_first = gather_blocks(first_pack.reshape(2 * shard_rows, -1))
    pair_rows = jnp.stack([gathered_rows, swap(gathered_rows, TP_BIT)], 1)
    slot_rows = jnp.stack([pair_rows, swap(pair_rows, CORE_BIT)], 1)
    slot_rows = slot_rows.reshape(-1, width)
    first_full = full_rows(gathered_first)
    later_pack = to_core(later_parts, None).reshape(2 * shard_rows, -1)
    out_piece = gather_blocks(later_pack[:, :head_cols])
    up_piece = gather_blocks(later_pack[:, head_cols : head_cols + unit_cols])
    down_piece = gather_blocks(later_pack[:, head_cols + unit_cols :])
    out_weight = full_rows(out_piece)
    up_weight = full_rows(up_piece)
    down_weight = full_rows(down_piece)
    qkv_weight = first_full[:, : 3 * head_cols]
    vector_cols = first_full[:, 3 * head_cols :].astype(wide)
    (
        query_bias_all,
        value_bias_all,
        out_bias,
        gain_one,
        shift_one,
        down_bias,
        gain_two,
        shift_two,
    ) = [vector_cols[:, i] for i in range(8)]
    up_bias_all = vector_cols[:, 8 : 8 + b_up.shape[0] // shard_rows].reshape(-1)
    quarter = 2 * tp_bit + core_bit
    query_bias = lax.dynamic_slice_in_dim(query_bias_all, quarter * head_cols, head_cols)
    value_bias = lax.dynamic_slice_in_dim(value_bias_all, quarter * head_cols, head_cols)
    up_bias = lax.dynamic_slice_in_dim(up_bias_all, quarter * unit_cols, unit_cols)

    def positions_of(block_ids):
        shape = (block_ids.shape[0], 2, 2, 2, shard_pos)
        iota = lambda dim: lax.broadcasted_iota(jnp.int32, shape, dim)
        place = block_ids.reshape(-1, 1, 1, 1, 1) * 2 + (iota(3) ^ slot_bit)
        place = (place * 2 + (iota(1) ^ core_bit)) * 2 + (iota(2) ^ tp_bit)
        return (place * shard_pos + iota(4)).reshape(-1)

    length = lax.dynamic_index_in_dim(lengths, slot_bit, 0, keepdims=False)
    slot_live = positions_of(jnp.arange(blocks)) < length
    group_live = positions_of(block.reshape(1)) < length
    row_live = group_live[:rows_here]

    group_count = 4 * rows_here
    own_rows = lax.dynamic_slice_in_dim(slot_rows, block * group_count, group_count, 0)

    def as_heads(values):
        return values.reshape(values.shape[0], heads, HD)

    queries = (
        jnp.dot(slot_rows, qkv_weight[:, :head_cols], preferred_element_type=wide) + query_bias
    ).astype(low_type)
    keys = jnp.dot(
        slot_rows, qkv_weight[:, head_cols : 2 * head_cols], preferred_element_type=wide
    ).astype(low_type)
    values = (
        jnp.dot(slot_rows, qkv_weight[:, 2 * head_cols :], preferred_element_type=wide)
        + value_bias
    ).astype(low_type)
    query_all, key_all, value_all = as_heads(queries), as_heads(keys), as_heads(values)

    def own_of(array):
        return lax.dynamic_slice_in_dim(array, block * group_count, group_count, 0)

    query_own, key_own, value_own = own_of(query_all), own_of(key_all), own_of(value_all)
    scores = (
        jnp.einsum("qhd,khd->hqk", query_own, key_all, preferred_element_type=wide) * score_scale
    )
    masked = jnp.where(slot_live[None, None, :], scores, masked_score)
    top = jnp.max(masked, axis=2, keepdims=True)
    total = jnp.sum(jnp.exp(masked - top), axis=2, keepdims=True)
    log_total = top + jnp.log(total)
    weights = jnp.exp(masked - log_total)
    attended = jnp.einsum(
        "hqk,khd->qhd", weights.astype(low_type), value_all, preferred_element_type=wide
    )
    attended_low = attended.reshape(group_count, head_cols).astype(low_type)

    branch_one = sum_group(
        jnp.einsum("th,dh->td", attended_low, out_weight, preferred_element_type=wide)
    )
    first_sum = rows_low.astype(wide) + branch_one + out_bias
    normed_one, scale_one = norm_parts(first_sum)
    first_out = normed_one * gain_one + shift_one
    group_first = gather_group(first_out.astype(low_type))
    preact = jnp.dot(group_first, up_weight, preferred_element_type=wide) + up_bias
    spread = 0.5 * (1.0 + lax.erf(preact * (0.5**0.5)))
    active_low = (preact * spread).astype(low_type)
    branch_two = sum_group(
        jnp.einsum("tf,df->td", active_low, down_weight, preferred_element_type=wide)
    )
    normed_two, scale_two = norm_parts(first_out + branch_two + down_bias)
    output = normed_two * gain_two + shift_two
    grad_out = to_slot(cotangent).astype(wide) * row_live[:, None].astype(wide)
    second_grad = norm_back(grad_out, normed_two, scale_two, gain_two)
    gain_two_grad = jnp.sum(grad_out * normed_two, axis=0)
    shift_two_grad = jnp.sum(grad_out, axis=0)
    branch_two_grad = second_grad.astype(low_type)
    down_bias_grad = jnp.sum(branch_two_grad.astype(wide), axis=0)
    group_two = gather_group(branch_two_grad)
    active_grad = jnp.einsum("td,df->tf", group_two, down_weight, preferred_element_type=wide)
    slope = spread + preact * jnp.exp(-0.5 * preact * preact) * (2.0 * jnp.pi) ** (-0.5)
    preact_grad = (active_grad * slope).astype(low_type)
    up_bias_grad = jnp.sum(preact_grad.astype(wide), axis=0)
    first_out_grad = second_grad + sum_group(
        jnp.einsum("tf,df->td", preact_grad, up_weight, preferred_element_type=wide)
    )

    def sum_weight(partial):
        cols = partial.shape[1]
        split = partial.astype(low_type).reshape(blocks, 2, 2 * shard_rows, cols)
        own = lax.dynamic_index_in_dim(split, slot_bit, 1, keepdims=False)
        other = lax.dynamic_index_in_dim(split, 1 - slot_bit, 1, keepdims=False)
        half = own.astype(wide) + swap(other, SLOT_BIT).astype(wide)
        pieces = over_blocks(half.astype(low_type))
        summed = jnp.sum(pieces.astype(wide), axis=0).reshape(2, shard_rows, cols)
        mine = lax.dynamic_index_in_dim(summed, core_bit, 0, keepdims=False)
        theirs = lax.dynamic_index_in_dim(summed, 1 - core_bit, 0, keepdims=False)
        return in_order(core_bit, mine, swap(theirs, CORE_BIT), 1)

    up_grad = sum_weight(
        jnp.einsum("td,tf->df", group_first, preact_grad, preferred_element_type=wide)
    )
    down_grad = sum_weight(
        jnp.einsum("td,tf->df", group_two, active_low, preferred_element_type=wide)
    )
    gain_one_grad = jnp.sum(first_out_grad * normed_one, axis=0)
    shift_one_grad = jnp.sum(first_out_grad, axis=0)
    first_grad = norm_back(first_out_grad, normed_one, scale_one, gain_one)
    branch_one_grad = first_grad.astype(low_type)
    out_bias_grad = jnp.sum(branch_one_grad.astype(wide), axis=0)
    group_one = gather_group(branch_one_grad)
    attended_grad = jnp.dot(group_one, out_weight, preferred_element_type=wide).astype(low_type)
    grad_all = as_heads(gather_blocks(attended_grad).reshape(-1, head_cols))
    grad_own = as_heads(attended_grad)
    delta = jnp.einsum("qhd,qhd->hq", grad_own.astype(wide), attended)
    row_stats = gather_blocks(jnp.stack([log_total[:, :, 0], delta]))
    row_stats = jnp.moveaxis(row_stats, 0, 2).reshape(2, heads, -1)
    out_grad = sum_weight(
        jnp.einsum("td,th->dh", group_one, attended_low, preferred_element_type=wide)
    )

    weight_grad = jnp.einsum("qhd,khd->hqk", grad_own, value_all, preferred_element_type=wide)
    score_grad = (weights * (weight_grad - delta[:, :, None])).astype(low_type)
    query_grad = (
        jnp.einsum("hqk,khd->qhd", score_grad, key_all, preferred_element_type=wide) * score_scale
    )
    scores_back = (
        jnp.einsum("qhd,khd->hqk", query_all, key_own, preferred_element_type=wide) * score_scale
    )
    weights_back = jnp.where(
        group_live[None, None, :], jnp.exp(scores_back - row_stats[0][:, :, None]), 0.0
    )
    value_grad = jnp.einsum(
        "hqk,qhd->khd", weights_back.astype(low_type), grad_all, preferred_element_type=wide
    )
    back_grad = jnp.einsum("qhd,khd->hqk", grad_all, value_own, preferred_element_type=wide)
    back_score = (weights_back * (back_grad - row_stats[1][:, :, None])).astype(low_type)
    key_grad = (
        jnp.einsum("hqk,qhd->khd", back_score, query_all, preferred_element_type=wide)
        * score_scale
    )
    qkv_grad = jnp.concatenate(
        [
            grad.reshape(group_count, head_cols).astype(low_type)
            for grad in (query_grad, key_grad, value_grad)
        ],
        1,
    )
    qkv_sums = sum_weight(
        jnp.einsum("td,te->de", own_rows, qkv_grad, preferred_element_type=wide)
    )
    hidden_grad = first_grad + sum_group(
        jnp.einsum("te,de->td", qkv_grad, qkv_weight, preferred_element_type=wide)
    )
    bias_sums = jnp.sum(qkv_grad.astype(wide), axis=0)

    def widen(part):
        full = jnp.zeros((4 * part.shape[0],), wide)
        return lax.dynamic_update_slice_in_dim(full, part, quarter * part.shape[0], 0)

    fsdp_count = lax.axis_size("fsdp")
    all_vectors = jnp.concatenate(
        [
            vector.reshape(fsdp_count, -1)
            for vector in (
                widen(bias_sums[:head_cols]),
                widen(bias_sums[2 * head_cols :]),
                out_bias_grad,
                gain_one_grad,
                shift_one_grad,
                down_bias_grad,
                gain_two_grad,
                shift_two_grad,
                widen(up_bias_grad),
            )
        ],
        1,
    )
    vector_sum = jnp.sum(lax.all_to_all(all_vectors, "fsdp", 0, 0, tiled=True), axis=0)
    vector_sum = vector_sum + swap(vector_sum, TP_BIT)
    vector_grads = [
        vector_sum[i * shard_rows : (i + 1) * shard_rows] for i in range(8)
    ] + [vector_sum[8 * shard_rows :]]

    def columns(array):
        return array.reshape(shard_rows, -1)

    query_sum, key_sum, value_sum = [
        columns(qkv_sums[:, :, i * head_cols : (i + 1) * head_cols]) for i in range(3)
    ]
    return (
        from_slot(output.astype(low_type)),
        from_slot(hidden_grad),
        query_sum,
        vector_grads[0],
        key_sum,
        value_sum,
        vector_grads[1],
        jnp.transpose(columns(out_grad)),
        vector_grads[2],
        vector_grads[3],
        vector_grads[4],
        columns(up_grad),
        vector_grads[8],
        jnp.transpose(columns(down_grad)),
        vector_grads[5],
        vector_grads[6],
        vector_grads[7],
    )

BIT_TP, BIT_CORE, BIT_SIDE, BIT_LOW, BIT_HIGH = 1, 2, 4, 8, 16
TEAM_BITS = (BIT_TP, BIT_LOW, BIT_TP | BIT_LOW)
PART_BITS = (BIT_SIDE, BIT_CORE, BIT_SIDE | BIT_CORE)


class Place:
    def __init__(self):
        fsdp = lax.axis_index("fsdp")
        self.tp = lax.axis_index("tp")
        self.core = fsdp & 1
        self.side = (fsdp >> 1) & 1
        self.low = (fsdp >> 2) & 1
        self.high = fsdp >> 3
        self.quarter = 2 * self.tp + self.low


def run_kernel(body, outs, *operands, scratch=(), sems=0, apart=False, us=1.0, name=None):
    def space(operand):
        if operand.dtype == jnp.int32:
            return pltpu.SMEM
        return pltpu.HBM if apart else pltpu.VMEM

    scratches = [pltpu.VMEM(shape, kind) for shape, kind in scratch]
    if sems:
        scratches.append(pltpu.SemaphoreType.DMA((sems,)))
    return pl.pallas_call(
        body,
        out_shape=[jax.ShapeDtypeStruct(shape, kind) for shape, kind in outs],
        in_specs=[pl.BlockSpec(memory_space=space(operand)) for operand in operands],
        out_specs=[pl.BlockSpec(memory_space=pltpu.VMEM)] * len(outs),
        scratch_shapes=scratches,
        compiler_params=pltpu.CompilerParams(vmem_limit_bytes=8 << 20),
        cost_estimate=pl.CostEstimate(
            flops=int(us * 1.0e7), transcendentals=0, bytes_accessed=int(us * 1.0e4)
        ),
        name=name,
    )(*[pltpu.with_memory_space_constraint(op, pltpu.HBM) if apart else op for op in operands])


def tie(value, *others):
    return lax.optimization_barrier((value, others))[0]


def mul(left, right, left_dim=1, right_dim=0):
    return lax.dot_general(
        left, right, (((left_dim,), (right_dim,)), ((), ())), preferred_element_type=wide
    )


def bit_of(index, stride):
    return (index // stride) & 1


def place_of(index, parts, shard_pos):
    here = Place()
    shard = index & (shard_pos - 1)
    high = here.high ^ bit_of(index, shard_pos)
    tp = here.tp ^ bit_of(index, 2 * shard_pos)
    low = here.low ^ bit_of(index, 4 * shard_pos)
    side, core = here.side, here.core
    if parts:
        side = side ^ bit_of(index, 8 * shard_pos)
        core = core ^ bit_of(index, 16 * shard_pos)
    block = (high * 2 + low) * 4 + side * 2 + core
    return (block * 2 + tp) * shard_pos + shard


def live_rows_of(lengths_ref, index, parts, shard_pos):
    return place_of(index, parts, shard_pos) < lengths_ref[Place().high]


def row_of(chip, core, rows):
    return pl.ds(pl.multiple_of((2 * chip + core) * rows, 16), rows)


def join_pieces(piece_refs, full_ref, rows, begin, cols=slice(None)):
    here = Place()
    for which, ref in enumerate(piece_refs):
        side, core = here.side ^ ((which >> 1) & 1), here.core ^ (which >> 2)
        for inner in range(2):
            block = (here.high ^ (which & 1)) * 2 + (here.low ^ inner)
            piece = ref[inner, begin : begin + rows, cols]
            full_ref[row_of(block * 2 + side, core, rows), :] = piece


def split_rows(full_ref, keep_ref, send_ref, begin, cols):
    core = Place().core
    rows = keep_ref.shape[1]
    for chip in range(keep_ref.shape[0]):
        keep_ref[chip, :, begin : begin + cols] = full_ref[row_of(chip, core, rows), 0:cols]
        send_ref[chip] = full_ref[row_of(chip, 1 - core, rows), 0:cols]


def pack_kernel(count, *refs):
    sources, refs = refs[:count], refs[count:]
    outs, held, sems = refs[:7], refs[7:-1], refs[-1]
    copies = [
        pltpu.make_async_copy(source, target, sems.at[i])
        for i, (source, target) in enumerate(zip(sources, held))
    ]
    for copy in copies:
        copy.start()
    wq_ref, wk_ref, wv_ref, wo_ref, wu_ref, wd_ref = held[:6]
    own_ref, send_ref, later_own_ref, near_ref, hidden_ref, cot_ref, other_ref = outs
    size, shard = send_ref.shape[0], hidden_ref.shape[0]
    rows = wq_ref.shape[0]
    head_cols = wq_ref.shape[1] // 2
    unit_cols = wu_ref.shape[1] // 2
    low = Place().low
    near = Place().high == 0
    for i, out_ref in ((15, hidden_ref), (16, cot_ref)):
        copies[i].wait()
        first, second = held[i][:, 0, :], held[i][:, 1, :]
        out_ref[...] = jnp.where(near, first, second)
        other_ref[(i - 15) * shard : (i - 14) * shard, :] = jnp.where(near, second, first)
    for copy in copies[6:15]:
        copy.wait()
    vectors = [ref[...].astype(wide).reshape(1, rows) for ref in held[6:14]]
    block = jnp.concatenate(
        [
            jnp.pad(jnp.concatenate(vectors, 0), ((0, 0), (0, 4 * rows - rows))),
            held[14][...].astype(wide).reshape(1, 4 * rows),
            jnp.zeros((7, 4 * rows), wide),
        ],
        0,
    ).astype(low_type)
    for out_ref in (own_ref, send_ref, near_ref):
        out_ref[rows : rows + 16, 0 : 4 * rows] = block
        out_ref[rows : rows + 16, 4 * rows :] = jnp.zeros(
            (16, out_ref.shape[1] - 4 * rows), low_type
        )
    for copy in copies[:6]:
        copy.wait()
    for half in range(2):
        heads = slice(half * head_cols, (half + 1) * head_cols)
        units = slice(half * unit_cols, (half + 1) * unit_cols)

        def put_first(first_ref):
            for i, ref in enumerate((wq_ref, wk_ref, wv_ref, wo_ref)):
                first_ref[0:rows, i * head_cols : (i + 1) * head_cols] = ref[:, heads]

        def put_later(later_ref, begin):
            later_ref[begin : begin + rows, :] = wu_ref[:, units]
            later_ref[begin + rows : begin + 2 * rows, :] = wd_ref[:, units]

        @pl.when(low == half)
        def _():
            put_first(own_ref)
            put_later(later_own_ref, 0)

        @pl.when(low != half)
        def _():
            put_first(send_ref)
            put_first(near_ref)
            put_later(near_ref, size)


def by_chip_row(here, refs, high, low, rows, cols):
    near = high == 0
    p0, p1, p2, p3 = [
        jnp.where(
            near,
            refs[2 * part][low, rows : rows + 16, 0:cols].astype(wide),
            refs[2 * part + 1][low, rows : rows + 16, 0:cols].astype(wide),
        )
        for part in range(4)
    ]
    left = here.side == 0
    own = jnp.where(left, p0, p1), jnp.where(left, p1, p0)
    other = jnp.where(left, p2, p3), jnp.where(left, p3, p2)
    even = here.core == 0
    result = []
    for side in range(2):
        result.append(jnp.where(even, own[side], other[side]))
        result.append(jnp.where(even, other[side], own[side]))
    return result


def project_kernel(
    keep_ref, got_ref, tp_ref, low_ref, both_ref, *refs
):
    parts, outs = refs[:8], refs[8:]
    rows_ref, query_ref, pair_ref, rest_ref, weight_ref, out_weight_ref = outs
    rows = parts[0].shape[1] - 16
    head_cols = query_ref.shape[1]
    join_pieces(parts, weight_ref, rows, 0, slice(0, 3 * head_cols))
    join_pieces(parts, out_weight_ref, rows, 0, slice(3 * head_cols, 4 * head_cols))
    shard = keep_ref.shape[0]
    rows_ref[0:shard, :] = keep_ref[...]
    rows_ref[shard : 2 * shard, :] = got_ref[0:shard, :]
    for i, ref in enumerate((tp_ref, low_ref, both_ref)):
        rows_ref[2 * shard * (i + 1) : 2 * shard * (i + 2), :] = ref[...]
    here = Place()
    biases = jnp.concatenate(by_chip_row(here, parts, here.high ^ here.tp, 0, rows, rows), 1)
    query_bias, value_bias = biases[0:1], biases[1:2]
    made = mul(rows_ref[...], weight_ref[...])
    query_ref[...] = (made[:, 0:head_cols] + query_bias).astype(low_type)
    values = made[:, 2 * head_cols :] + value_bias
    split = pair_ref.shape[1] - head_cols
    pair_ref[:, 0:head_cols] = made[:, head_cols : 2 * head_cols].astype(low_type)
    pair_ref[:, head_cols:] = values[:, 0:split].astype(low_type)
    rest_ref[...] = values[:, split:].astype(low_type)


def joined_pair(pairs, rests, head_cols):
    pair = jnp.concatenate([ref[...] for ref in pairs], 0)
    rest = jnp.concatenate([ref[...] for ref in rests], 0)
    return pair[:, 0:head_cols], jnp.concatenate([pair[:, head_cols:], rest], 1)


def head_of(array, head):
    return array[:, head * HD : (head + 1) * HD]


def attend_kernel(
    shard_pos, lengths_ref, query_ref, *refs
):
    pieces, (weight_ref, low_ref, stats_ref, keep_ref, *sends) = refs[:8], refs[8:]
    head_cols = query_ref.shape[1]
    count = query_ref.shape[0]
    keys, values = joined_pair(pieces[:4], pieces[4:], head_cols)
    queries = query_ref[...] * HD ** (-0.5)
    lanes = lax.broadcasted_iota(jnp.int32, (1, keys.shape[0]), 1)
    live = live_rows_of(lengths_ref, lanes, True, shard_pos)
    column = lax.broadcasted_iota(jnp.int32, (count, 128), 1)
    stats = jnp.zeros((count, 128), wide)
    parts = []
    for head in range(head_cols // HD):
        scores = mul(head_of(queries, head), head_of(keys, head), 1, 1)
        scores = jnp.where(live, scores, masked_score)
        top = jnp.max(scores, axis=1, keepdims=True)
        grown = jnp.exp(scores - top)
        total = jnp.sum(grown, axis=1, keepdims=True)
        weights = (grown * (1.0 / total)).astype(low_type)
        parts.append(mul(weights, head_of(values, head)))
        stats = jnp.where(column == head, top + jnp.log(total), stats)
    attended = jnp.concatenate(parts, 1).astype(low_type)
    low_ref[...] = attended
    stats_ref[...] = stats
    give_out(mul(attended, weight_ref[...], 1, 1), keep_ref, sends)


def full_kernel(*refs):
    pieces, outs = refs[:8], refs[8:]
    rows = pieces[0].shape[1] // 2
    for i, out_ref in enumerate(outs):
        join_pieces(pieces, out_ref, rows, i * rows)


def lines_kernel(*refs):
    parts, (vector_ref, bias_ref) = refs[:8], refs[8:]
    here = Place()
    rows = parts[0].shape[1] - 16
    vectors = []
    for block in range(4):
        high, low = (block >> 1) ^ here.high, (block & 1) ^ here.low
        vectors += by_chip_row(here, parts, high, low, rows, rows)
    vector_ref[...] = jnp.concatenate(vectors, 1)[0:8]
    bias = by_chip_row(here, parts, here.high ^ here.tp, 0, rows, 4 * rows)
    bias_ref[...] = jnp.concatenate(bias, 1)[8:9]


def give_out(partial, keep_ref, sends):
    count = keep_ref.shape[0]
    keep_ref[...] = partial[0:count]
    for i, ref in enumerate(sends):
        ref[...] = partial[(i + 1) * count : (i + 2) * count].astype(low_type)


def collect(keep_ref, *got):
    total = keep_ref[...]
    for ref in got:
        total = total + ref[...].astype(wide)
    return total


def vector_row(vector_ref, row):
    return vector_ref[row : row + 1, :]


def first_norm_kernel(
    keep_ref, got1_ref, got2_ref, got3_ref, own_ref, vector_ref,
    out_ref, low_ref, normed_ref, scale_ref,
):
    branch = collect(keep_ref, got1_ref, got2_ref, got3_ref)
    rows = own_ref[0 : branch.shape[0], :].astype(wide)
    normed, scale = norm_parts(rows + branch + vector_row(vector_ref, 2))
    out = normed * vector_row(vector_ref, 3) + vector_row(vector_ref, 4)
    out_ref[...] = out
    low_ref[...] = out.astype(low_type)
    normed_ref[...] = normed
    scale_ref[...] = jnp.broadcast_to(scale, scale_ref.shape)


def spread_of(values):
    scaled = jnp.clip(values * (0.5**0.5), -3.832506856900711, 3.832506856900711)
    square = scaled * scaled
    top = jnp.full_like(values, 0.00022905065861350646)
    for term in (0.0034082910107109506, 0.050955695062380861, 0.18520832239976145, 1.128379143519084):
        top = top * square + term
    under = jnp.full_like(values, -1.1791602954361697e-7)
    for term in (
        0.000023547966471313185,
        0.0010179625278914885,
        0.014070470171167667,
        0.11098505178285362,
        0.49746925110067538,
        1.0,
    ):
        under = under * square + term
    return 0.5 + 0.5 * (scaled * top / under)


def hidden_kernel(
    own_ref, got1_ref, got2_ref, got3_ref, up_ref, down_ref, bias_ref,
    keep_ref, send1_ref, send2_ref, send3_ref, active_ref, pre_ref, spread_ref, rows_ref,
):
    rows = jnp.concatenate([r[...] for r in (own_ref, got1_ref, got2_ref, got3_ref)], 0)
    rows_ref[...] = rows
    preact = mul(rows, up_ref[...]) + bias_ref[...]
    spread = spread_of(preact)
    active = (preact * spread).astype(low_type)
    active_ref[...] = active
    pre_ref[...] = preact
    spread_ref[...] = spread
    give_out(mul(active, down_ref[...], 1, 1), keep_ref, (send1_ref, send2_ref, send3_ref))


def slope_kernel(pre_ref, spread_ref, slope_ref):
    preact = pre_ref[...]
    density = jnp.exp(-0.5 * preact * preact) * (2.0 * math.pi) ** (-0.5)
    slope_ref[...] = spread_ref[...] + preact * density


def second_norm_kernel(
    lengths_ref, keep_ref, got1_ref, got2_ref, got3_ref, first_ref, own_ref, slot_ref, vector_ref,
    output_ref, grad_ref, low_ref, sums_ref,
):
    shard_pos = own_ref.shape[0]
    branch = collect(keep_ref, got1_ref, got2_ref, got3_ref)
    normed, scale = norm_parts(first_ref[...] + branch + vector_row(vector_ref, 5))
    gain = vector_row(vector_ref, 6)
    output_ref[...] = (normed * gain + vector_row(vector_ref, 7)).astype(low_type)
    index = lax.broadcasted_iota(jnp.int32, (2 * shard_pos, 1), 0)
    live = live_rows_of(lengths_ref, index, False, shard_pos)
    grad = jnp.concatenate([own_ref[...], slot_ref[shard_pos:, :]], 0).astype(wide)
    grad = jnp.where(live, grad, 0.0)
    second = norm_back(grad, normed, scale, gain)
    grad_ref[...] = second
    low = second.astype(low_type)
    low_ref[...] = low
    sums_ref[0:1, :] = jnp.sum(low.astype(wide), axis=0, keepdims=True)
    sums_ref[1:2, :] = jnp.sum(grad * normed, axis=0, keepdims=True)
    sums_ref[2:3, :] = jnp.sum(grad, axis=0, keepdims=True)


def hidden_back_kernel(
    own_ref, got1_ref, got2_ref, got3_ref, slope_ref, up_ref, down_ref,
    keep_ref, send1_ref, send2_ref, send3_ref, pre_ref, rows_ref, sums_ref,
):
    rows = jnp.concatenate([r[...] for r in (own_ref, got1_ref, got2_ref, got3_ref)], 0)
    rows_ref[...] = rows
    pre = (mul(rows, down_ref[...]) * slope_ref[...]).astype(low_type)
    pre_ref[...] = pre
    sums_ref[...] = jnp.sum(pre.astype(wide), axis=0, keepdims=True)
    give_out(mul(pre, up_ref[...], 1, 1), keep_ref, (send1_ref, send2_ref, send3_ref))


def weight_kernel(pairs, extra, *refs):
    operands = refs[: 2 * pairs + extra]
    keep_ref, *sends, full_ref = refs[2 * pairs + extra :]
    begin = 0
    for i, send_ref in enumerate(sends):
        left, right = operands[2 * i], operands[2 * i + 1]
        cols = right.shape[1]
        full_ref[:, 0:cols] = mul(left[...], right[...], 0, 0).astype(low_type)
        if extra and i == pairs - 1:
            total = operands[-2][...] + operands[-1][...]
            blank = jnp.zeros((128 - total.shape[0], total.shape[1]), wide)
            total = jnp.transpose(jnp.concatenate([total, blank], 0))
            full_ref[:, cols : cols + 128] = total.astype(low_type)
            cols += 128
        split_rows(full_ref, keep_ref, send_ref, begin, cols)
        begin += cols


def fold_kernel(count, bit, stride, *refs):
    keeps, got, outs = refs[:count], refs[count:-2], refs[-2:]
    own = getattr(Place(), bit)
    for choice, out_ref in enumerate(outs):
        for block in range(out_ref.shape[0]):
            index = block * stride[0] + (own ^ choice) * stride[1]
            begin = 0
            for i, got_ref in enumerate(got):
                end = begin + got_ref.shape[2]
                if count == 1:
                    total = keeps[0][index, :, begin:end].astype(wide)
                else:
                    total = keeps[i][index].astype(wide)
                out_ref[block, :, begin:end] = (total + got_ref[index].astype(wide)).astype(
                    out_ref.dtype
                )
                begin = end


def block_fold_kernel(keep_ref, got_ref, *outs):
    here = Place()
    for choice, out_ref in enumerate(outs):
        index = (here.high ^ (choice >> 1)) * 2 + (here.low ^ (choice & 1))
        out_ref[...] = (keep_ref[index] + got_ref[index].astype(wide)).astype(out_ref.dtype)


def final_fold_kernel(*refs):
    inputs, (own_ref, send_ref) = refs[:-2], refs[-2:]
    low = Place().low
    for choice, out_ref in ((low, own_ref), (1 - low, send_ref)):
        total = inputs[0][choice].astype(wide)
        for ref in inputs[1:]:
            total = total + ref[choice].astype(wide)
        out_ref[...] = total.astype(out_ref.dtype)


def total_kernel(spans, count, *refs):
    sources, outs = refs[:count], refs[count:]
    even = Place().low == 0
    own, got = sources[0][...], sources[1][...].astype(wide)
    if count == 4:
        own = own + sources[2][...].astype(wide)
        got = got + sources[3][...].astype(wide)
    for out_ref, (begin, end) in zip(outs, spans):
        cols = end - begin
        mine, other = own[:, begin:end], got[:, begin:end]
        out_ref[:, 0:cols] = jnp.where(even, mine, other)
        out_ref[:, cols:] = jnp.where(even, other, mine)
    vectors = outs[len(spans) :]
    if vectors:
        end = own.shape[1]
        rows = jnp.transpose(own[:, end - 128 :] + got[:, end - 128 :])
        for i, out_ref in enumerate(vectors[:-1]):
            out_ref[...] = rows[i : i + 1, :].reshape(out_ref.shape)
        first = len(vectors) - 1
        parts = [rows[first + i : first + i + 1, :] for i in range(4)]
        vectors[-1][...] = jnp.concatenate(parts, 1).reshape(vectors[-1].shape)


def first_back_kernel(
    keep_ref, got1_ref, got2_ref, got3_ref, second_ref, normed_ref, scale_ref, vector_ref,
    grad_ref, low_ref, sums_ref,
):
    grad = second_ref[...] + collect(keep_ref, got1_ref, got2_ref, got3_ref)
    normed = normed_ref[...]
    first = norm_back(grad, normed, scale_ref[:, 0:1], vector_row(vector_ref, 3))
    grad_ref[...] = first
    low = first.astype(low_type)
    low_ref[...] = low
    sums_ref[0:1, :] = jnp.sum(low.astype(wide), axis=0, keepdims=True)
    sums_ref[1:2, :] = jnp.sum(grad * normed, axis=0, keepdims=True)
    sums_ref[2:3, :] = jnp.sum(grad, axis=0, keepdims=True)


def attended_back_kernel(
    own_ref, got1_ref, got2_ref, got3_ref, weight_ref, low_ref, stats_ref, query_ref,
    packet_ref, rows_ref, sums_ref,
):
    rows = jnp.concatenate([r[...] for r in (own_ref, got1_ref, got2_ref, got3_ref)], 0)
    rows_ref[...] = rows
    made = mul(rows, weight_ref[...])
    head_cols = made.shape[1]
    sums_ref[...] = jnp.sum(made, axis=0, keepdims=True)
    grad = made.astype(low_type)
    packet_ref[:, 0:head_cols] = grad
    packet_ref[:, head_cols : 2 * head_cols] = query_ref[...]
    both = grad.astype(wide) * low_ref[...].astype(wide)
    column = lax.broadcasted_iota(jnp.int32, (made.shape[0], 128), 1)
    stats = stats_ref[...]
    levels = jnp.zeros_like(stats)
    heads = head_cols // HD
    for head in range(heads):
        delta = jnp.sum(head_of(both, head), axis=1, keepdims=True)
        for place, left in ((head, stats[:, head : head + 1]), (heads + head, delta)):
            for level in range(2):
                piece = left.astype(low_type).astype(wide)
                left = left - piece
                levels = jnp.where(column == 2 * place + level, piece, levels)
    packet_ref[:, 2 * head_cols :] = levels.astype(low_type)


def stat_of(packet, head_cols, place):
    base = 2 * head_cols + 2 * place
    first, second = packet[:, base : base + 1], packet[:, base + 1 : base + 2]
    return first.astype(wide) + second.astype(wide)


def query_back_kernel(shard_pos, lengths_ref, packet_ref, *refs):
    pieces, (out_ref, sums_ref) = refs[:8], refs[8:]
    head_cols = out_ref.shape[1]
    heads = head_cols // HD
    keys, values = joined_pair(pieces[:4], pieces[4:], head_cols)
    packet = packet_ref[...]
    grad = packet[:, 0:head_cols]
    queries = packet[:, head_cols : 2 * head_cols] * HD ** (-0.5)
    lanes = lax.broadcasted_iota(jnp.int32, (1, keys.shape[0]), 1)
    live = live_rows_of(lengths_ref, lanes, True, shard_pos)
    parts = []
    for head in range(heads):
        scores = mul(head_of(queries, head), head_of(keys, head), 1, 1)
        scores = jnp.where(live, scores, masked_score)
        weights = jnp.exp(scores - stat_of(packet, head_cols, head))
        weight_grad = mul(head_of(grad, head), head_of(values, head), 1, 1)
        weight_grad = weight_grad - stat_of(packet, head_cols, heads + head)
        parts.append(mul((weights * weight_grad).astype(low_type), head_of(keys, head)))
    made = (jnp.concatenate(parts, 1) * HD ** (-0.5)).astype(low_type)
    out_ref[...] = made
    sums_ref[...] = jnp.sum(made.astype(wide), axis=0, keepdims=True)


def pair_back_kernel(
    shard_pos, lengths_ref, pair_ref, rest_ref, query_grad_ref, weight_ref,
    g0_ref, g1_ref, g2_ref, g3_ref,
    keep_ref, send1_ref, send2_ref, send3_ref, made_ref,
):
    head_cols = query_grad_ref.shape[1]
    heads = head_cols // HD
    keys, values = joined_pair((pair_ref,), (rest_ref,), head_cols)
    packet = jnp.concatenate([ref[...] for ref in (g0_ref, g1_ref, g2_ref, g3_ref)], 0)
    grad = packet[:, 0:head_cols]
    queries = packet[:, head_cols : 2 * head_cols] * HD ** (-0.5)
    index = lax.broadcasted_iota(jnp.int32, (keys.shape[0], 1), 0)
    live = live_rows_of(lengths_ref, index, False, shard_pos)
    stats = jnp.transpose(packet[:, 2 * head_cols :].astype(wide))
    key_parts, value_parts = [], []
    for head in range(heads):
        log_total = stats[2 * head : 2 * head + 1] + stats[2 * head + 1 : 2 * head + 2]
        at = 2 * (heads + head)
        delta = stats[at : at + 1] + stats[at + 1 : at + 2]
        scores = mul(head_of(keys, head), head_of(queries, head), 1, 1)
        scores = jnp.where(live, scores, masked_score)
        weights = jnp.exp(scores - log_total)
        weight_grad = mul(head_of(values, head), head_of(grad, head), 1, 1)
        score_grad = (weights * (weight_grad - delta)).astype(low_type)
        key_parts.append(mul(score_grad, head_of(queries, head)))
        value_parts.append(mul(weights.astype(low_type), head_of(grad, head)))
    made = jnp.concatenate(
        [query_grad_ref[...]] + [part.astype(low_type) for part in key_parts + value_parts], 1
    )
    made_ref[...] = made
    give_out(mul(made, weight_ref[...], 1, 1), keep_ref, (send1_ref, send2_ref, send3_ref))


def slots_kernel(grad_ref, out_ref, got_ref, output_ref, hidden_grad_ref):
    near = Place().high == 0
    count, width = grad_ref.shape
    for target, own, got in (
        (hidden_grad_ref, grad_ref[...], got_ref[:, 0:width].astype(wide)),
        (output_ref, out_ref[0:count, :], got_ref[:, width:]),
    ):
        target[:, 0, :] = jnp.where(near, own, got)
        target[:, 1, :] = jnp.where(near, got, own)


def last_kernel(keep_ref, got1_ref, got2_ref, got3_ref, first_ref, output_ref, own_ref, send_ref):
    total = first_ref[...] + collect(keep_ref, got1_ref, got2_ref, got3_ref)
    count, width = own_ref.shape
    own_ref[...] = total[0:count]
    send_ref[:, 0:width] = total[count:].astype(send_ref.dtype)
    send_ref[:, width:] = output_ref[count:, :]


def vectors_kernel(shards, query_ref, value_ref, first_ref, second_ref, unit_ref, out_ref):
    width = out_ref.shape[1] // shards
    per = shards // 4
    quarter = Place().quarter
    out_ref[...] = jnp.zeros_like(out_ref)
    out_ref[2:5, :] = first_ref[0:3, :]
    out_ref[5:8, :] = second_ref[0:3, :]
    for which in range(4):

        @pl.when(quarter == which)
        def _():
            span = slice(which * per * width, (which + 1) * per * width)
            out_ref[0:1, span] = query_ref[...]
            out_ref[1:2, span] = value_ref[...]
            for i in range(4):
                parts = []
                for local in range(per):
                    begin = (4 * local + i) * width
                    parts.append(unit_ref[:, begin : begin + width])
                out_ref[8 + i : 9 + i, span] = jnp.concatenate(parts, 1)


def send_team(parts):
    return tuple(swap(parts[i], TEAM_BITS[i]) for i in (1, 0, 2))


def gather_team(rows):
    return tuple(swap(rows, bit) for bit in TEAM_BITS[::-1])[::-1]


def gather_parts(rows):
    side = swap(rows, BIT_SIDE)
    return rows, side, swap(rows, BIT_CORE), swap(side, BIT_CORE)


def local_32(
    hidden_in,
    cotangent,
    lengths,
    w_query,
    b_query,
    w_key,
    w_value,
    b_value,
    w_out,
    b_out,
    first_gain,
    first_shift,
    w_up,
    b_up,
    w_down,
    b_down,
    second_gain,
    second_shift,
):
    shard_pos, seq_count, width = hidden_in.shape
    rows_here = 2 * shard_pos
    group = 4 * rows_here
    shard_rows = w_query.shape[0]
    head_cols = w_query.shape[1] // 2
    unit_cols = w_up.shape[1] // 2
    chips = lax.axis_size("fsdp") // 2
    pair_cols = -(-head_cols // 128) * 128

    sources = (
        w_query, w_key, w_value, jnp.transpose(w_out), w_up, jnp.transpose(w_down),
        b_query, b_value, b_out, first_gain, first_shift, b_down, second_gain, second_shift, b_up,
        hidden_in, cotangent,
    )
    first = ((shard_rows + 16, 4 * head_cols), low_type)
    later = ((2 * shard_rows, unit_cols), low_type)
    near = ((3 * shard_rows + 16, unit_cols), low_type)
    shard = ((shard_pos, width), low_type)
    *packs, hidden_own, cot_own, other = run_kernel(
        functools.partial(pack_kernel, len(sources)),
        [first, first, later, near, shard, shard, ((rows_here, width), low_type)],
        *sources,
        scratch=[(source.shape, source.dtype) for source in sources],
        sems=len(sources),
        apart=True,
        us=3.0,
        name="pack",
    )

    slot_rows = swap(other, BIT_HIGH)
    first_own, first_send, later_own, near_send = tuple(packs)
    near_got = swap(near_send, BIT_LOW)
    size = first_own.shape[0]
    f2, f3 = swap(first_own, BIT_HIGH), swap(first_send, BIT_HIGH | BIT_LOW)
    first_near = jnp.stack([first_own, near_got[:size]])
    first_near_side = swap(first_near, BIT_SIDE)
    team_rows = gather_team(
        tie(jnp.concatenate([hidden_own, slot_rows[:shard_pos]], 0), packs)
    )
    first_far = tie(jnp.stack([f2, f3]), first_near_side)
    first_far_side = swap(first_far, BIT_SIDE)
    later_near = jnp.stack([later_own, near_got[size:]])
    later_far = swap(tie(later_near, first_far), BIT_HIGH)
    first_pieces = (
        first_near,
        first_far,
        first_near_side,
        first_far_side,
        swap(first_near, BIT_CORE),
        swap(first_far, BIT_CORE),
        swap(first_near_side, BIT_CORE),
        swap(tie(first_far_side, team_rows, later_near), BIT_CORE),
    )

    group_rows, queries, pair, rest, qkv_weight, out_weight = run_kernel(
        project_kernel,
        [
            ((group, width), low_type),
            ((group, head_cols), low_type),
            ((group, pair_cols), low_type),
            ((group, 2 * head_cols - pair_cols), low_type),
            ((width, 3 * head_cols), low_type),
            ((width, head_cols), low_type),
        ],
        hidden_own, slot_rows, *team_rows, *first_pieces,
        name="project",
    )
    pair_parts, rest_parts = gather_parts(pair), gather_parts(rest)
    later_near_side = swap(tie(later_near, pair_parts[1]), BIT_SIDE)
    near_core = swap(tie(later_near, pair_parts[1]), BIT_CORE)
    vectors, up_bias = run_kernel(
        lines_kernel,
        [((8, width), wide), ((1, unit_cols), wide)],
        *tie(first_pieces, pair),
        us=0.5,
        name="lines",
    )
    rows_shape = (rows_here, width)
    given = [(rows_shape, wide)] + [(rows_shape, low_type)] * 3
    attended_low, stats, keep, *sends = run_kernel(
        functools.partial(attend_kernel, shard_pos),
        [((group, head_cols), low_type), ((group, 128), wide)] + given,
        lengths, tie(queries, vectors), *pair_parts, *rest_parts, out_weight,
        us=3.0,
        name="attend",
    )
    sends = send_team(sends)
    later_far_side = swap(tie(later_far, attended_low), BIT_SIDE)
    far_core = swap(tie(later_far, sends[0]), BIT_CORE)
    first_out, first_low, normed, scale = run_kernel(
        first_norm_kernel,
        [(rows_shape, wide), (rows_shape, low_type), (rows_shape, wide), ((rows_here, 128), wide)],
        keep, *sends, group_rows, vectors,
        us=0.5,
        name="first_norm",
    )
    first_team = gather_team(first_low)
    later_sides = later_near, later_far, later_near_side, later_far_side
    waited = tie((later_near_side, later_far_side), first_low)
    later_pieces = later_sides + (
        near_core, far_core, swap(waited[0], BIT_CORE), swap(waited[1], BIT_CORE)
    )
    up_weight, down_weight = run_kernel(
        full_kernel,
        [((width, unit_cols), low_type)] * 2,
        *later_pieces,
        us=1.0,
        name="full_units",
    )
    keep, s1, s2, s3, active, preact, spread, first_rows = run_kernel(
        hidden_kernel,
        given
        + [((group, unit_cols), low_type)]
        + [((group, unit_cols), wide)] * 2
        + [((group, width), low_type)],
        first_low, *first_team, up_weight, down_weight, up_bias,
        us=2.0,
        name="hidden",
    )
    sends = send_team((s1, s2, s3))
    (slope,) = run_kernel(
        slope_kernel, [((group, unit_cols), wide)], preact, spread, us=0.7, name="slope"
    )
    output, second_grad, second_low, second_sums = run_kernel(
        second_norm_kernel,
        [(rows_shape, low_type), (rows_shape, wide), (rows_shape, low_type), ((8, width), wide)],
        lengths, keep, *sends, first_out, cot_own, slot_rows, vectors,
        name="second_norm",
    )
    second_team = gather_team(second_low)
    def weight_parts(operands, name, extra=()):
        parts = [right.shape[1] for right in operands[1::2]]
        parts[-1] += 128 if extra else 0
        shapes = [(chips, shard_rows, cols) for cols in [sum(parts)] + parts]
        kept, *sent = run_kernel(
            functools.partial(weight_kernel, len(parts), len(extra)),
            [(shape, low_type) for shape in shapes],
            *operands, *extra,
            scratch=[((width, max(parts)), low_type)],
            name=name,
        )
        return kept, sent

    def finish(sources, spans, name, vectors=()):
        outs = [(shard_rows, 2 * (end - begin)) for begin, end in spans] + list(vectors)
        return run_kernel(
            functools.partial(total_kernel, spans, len(sources)),
            [(shape, wide) for shape in outs],
            *sources,
            us=0.7,
            name=name,
        )

    def fold(bit, stride, kept, got, name):
        cols = sum(part.shape[2] for part in kept)
        shape = (kept[0].shape[0] // 2, shard_rows, cols)
        return run_kernel(
            functools.partial(fold_kernel, len(kept), bit, stride),
            [(shape, wide), (shape, low_type)],
            *kept, *got,
            us=0.7,
            name=name + "_fold_" + bit,
        )

    keep, s1, s2, s3, pre_grad, second_rows, unit_sums = run_kernel(
        hidden_back_kernel,
        given
        + [((group, unit_cols), low_type), ((group, width), low_type), ((1, unit_cols), wide)],
        second_low, *second_team, slope, up_weight, down_weight,
        us=1.5,
        name="hidden_back",
    )
    unit_kept, unit_sent = weight_parts(
        (second_rows, active, first_rows, pre_grad), "unit_weights"
    )
    unit_got = [swap(part, BIT_CORE) for part in unit_sent]
    unit_kept, unit_sent = fold("side", (2, 1), [unit_kept], unit_got, "unit")
    unit_got = swap(unit_sent, BIT_SIDE)
    sends = send_team(tie((s1, s2, s3), unit_sent))
    first_grad, one_low, first_sums = run_kernel(
        first_back_kernel,
        [(rows_shape, wide), (rows_shape, low_type), ((8, width), wide)],
        keep, *sends, second_grad, normed, scale, vectors,
        us=0.7,
        name="first_back",
    )
    one_team = gather_team(one_low)
    packet, one_rows, value_sums = run_kernel(
        attended_back_kernel,
        [
            ((group, 2 * head_cols + 128), low_type),
            ((group, width), low_type),
            ((1, head_cols), wide),
        ],
        one_low, *one_team, out_weight, attended_low, stats, queries,
        us=0.7,
        name="attended_back",
    )
    packet_side = swap(packet, BIT_SIDE)
    query_grad, query_sums = run_kernel(
        functools.partial(query_back_kernel, shard_pos),
        [((group, head_cols), low_type), ((1, head_cols), wide)],
        lengths, packet, *pair_parts, *rest_parts,
        us=3.0,
        name="query_back",
    )
    packets = (
        packet,
        packet_side,
        swap(packet, BIT_CORE),
        swap(tie(packet_side, query_grad), BIT_CORE),
    )
    (sums,) = run_kernel(
        functools.partial(vectors_kernel, 2 * chips),
        [((16, width), wide)],
        query_sums, value_sums, first_sums, second_sums, unit_sums,
        us=0.5,
        name="vectors",
    )
    sums_got = swap(sums, BIT_TP)
    unit_kept, unit_sent = fold("high", (1, 2), [tie(unit_kept, packet)], [unit_got], "unit")
    unit_got = swap(unit_sent, BIT_HIGH)
    keep, s1, s2, s3, qkv_grad = run_kernel(
        functools.partial(pair_back_kernel, shard_pos),
        given + [((group, 3 * head_cols), low_type)],
        lengths, tie(pair, unit_kept), rest, query_grad, qkv_weight, *packets,
        us=4.0,
        name="pair_back",
    )
    late_kept, late_sent = weight_parts(
        (one_rows, attended_low, group_rows, tie(qkv_grad, unit_got)),
        "head_weights",
        (sums, sums_got),
    )
    late_got = [swap(part, BIT_CORE) for part in late_sent]
    lasts = send_team((s1, s2, s3))
    late_kept, late_sent = fold("side", (2, 1), [late_kept], late_got, "late")
    late_got = swap(late_sent, BIT_SIDE)
    late_shape = late_kept.shape[1:]
    late_own, s1, s2, s3 = run_kernel(
        block_fold_kernel,
        [(late_shape, wide)] + [(late_shape, low_type)] * 3,
        late_kept, late_got,
        us=0.5,
        name="late_block",
    )
    late_sums = (
        late_own, swap(s1, BIT_LOW), swap(s2, BIT_HIGH), swap(s3, BIT_HIGH | BIT_LOW)
    )
    grad_own, grad_send = run_kernel(
        last_kernel,
        [((shard_pos, width), wide), ((shard_pos, 2 * width), low_type)],
        tie(keep, late_kept), *lasts, first_grad, output,
        us=0.5,
        name="last",
    )
    grad_got = swap(grad_send, BIT_HIGH)
    unit_own, unit_sent = run_kernel(
        final_fold_kernel,
        [(unit_kept.shape[1:], wide), (unit_kept.shape[1:], low_type)],
        unit_kept, unit_got,
        us=0.5,
        name="unit_low",
    )
    down_grad, up_grad = finish(
        (unit_own, swap(unit_sent, BIT_LOW)), ((0, unit_cols), (unit_cols, 2 * unit_cols)), "unit_total"
    )
    out_grad, query_total, key_total, value_total, *shares = finish(
        tie(late_sums, down_grad, up_grad),
        [(i * head_cols, (i + 1) * head_cols) for i in range(4)],
        "late_total",
        [(shard_rows,)] * 8 + [b_up.shape],
    )
    whole_output, hidden_grad = run_kernel(
        slots_kernel,
        [(hidden_in.shape, low_type), (hidden_in.shape, wide)],
        grad_own, output, grad_got,
        us=0.5,
        name="slots",
    )
    return (
        whole_output,
        hidden_grad,
        query_total,
        shares[0],
        key_total,
        value_total,
        shares[1],
        jnp.transpose(out_grad),
        shares[2],
        shares[3],
        shares[4],
        up_grad,
        shares[8],
        jnp.transpose(down_grad),
        shares[5],
        shares[6],
        shares[7],
    )


def solution(mesh):
    in_specs = (
        P(("fsdp", "tp"), None, None),
        P(("fsdp", "tp"), None, None),
        P(),
        P("fsdp", "tp"),
        P("fsdp"),
        P("fsdp", "tp"),
        P("fsdp", "tp"),
        P("fsdp"),
        P("tp", "fsdp"),
        P("fsdp"),
        P("fsdp"),
        P("fsdp"),
        P("fsdp", "tp"),
        P("fsdp"),
        P("tp", "fsdp"),
        P("fsdp"),
        P("fsdp"),
        P("fsdp"),
    )
    out_specs = (
        P(("fsdp", "tp"), None, None),
        P(("fsdp", "tp"), None, None),
        P("fsdp", "tp"),
        P("fsdp"),
        P("fsdp", "tp"),
        P("fsdp", "tp"),
        P("fsdp"),
        P("tp", "fsdp"),
        P("fsdp"),
        P("fsdp"),
        P("fsdp"),
        P("fsdp", "tp"),
        P("fsdp"),
        P("tp", "fsdp"),
        P("fsdp"),
        P("fsdp"),
        P("fsdp"),
    )
    program = local_32 if mesh.shape["fsdp"] == 16 else local
    return jax.shard_map(program, mesh=mesh, in_specs=in_specs, out_specs=out_specs, check_vma=False)
```
